32 devices in a mesh: seq: 8 (over y, x, core), mp: 4 (over z).
Axes of the slice: x: 2, y: 2, z: 4, core: 2. Of those that a mesh axis runs over, the one named last changes fastest.
Arguments:
- coarse: bfloat16 [768, 1024], P('mp', 'seq'), may hold values from -6 to 6
- skip: bfloat16 [768, 2048], P('mp', 'seq'), may hold values from -6 to 6
- conv_weight: bfloat16 [3, 768, 768], P(None, 'mp'), may hold values from -0.125 to 0.125
- conv_bias: float32 [768], P('mp'), may hold values from -3 to 3
- head_weight: bfloat16 [768, 512], P(None, 'mp'), may hold values from -0.21875 to 0.21875
- head_bias: float32 [512], P('mp'), may hold values from -3 to 3
- counts: int32 [2048, 512], P('seq', 'mp'), may hold values from 0 to 3
- seg_mask: int32 [1, 512], P(None, 'mp'), may hold values 0 or 1
Outputs:
- grad_skip: bfloat16 [768, 2048], P('mp', 'seq')
- grad_coarse: bfloat16 [768, 1024], P('mp', 'seq')
- grad_head: float32 [768, 512], P('seq', 'mp')
- grad_conv: float32 [768, 3, 768], P('seq', None, 'mp')
The draws below stay inside these ranges and needn't reach their ends.
All inputs are finite; a program needn't handle non-finite values. No bound on the sum of `seg_mask` on one device may be relied on, other than what follows from the above.
Results may differ from the reference program's by a relative error of at most 0.0068.
Values may be sent and summed in bfloat16 or wider, within the bound.
No kernel may reach another device: no remote copies, remote signals or barrier semaphores. Data moves between devices by JAX's collectives and lax.ppermute only.
A program may use at most 64 MiB of HBM per device.

```python
import jax
import jax.numpy as jnp
from jax import lax

C = 768
TRACKS = 512
KERNEL = 3
TOKENS = 2048
SEG = 2048
NSEG = 1


def place_ends(drawn, rng, smallest, high):
    index_at = [jax.random.randint(jax.random.fold_in(rng, axis), (), 0, length) for axis, length in enumerate(drawn.shape)]
    longest = drawn.shape.index(max(drawn.shape))
    beside = index_at[:longest] + [(index_at[longest] + 1) % drawn.shape[longest]] + index_at[longest + 1:]
    return drawn.at[tuple(index_at)].set(smallest).at[tuple(beside)].set(high)


def steps_of(rng, shape, split, smallest, largest):
    level = 1.0
    for axis_at, blocks in split:
        steps = jax.random.uniform(jax.random.fold_in(jax.random.fold_in(rng, 6), axis_at), (blocks,), jnp.float32, smallest / len(split), largest / len(split))
        level = level * jnp.repeat(jnp.exp(steps), shape[axis_at] // blocks).reshape((-1,) + (1,) * (len(shape) - 1 - axis_at))
    return level


def scatter_about(key, shape, spread, limit, cuts=(), kind=jnp.bfloat16):
    factor_of = steps_of(key, shape, cuts, -0.22, 0.18) if cuts else 1.0
    entries = jax.random.normal(key, shape, jnp.float32) * spread * factor_of
    return jnp.minimum(jnp.maximum(entries, -limit), limit).astype(kind)


def setup_inputs(seed: int = 0) -> dict:
    arg_keys = jax.random.split(jax.random.key(seed), 9)
    coarse = scatter_about(arg_keys[0], (C, TOKENS // 2), 1.0, 6.0, ((0, 4), (1, 8)))
    skip = scatter_about(arg_keys[1], (C, TOKENS), 1.0, 6.0, ((0, 4), (1, 8)))
    conv_weight = scatter_about(arg_keys[2], (KERNEL, C, C), (KERNEL * C) ** -0.5, 0.125, ((1, 4),))
    conv_bias = scatter_about(arg_keys[3], (C,), 0.5, 3.0, ((0, 4),), jnp.float32)
    head_weight = scatter_about(arg_keys[4], (C, TRACKS), C ** -0.5, 0.21875, ((1, 4),))
    head_bias = scatter_about(arg_keys[5], (TRACKS,), 0.5, 3.0, ((0, 4),), jnp.float32)
    counts = place_ends(jax.random.randint(arg_keys[6], (TOKENS, TRACKS), 0, 4), jax.random.fold_in(arg_keys[6], 1), 0, 3).astype(jnp.int32)
    seg_mask = place_ends((jax.random.randint(arg_keys[7], (NSEG, TRACKS), 0, 4) < 3).astype(jnp.int32), jax.random.fold_in(arg_keys[7], 1), 0, 1)
    return {"coarse": coarse, "skip": skip, "conv_weight": conv_weight, "conv_bias": conv_bias, "head_weight": head_weight, "head_bias": head_bias, "counts": counts, "seg_mask": seg_mask}


root_two_pi = 0.7978845608028654
cubic_coef = 0.044715

def gelu_value(inputs):
    inner = root_two_pi * (inputs + cubic_coef * inputs * inputs * inputs)
    return 0.5 * inputs * (1.0 + jnp.tanh(inner))

def gelu_slope(inputs):
    inner = root_two_pi * (inputs + cubic_coef * inputs * inputs * inputs)
    tangent = jnp.tanh(inner)
    return 0.5 * (1.0 + tangent) + 0.5 * inputs * (1.0 - tangent * tangent) * root_two_pi * (1.0 + 3.0 * cubic_coef * inputs * inputs)

def reference(coarse, skip, conv_weight, conv_bias, head_weight, head_bias, counts, seg_mask):
    length = skip.shape[1]
    taps = conv_weight.shape[0]
    reach = taps // 2
    tracks_all = head_weight.shape[1]
    doubled = jnp.repeat(coarse.T.astype(jnp.float32), 2, axis=0)
    summed = (doubled + skip.T.astype(jnp.float32)).astype(jnp.bfloat16)
    padded = jnp.pad(summed, ((reach, reach), (0, 0)))
    conv_out = jnp.zeros((length, conv_weight.shape[1]), jnp.float32)
    for offset in range(taps):
        conv_out = conv_out + jnp.dot(padded[offset:offset + length], conv_weight[offset].T, preferred_element_type=jnp.float32)
    before = conv_out + conv_bias
    hidden = (summed.astype(jnp.float32) + gelu_value(before)).astype(jnp.bfloat16)
    logits = jnp.dot(hidden, head_weight, preferred_element_type=jnp.float32) + head_bias
    predicted = jax.nn.softplus(logits) + 0.5
    observed = counts.astype(jnp.float32)
    segments = length // SEG
    pred_total = lax.optimization_barrier(jnp.sum(predicted.reshape(segments, SEG, tracks_all), axis=1))
    count_total = lax.optimization_barrier(jnp.sum(observed.reshape(segments, SEG, tracks_all), axis=1))
    mask_float = seg_mask.astype(jnp.float32)
    ratio = (mask_float * 4.0 * count_total / pred_total)[:, None, :]
    mask_wide = mask_float[:, None, :]
    slope_pred = mask_wide * (1.0 - 5.0 * observed.reshape(segments, SEG, tracks_all) / predicted.reshape(segments, SEG, tracks_all)) + ratio
    slope_pred = slope_pred.reshape(length, tracks_all)
    grad_logits = (slope_pred * jax.nn.sigmoid(logits)).astype(jnp.bfloat16)
    grad_hidden = jnp.dot(grad_logits, head_weight.T, preferred_element_type=jnp.float32)
    scale_back = 1.0 / jnp.sqrt(jnp.float32(length))
    grad_head = jnp.dot(hidden.T, grad_logits, preferred_element_type=jnp.float32) * scale_back
    grad_before = (grad_hidden * gelu_slope(before)).astype(jnp.bfloat16)
    grad_padded = jnp.pad(grad_before, ((reach, reach), (0, 0)))
    back = jnp.zeros((length, conv_weight.shape[2]), jnp.float32)
    for offset in range(taps):
        start_row = 2 * reach - offset
        back = back + jnp.dot(grad_padded[start_row:start_row + length], conv_weight[offset], preferred_element_type=jnp.float32)
    grad_input = grad_hidden + back
    grad_skip = grad_input.astype(jnp.bfloat16)
    grad_coarse = lax.optimization_barrier(jnp.sum(grad_input.reshape(length // 2, 2, grad_input.shape[1]), axis=1)).astype(jnp.bfloat16)
    pieces = []
    for offset in range(taps):
        pieces.append(jnp.dot(padded[offset:offset + length].T, grad_before, preferred_element_type=jnp.float32))
    grad_conv = jnp.stack(pieces, axis=1) * scale_back
    return (grad_skip.T, grad_coarse.T, grad_head, grad_conv)
```

```python
import math

import jax
import jax.numpy as jnp
from jax import lax
from jax.sharding import PartitionSpec as P

root_two_pi = 0.7978845608028654
cubic_coef = 0.044715
multi_weight = 5.0
pseudo_count = 0.5


def swap(block, axis, mask):
    count = lax.axis_size(axis)
    return lax.ppermute(block, axis, [(i, i ^ mask) for i in range(count)])


def shifted(block, axis, step):
    count = lax.axis_size(axis)
    pairs = [(i, i + step) for i in range(count) if 0 <= i + step < count]
    return lax.ppermute(block, axis, pairs)


def gathered(block, axis):
    return [block] + [swap(block, axis, j) for j in range(1, lax.axis_size(axis))]


def gelu_parts(inputs):
    inner = root_two_pi * (inputs + cubic_coef * inputs * inputs * inputs)
    tangent = jnp.tanh(inner)
    value = 0.5 * inputs * (1.0 + tangent)
    slope = 0.5 * (1.0 + tangent) + 0.5 * inputs * (1.0 - tangent * tangent) * root_two_pi * (
        1.0 + 3.0 * cubic_coef * inputs * inputs
    )
    return value, slope


def contract_first(left, right):
    return lax.dot_general(
        left, right, (((0,), (0,)), ((), ())), preferred_element_type=jnp.float32
    )


def contract_last(left, right):
    return lax.dot_general(
        left, right, (((1,), (1,)), ((), ())), preferred_element_type=jnp.float32
    )


def scattered(parts, axis, mine):
    count = lax.axis_size(axis)
    bits, low = count.bit_length() - 1, 0
    while low < bits:
        wide = 1 if low == 0 else min(2, bits - low)
        size = 1 << wide
        parts = parts.reshape((parts.shape[0] // size, size) + parts.shape[1:])
        at = (mine >> low) & (size - 1)
        small = parts.astype(jnp.bfloat16)
        kept = lax.dynamic_index_in_dim(parts, at, 1, keepdims=False)
        for step in range(1, size):
            piece = lax.dynamic_index_in_dim(small, at ^ step, 1, keepdims=False)
            kept = kept + swap(piece, axis, step << low).astype(jnp.float32)
        parts = kept
        low += wide
    return parts[0]


def shards(coarse, skip, conv_weight, conv_bias, head_weight, head_bias, counts, seg_mask):
    width_dev, length_dev = skip.shape
    taps = conv_weight.shape[0]
    reach = taps // 2
    seq_count, mp_count = lax.axis_size("seq"), lax.axis_size("mp")
    tracks_dev = head_weight.shape[1]
    scale_back = 1.0 / math.sqrt(length_dev * seq_count)
    place, column = lax.axis_index("seq"), lax.axis_index("mp")

    doubled = jnp.repeat(coarse.astype(jnp.float32), 2, axis=1)
    summed = (doubled + skip.astype(jnp.float32)).astype(jnp.bfloat16)
    low = shifted(summed[:, length_dev - reach :], "seq", 1)
    high = shifted(summed[:, :reach], "seq", -1)
    edges = gathered(jnp.concatenate([low, high], axis=1), "mp")
    pieces = gathered(summed, "mp")
    widened = jnp.concatenate(
        [
            jnp.concatenate([edge[:, :reach], piece, edge[:, reach:]], axis=1)
            for edge, piece in zip(edges, pieces)
        ],
        axis=0,
    )
    split = conv_weight.reshape(taps, width_dev, mp_count, width_dev)
    weight = jnp.concatenate(
        [lax.dynamic_index_in_dim(split, column ^ j, 2, keepdims=False) for j in range(mp_count)],
        axis=2,
    )
    head_split = head_weight.reshape(mp_count, width_dev, tracks_dev)
    head = jnp.concatenate(
        [lax.dynamic_index_in_dim(head_split, column ^ j, 0, keepdims=False) for j in range(mp_count)],
        axis=0,
    )
    before = conv_bias[:, None]
    for offset in range(taps):
        before = before + jnp.dot(
            weight[offset],
            widened[:, offset : offset + length_dev],
            preferred_element_type=jnp.float32,
        )
    value, slope = gelu_parts(before)
    hidden = (summed.astype(jnp.float32) + value).astype(jnp.bfloat16)
    hidden_full = jnp.concatenate(gathered(hidden, "mp"), axis=0)
    logits = contract_first(hidden_full, head) + head_bias
    predicted = jax.nn.softplus(logits) + pseudo_count
    observed = counts.astype(jnp.float32)
    sums = jnp.stack([jnp.sum(predicted, axis=0), jnp.sum(observed, axis=0)])
    span = seq_count // seg_mask.shape[0]
    totals = sums
    for step in range(1, span):
        totals = totals + swap(sums, "seq", step)
    mask_row = lax.dynamic_slice_in_dim(seg_mask, place // span, 1, 0).astype(jnp.float32)
    slope_pred = mask_row * (
        1.0 + (multi_weight - 1.0) * totals[1] / totals[0] - multi_weight * observed / predicted
    )
    grad_logits = (slope_pred * jax.nn.sigmoid(logits)).astype(jnp.bfloat16)

    def over_columns(parts):
        rows = parts.reshape(mp_count, width_dev, length_dev)
        small = rows.astype(jnp.bfloat16)
        total = rows[0]
        for j in range(1, mp_count):
            total = total + swap(small[j], "mp", j).astype(jnp.float32)
        return total

    grad_hidden = over_columns(contract_last(head, grad_logits))
    grad_before = (grad_hidden * slope).astype(jnp.bfloat16)
    low = shifted(grad_before[:, length_dev - reach :], "seq", 1)
    high = shifted(grad_before[:, :reach], "seq", -1)
    grad_padded = jnp.concatenate([low, grad_before, high], axis=1)
    carry = 0.0
    for offset in range(taps):
        first = 2 * reach - offset
        carry = carry + contract_first(weight[offset], grad_padded[:, first : first + length_dev])
    grad_input = grad_hidden + over_columns(carry)
    grad_skip = grad_input.astype(jnp.bfloat16)
    grad_coarse = jnp.sum(grad_input.reshape(width_dev, length_dev // 2, 2), axis=2).astype(
        jnp.bfloat16
    )
    grads = jnp.concatenate(
        [contract_last(widened[:, k : k + length_dev], grad_before) for k in range(taps)]
        + [jnp.dot(hidden_full, grad_logits, preferred_element_type=jnp.float32)],
        axis=1,
    )
    grads = grads.reshape(seq_count, -1, grads.shape[1])
    mine = place ^ (column * (seq_count // mp_count))
    grads = scattered(grads, "seq", mine) * scale_back
    grad_conv = grads[:, : taps * width_dev].reshape(-1, taps, width_dev)
    grad_head = grads[:, taps * width_dev :]
    return (grad_skip, grad_coarse, grad_head, grad_conv)


def solution(mesh):
    in_specs = (
        P("mp", "seq"),
        P("mp", "seq"),
        P(None, "mp", None),
        P("mp"),
        P(None, "mp"),
        P("mp"),
        P("seq", "mp"),
        P(None, "mp"),
    )
    out_specs = (P("mp", "seq"), P("mp", "seq"), P("seq", "mp"), P("seq", None, "mp"))
    return jax.shard_map(shards, mesh=mesh, in_specs=in_specs, out_specs=out_specs, check_vma=False)
```

```python
import functools
import math

import jax
import jax.numpy as jnp
from jax import lax
from jax.experimental import pallas as pl
from jax.experimental.pallas import tpu as pltpu
from jax.sharding import PartitionSpec as P

root_two_pi = 0.7978845608028654
cubic_coef = 0.044715
multi_weight = 5.0
pseudo_count = 0.5
edge_rows = 16
edge_lanes = 128
bf16, f32 = jnp.bfloat16, jnp.float32


def swap(block, axis, mask):
    count = lax.axis_size(axis)
    return lax.ppermute(block, axis, [(i, i ^ mask) for i in range(count)])


def shifted(block, axis, step):
    count = lax.axis_size(axis)
    pairs = [(i, i + step) for i in range(count) if 0 <= i + step < count]
    return lax.ppermute(block, axis, pairs)


def gathered(block, axis):
    return [block] + [swap(block, axis, j) for j in range(1, lax.axis_size(axis))]


def staged(low, bits):
    while low < bits:
        wide = 1 if low == 0 else min(2, bits - low)
        yield low, wide
        low += wide


def scattered(parts, axis):
    bits = lax.axis_size(axis).bit_length() - 1
    mine = lax.axis_index(axis)
    for low, wide in staged(0, bits):
        size = 1 << wide
        parts = parts.reshape((parts.shape[0] // size, size) + parts.shape[1:])
        at = (mine >> low) & (size - 1)
        small = parts.astype(bf16)
        kept = lax.dynamic_index_in_dim(parts, at, 1, keepdims=False)
        for step in range(1, size):
            piece = lax.dynamic_index_in_dim(small, at ^ step, 1, keepdims=False)
            kept = kept + swap(piece, axis, step << low).astype(f32)
        parts = kept
    return parts[0]


def totalled(block, axis, span):
    for low, wide in staged(0, span.bit_length() - 1):
        block = sum([swap(block, axis, step << low) for step in range(1, 1 << wide)], block)
    return block


def dot(left, right, dims, precision=None):
    return lax.dot_general(
        left, right, (dims, ((), ())), preferred_element_type=f32, precision=precision
    )


nn, nt, tn = ((1,), (0,)), ((1,), (1,)), ((0,), (0,))


def iota(shape, axis):
    return lax.broadcasted_iota(jnp.int32, shape, axis)


def chosen(shape, pairs):
    rows, columns = iota(shape, 0), iota(shape, 1)
    hit = functools.reduce(jnp.logical_or, [(rows == r) & (columns == c) for r, c in pairs])
    return jnp.where(hit, 1.0, 0.0).astype(bf16)


def call(body, outs, *args, scratch=()):
    return pl.pallas_call(
        body,
        out_shape=[jax.ShapeDtypeStruct(shape, kind) for shape, kind in outs],
        in_specs=[pl.BlockSpec(memory_space=pltpu.VMEM)] * len(args),
        out_specs=[pl.BlockSpec(memory_space=pltpu.VMEM)] * len(outs),
        scratch_shapes=[pltpu.VMEM(shape, kind) for shape, kind in scratch],
    )(*args)


def block_rows(column, j, size):
    return pl.ds(pl.multiple_of((column ^ j) * size, size), size)


def prepare(coarse, skip, counts, summed, ahead, behind, own):
    width, length = skip.shape
    tracks = counts.shape[1]
    pairs = jnp.where(
        iota((coarse.shape[1], length), 0) == iota((coarse.shape[1], length), 1) // 2, 1.0, 0.0
    ).astype(bf16)
    total = (dot(coarse[...], pairs, nn) + skip[...].astype(f32)).astype(bf16)
    summed[...] = total
    for out, picks, slot, row in (
        (ahead, ((0, length - 2), (1, length - 1)), 6, length - 1),
        (behind, ((4, 0), (5, 1)), 7, 0),
        (own, ((2, 0), (3, length - 1)), None, None),
    ):
        rows = dot(chosen((edge_rows, length), picks), total, nt).astype(bf16)
        out[...] = jnp.zeros(out.shape, bf16)
        out[:, :width] = rows
        if slot is not None:
            line = jnp.broadcast_to(counts[row : row + 1, :].astype(f32), (edge_rows, tracks))
            held = out[:, :tracks].astype(f32)
            out[:, :tracks] = jnp.where(iota(held.shape, 0) == slot, line, held).astype(bf16)


def gelu_parts(inputs):
    inner = root_two_pi * (inputs + cubic_coef * inputs * inputs * inputs)
    tangent = jnp.tanh(inner)
    value = 0.5 * inputs * (1.0 + tangent)
    slope = 0.5 * (1.0 + tangent) + 0.5 * inputs * (1.0 - tangent * tangent) * root_two_pi * (
        1.0 + 3.0 * cubic_coef * inputs * inputs
    )
    return value, slope


def assembled(pieces, whole, column, width, length):
    spread = jnp.where(
        iota((edge_rows, edge_lanes), 0) == iota((edge_rows, edge_lanes), 1), 1.0, 0.0
    ).astype(bf16)
    for j, piece in enumerate(pieces):
        rows = block_rows(column, j, width)
        whole[rows, :length] = piece[:width, :]
        whole[rows, length:] = dot(piece[width:, :width], spread, tn).astype(bf16)


def convolve(mp_count, *refs):
    pieces, (weight, bias, message, slopes, full, whole) = refs[:mp_count], refs[mp_count:]
    width = weight.shape[0] // 3
    length = message.shape[1]
    column = lax.axis_index("mp")
    assembled(pieces, whole, column, width, length)
    full[...] = whole[:, :length]
    taps = [dot(weight[k * width : (k + 1) * width, :], whole[...], nn) for k in range(3)]
    lanes = iota((width, length), 1)
    edge = iota((width, edge_lanes), 1)
    inner = (
        taps[1][:, :length]
        + jnp.where(lanes == 0, taps[0][:, length + 1 : length + 2], pltpu.roll(taps[0][:, :length], 1, 1))
        + jnp.where(
            lanes == length - 1,
            taps[2][:, length + 4 : length + 5],
            pltpu.roll(taps[2][:, :length], length - 1, 1),
        )
        + bias[...]
    )
    outer = [
        sum(taps[k][:, length + first + k : length + first + k + 1] for k in range(3)) + bias[...]
        for first in (0, 3)
    ]
    outer = jnp.where(edge == 0, outer[0], jnp.where(edge == 1, outer[1], 0.0))
    own = whole[block_rows(column, 0, width), :].astype(f32)
    beside = jnp.where(edge == 0, own[:, length + 1 : length + 2], own[:, length + 4 : length + 5])
    value, slope = gelu_parts(inner)
    message[:width, :] = (own[:, :length] + value).astype(bf16)
    slopes[:, :length] = slope
    value, slope = gelu_parts(outer)
    hidden = (beside + value).astype(bf16)
    message[width:, :] = jnp.zeros((edge_rows, length), bf16)
    message[width:, :width] = dot(chosen((edge_rows, edge_lanes), ((0, 0), (1, 1))), hidden, nt).astype(bf16)
    slopes[:, length:] = slope


def predict(logits):
    return jnp.maximum(logits, 0.0) + jnp.log1p(jnp.exp(-jnp.abs(logits))) + pseudo_count


def score(mp_count, *refs):
    pieces, (head, bias, counts, logits, sums, full, whole) = refs[:mp_count], refs[mp_count:]
    width = head.shape[0] // mp_count
    length = counts.shape[0]
    assembled(pieces, whole, lax.axis_index("mp"), width, length)
    full[...] = whole[:, :length]
    scores = dot(whole[...], head[...], tn) + bias[...]
    logits[...] = scores[: length + edge_rows, :]
    tracks = head.shape[1]
    pred = jnp.sum(predict(scores[:length, :]), axis=0, keepdims=True)
    seen = jnp.sum(counts[...].astype(f32), axis=0, keepdims=True)
    row = iota((8, tracks), 0)
    sums[...] = jnp.where(row == 0, pred, jnp.where(row == 1, seen, 0.0))


def differentiate(logits, counts, edges, totals, mask, full, slope, grad_head):
    length, tracks = counts.shape
    pred_total, count_total = totals[0:1, :], totals[1:2, :]
    ratio = (multi_weight - 1.0) * count_total / pred_total

    def slope_of(scores, observed):
        inner = 1.0 + ratio - multi_weight * observed / predict(scores)
        return (mask[...] * inner * jax.nn.sigmoid(scores)).astype(bf16)

    slope[:length, :] = slope_of(logits[:length, :], counts[...].astype(f32))
    row = iota((edge_rows, tracks), 0)
    beside = edges[...].astype(f32)
    beside = jnp.where(row == 0, beside[6:7, :tracks], jnp.where(row == 1, beside[7:8, :tracks], 0.0))
    slope[length:, :] = slope_of(logits[length:, :], beside)
    grad_head[...] = dot(full[...], slope[:length, :], nn)


def backward(mp_count, seq_count, *refs):
    slopes, heads = refs[:mp_count], refs[mp_count : 2 * mp_count]
    gelu, full, weight, grads, carry, grad_own, stacked, total = refs[2 * mp_count :]
    width, length = heads[0].shape[0], full.shape[1]
    place, column = lax.axis_index("seq"), lax.axis_index("mp")
    inner = sum(dot(head[...], part[:length, :], nt) for head, part in zip(heads, slopes))
    outer = sum(dot(head[...], part[length:, :], nt) for head, part in zip(heads, slopes))
    middle = (inner * gelu[:, :length]).astype(bf16).astype(f32)
    outer = (outer * gelu[:, length : length + edge_rows]).astype(bf16).astype(f32)
    low = jnp.where(place == 0, 0.0, outer[:, 0:1])
    high = jnp.where(place == seq_count - 1, 0.0, outer[:, 1:2])
    lanes = iota((width, length), 1)
    stacked[:width, :] = jnp.where(lanes == length - 1, high, pltpu.roll(middle, length - 1, 1)).astype(bf16)
    stacked[width : 2 * width, :] = middle.astype(bf16)
    stacked[2 * width :, :] = jnp.where(lanes == 0, low, pltpu.roll(middle, 1, 1)).astype(bf16)
    grads[...] = dot(full[...], stacked[...], nt)
    total[...] = dot(weight[...], stacked[...], tn)
    grad_own[...] = inner + total[block_rows(column, 0, width), :]
    for j in range(1, mp_count):
        carry[j - 1] = total[block_rows(column, j, width), :].astype(bf16)


def finish(mp_count, *refs):
    own, parts, (grad_skip, grad_coarse) = refs[0], refs[1:mp_count], refs[mp_count:]
    total = own[...]
    for part in parts:
        total = total + part[...].astype(f32)
    grad_skip[...] = total.astype(bf16)
    length, half = grad_skip.shape[1], grad_coarse.shape[1]
    pairs = jnp.where(iota((length, half), 0) // 2 == iota((length, half), 1), 1.0, 0.0)
    grad_coarse[...] = dot(total, pairs, nn, lax.Precision.HIGHEST).astype(bf16)


def shards(coarse, skip, conv_weight, conv_bias, head_weight, head_bias, counts, seg_mask):
    width, length = skip.shape
    taps = conv_weight.shape[0]
    seq_count, mp_count = lax.axis_size("seq"), lax.axis_size("mp")
    channels, tracks = head_weight.shape
    scale_back = 1.0 / math.sqrt(length * seq_count)
    place, column = lax.axis_index("seq"), lax.axis_index("mp")
    weight = conv_weight.reshape(taps * width, channels)
    tall = width + edge_rows

    tile = ((edge_rows, length), bf16)
    summed, ahead, behind, own = call(
        prepare, [((width, length), bf16), tile, tile, tile], coarse, skip, counts
    )
    edges = shifted(ahead, "seq", 1) + shifted(behind, "seq", -1) + own
    head_rows = head_weight.reshape(mp_count, width, tracks)
    heads = [lax.dynamic_index_in_dim(head_rows, column, 0, keepdims=False)] + [
        swap(lax.dynamic_index_in_dim(head_rows, column ^ j, 0, keepdims=False), "mp", j)
        for j in range(1, mp_count)
    ]
    pieces = gathered(jnp.concatenate([summed, edges], axis=0), "mp")
    wide = length + edge_lanes
    message, gelu, full_in = call(
        functools.partial(convolve, mp_count),
        [((tall, length), bf16), ((width, wide), f32), ((channels, length), bf16)],
        *pieces, weight, conv_bias[:, None],
        scratch=[((channels, wide), bf16)],
    )
    pieces = gathered(message, "mp")
    logits, sums, full = call(
        functools.partial(score, mp_count),
        [((length + edge_rows, tracks), f32), ((8, tracks), f32), ((channels, length), bf16)],
        *pieces, head_weight, head_bias[None, :], counts,
        scratch=[((channels, wide), bf16)],
    )
    span = seq_count // seg_mask.shape[0]
    totals = totalled(sums, "seq", span)
    mask_row = lax.dynamic_slice_in_dim(seg_mask, place // span, 1, 0).astype(f32)
    slope, grad_head = call(
        differentiate,
        [((length + edge_rows, tracks), bf16), ((channels, tracks), f32)],
        logits, counts, edges, totals, mask_row, full,
    )
    slopes = gathered(slope, "mp")
    grad_head = scattered(grad_head.reshape(seq_count, -1, tracks), "seq") * scale_back
    grads, carry, grad_own = call(
        functools.partial(backward, mp_count, seq_count),
        [((channels, taps * width), f32), ((mp_count - 1, width, length), bf16), ((width, length), f32)],
        *slopes, *heads, gelu, full_in, weight,
        scratch=[((taps * width, length), bf16), ((channels, length), f32)],
    )
    parts = [swap(carry[j - 1], "mp", j) for j in range(1, mp_count)]
    grad_skip, grad_coarse = call(
        functools.partial(finish, mp_count),
        [((width, length), bf16), ((width, length // 2), bf16)],
        grad_own, *parts,
    )
    grads = scattered(grads.reshape(seq_count, -1, taps * width), "seq") * scale_back
    grad_conv = grads.reshape(-1, taps, width)
    return (grad_skip, grad_coarse, grad_head, grad_conv)


def solution(mesh):
    in_specs = (
        P("mp", "seq"),
        P("mp", "seq"),
        P(None, "mp", None),
        P("mp"),
        P(None, "mp"),
        P("mp"),
        P("seq", "mp"),
        P(None, "mp"),
    )
    out_specs = (P("mp", "seq"), P("mp", "seq"), P("seq", "mp"), P("seq", None, "mp"))
    return jax.shard_map(shards, mesh=mesh, in_specs=in_specs, out_specs=out_specs, check_vma=False)
```

```python
import functools
import math

import jax
import jax.numpy as jnp
from jax import lax
from jax.experimental import pallas as pl
from jax.experimental.pallas import tpu as pltpu
from jax.sharding import PartitionSpec as P


root_two_pi = 0.7978845608028654
cubic_coef = 0.044715
multi_weight = 5.0
pseudo_count = 0.5
edge_rows = 16
edge_lanes = 128
bf16, f32 = jnp.bfloat16, jnp.float32


def swap(block, axis, mask):
    count = lax.axis_size(axis)
    return lax.ppermute(block, axis, [(i, i ^ mask) for i in range(count)])


def shifted(block, axis, step):
    count = lax.axis_size(axis)
    pairs = [(i, i + step) for i in range(count) if 0 <= i + step < count]
    return lax.ppermute(block, axis, pairs)


def gathered(block, axis):
    parts = [block]
    for j in range(1, lax.axis_size(axis)):
        parts.append(swap(block, axis, j))
    return parts


def staged(low, bits):
    while low < bits:
        wide = 1 if low == 0 else min(2, bits - low)
        yield low, wide
        low += wide


def scattered(parts, axis):
    bits = lax.axis_size(axis).bit_length() - 1
    mine = lax.axis_index(axis)
    for low, wide in staged(0, bits):
        size = 1 << wide
        parts = parts.reshape((parts.shape[0] // size, size) + parts.shape[1:])
        at = (mine >> low) & (size - 1)
        small = parts.astype(bf16)
        kept = lax.dynamic_index_in_dim(parts, at, 1, keepdims=False)
        for step in range(1, size):
            piece = lax.dynamic_index_in_dim(small, at ^ step, 1, keepdims=False)
            kept = kept + swap(piece, axis, step << low).astype(f32)
        parts = kept
    return parts[0]


def totalled(block, axis, span):
    for low, wide in staged(0, span.bit_length() - 1):
        block = sum([swap(block, axis, step << low) for step in range(1, 1 << wide)], block)
    return block


def dot(left, right, dims, precision=None):
    return lax.dot_general(
        left, right, (dims, ((), ())), preferred_element_type=f32, precision=precision
    )


nn, nt, tn = ((1,), (0,)), ((1,), (1,)), ((0,), (0,))


def iota(shape, axis):
    return lax.broadcasted_iota(jnp.int32, shape, axis)


def chosen(shape, pairs):
    rows, columns = iota(shape, 0), iota(shape, 1)
    hit = functools.reduce(jnp.logical_or, [(rows == r) & (columns == c) for r, c in pairs])
    return jnp.where(hit, 1.0, 0.0).astype(bf16)


def call(body, outs, *args, scratch=(), grant=16 << 20, outside=(), last=False):
    spaces = [pltpu.HBM if i in outside else pltpu.VMEM for i in range(len(args))]
    return pl.pallas_call(
        body,
        out_shape=[
            jax.ShapeDtypeStruct(shape, kind) if last else pltpu.VMEM(shape, kind)
            for shape, kind in outs
        ],
        in_specs=[pl.BlockSpec(memory_space=space) for space in spaces],
        out_specs=[pl.BlockSpec(memory_space=pltpu.VMEM)] * len(outs),
        scratch_shapes=[
            pltpu.SemaphoreType.DMA(shape) if kind is None else pltpu.VMEM(shape, kind)
            for shape, kind in scratch
        ],
        compiler_params=pltpu.CompilerParams(vmem_limit_bytes=grant),
    )(*[pltpu.with_memory_space_constraint(arg, space) for arg, space in zip(args, spaces)])


def block_rows(column, j, size):
    return pl.ds(pl.multiple_of((column ^ j) * size, size), size)


def prepare(coarse_in, skip_in, counts_in, summed, ahead, behind, own, coarse, skip, top, bottom, done):
    width, length = skip.shape
    rows, tracks = top.shape
    copies = [
        pltpu.make_async_copy(source, target, done.at[i])
        for i, (source, target) in enumerate(
            (
                (coarse_in, coarse),
                (skip_in, skip),
                (counts_in.at[pl.ds(0, rows)], top),
                (counts_in.at[pl.ds(length - rows, rows)], bottom),
            )
        )
    ]
    for copy in copies:
        copy.start()
    for copy in copies:
        copy.wait()
    pairs = jnp.where(
        iota((coarse.shape[1], length), 0) == iota((coarse.shape[1], length), 1) // 2, 1.0, 0.0
    ).astype(bf16)
    total = (dot(coarse[...], pairs, nn) + skip[...].astype(f32)).astype(bf16)
    summed[...] = total
    for out, picks, slot, line in (
        (ahead, ((0, length - 2), (1, length - 1)), 6, bottom[rows - 1 : rows, :]),
        (behind, ((4, 0), (5, 1)), 7, top[0:1, :]),
        (own, ((2, 0), (3, length - 1)), None, None),
    ):
        picked = dot(chosen((edge_rows, length), picks), total, nt).astype(bf16)
        out[...] = jnp.zeros(out.shape, bf16)
        out[:, :width] = picked
        if slot is not None:
            line = jnp.broadcast_to(line.astype(f32), (edge_rows, tracks))
            held = picked[:, :tracks].astype(f32)
            out[:, :tracks] = jnp.where(iota(held.shape, 0) == slot, line, held).astype(bf16)


def stage(after, weight_in, weight, done):
    copy = pltpu.make_async_copy(weight_in, weight, done.at[0])
    copy.start()
    copy.wait()


def gelu_parts(inputs):
    inner = root_two_pi * (inputs + cubic_coef * inputs * inputs * inputs)
    tangent = jnp.tanh(inner)
    value = 0.5 * inputs * (1.0 + tangent)
    slope = 0.5 * (1.0 + tangent) + 0.5 * inputs * (1.0 - tangent * tangent) * root_two_pi * (
        1.0 + 3.0 * cubic_coef * inputs * inputs
    )
    return value, slope


def assembled(pieces, whole, column, width, length):
    spread = jnp.where(
        iota((edge_rows, edge_lanes), 0) == iota((edge_rows, edge_lanes), 1), 1.0, 0.0
    ).astype(bf16)
    for j, piece in enumerate(pieces):
        rows = block_rows(column, j, width)
        whole[rows, :length] = piece[:width, :]
        whole[rows, length:] = dot(piece[width:, :width], spread, tn).astype(bf16)


def convolve(mp_count, *refs):
    pieces, (weight, bias, message, slopes, full, whole) = refs[:mp_count], refs[mp_count:]
    width = weight.shape[0] // 3
    length = message.shape[1]
    column = lax.axis_index("mp")
    assembled(pieces, whole, column, width, length)
    full[...] = whole[:, :length]
    taps = [dot(weight[k * width : (k + 1) * width, :], whole[...], nn) for k in range(3)]
    lanes = iota((width, length), 1)
    edge = iota((width, edge_lanes), 1)
    inner = (
        taps[1][:, :length]
        + jnp.where(lanes == 0, taps[0][:, length + 1 : length + 2], pltpu.roll(taps[0][:, :length], 1, 1))
        + jnp.where(
            lanes == length - 1,
            taps[2][:, length + 4 : length + 5],
            pltpu.roll(taps[2][:, :length], length - 1, 1),
        )
        + bias[...]
    )
    outer = [
        sum(taps[k][:, length + first + k : length + first + k + 1] for k in range(3)) + bias[...]
        for first in (0, 3)
    ]
    outer = jnp.where(edge == 0, outer[0], jnp.where(edge == 1, outer[1], 0.0))
    own = whole[block_rows(column, 0, width), :].astype(f32)
    beside = jnp.where(edge == 0, own[:, length + 1 : length + 2], own[:, length + 4 : length + 5])
    value, slope = gelu_parts(inner)
    message[:width, :] = (own[:, :length] + value).astype(bf16)
    slopes[:, :length] = slope
    value, slope = gelu_parts(outer)
    hidden = (beside + value).astype(bf16)
    message[width:, :] = jnp.zeros((edge_rows, length), bf16)
    message[width:, :width] = dot(chosen((edge_rows, edge_lanes), ((0, 0), (1, 1))), hidden, nt).astype(bf16)
    slopes[:, length:] = slope


def predict(logits):
    return jnp.maximum(logits, 0.0) + jnp.log1p(jnp.exp(-jnp.abs(logits))) + pseudo_count


def score(mp_count, *refs):
    pieces, (head, bias, counts, logits, sums, full, whole) = refs[:mp_count], refs[mp_count:]
    width = head.shape[0] // mp_count
    length = counts.shape[0]
    assembled(pieces, whole, lax.axis_index("mp"), width, length)
    full[...] = whole[:, :length]
    scores = dot(whole[...], head[...], tn) + bias[...]
    logits[...] = scores[: length + edge_rows, :]
    tracks = head.shape[1]
    pred = jnp.sum(predict(scores[:length, :]), axis=0, keepdims=True)
    seen = jnp.sum(counts[...].astype(f32), axis=0, keepdims=True)
    row = iota((8, tracks), 0)
    sums[...] = jnp.where(row == 0, pred, jnp.where(row == 1, seen, 0.0))


def differentiate(logits, counts, edges, totals, mask, slope):
    length, tracks = counts.shape
    pred_total, count_total = totals[0:1, :], totals[1:2, :]
    ratio = (multi_weight - 1.0) * count_total / pred_total

    def slope_of(scores, observed):
        inner = 1.0 + ratio - multi_weight * observed / predict(scores)
        return (mask[...] * inner * jax.nn.sigmoid(scores)).astype(bf16)

    slope[:length, :] = slope_of(logits[:length, :], counts[...].astype(f32))
    row = iota((edge_rows, tracks), 0)
    beside = edges[...].astype(f32)
    beside = jnp.where(row == 0, beside[6:7, :tracks], jnp.where(row == 1, beside[7:8, :tracks], 0.0))
    slope[length:, :] = slope_of(logits[length:, :], beside)


def packed(out, base, source, start, chunk, both):
    tiles, half = both // 128, chunk // 2
    for t in range(tiles):
        rows = source[pl.ds(start, chunk), t * 128 : (t + 1) * 128]
        out[base + t * chunk : base + (t + 1) * chunk, :] = rows.astype(out.dtype)
    if both % 128:
        pair = [source[pl.ds(start + i * half, half), tiles * 128 :] for i in range(2)]
        at = base + tiles * chunk
        out[at : at + half, :] = jnp.concatenate(pair, axis=1).astype(out.dtype)


def packed_rows(chunk, both):
    return chunk * both // 128


def backward(mp_count, seq_count, split, *refs):
    slopes, heads = refs[:mp_count], refs[mp_count : 2 * mp_count]
    gelu, full, hidden, weight, *outs = refs[2 * mp_count :]
    own, *outs = outs
    carry, outs = outs[: mp_count - 1], outs[mp_count - 1 :]
    width, length = heads[0].shape[0], full.shape[1]
    tracks = heads[0].shape[1]
    place, column = lax.axis_index("seq"), lax.axis_index("mp")
    inner = sum(dot(head[...], part[:length, :], nt) for head, part in zip(heads, slopes))
    outer = sum(dot(head[...], part[length:, :], nt) for head, part in zip(heads, slopes))
    middle = (inner * gelu[:, :length]).astype(bf16).astype(f32)
    outer = (outer * gelu[:, length : length + edge_rows]).astype(bf16).astype(f32)
    low = jnp.where(place == 0, 0.0, outer[:, 0:1])
    high = jnp.where(place == seq_count - 1, 0.0, outer[:, 1:2])
    lanes = iota((width, length), 1)
    stacked = outs[-1]
    stacked[:width, :] = jnp.where(lanes == length - 1, high, pltpu.roll(middle, length - 1, 1)).astype(bf16)
    stacked[width : 2 * width, :] = middle.astype(bf16)
    stacked[2 * width :, :] = jnp.where(lanes == 0, low, pltpu.roll(middle, 1, 1)).astype(bf16)
    grads, total = outs[-3], outs[-2]
    grads[:, :tracks] = dot(hidden[...], slopes[0][:length, :], nn)
    grads[:, tracks:] = dot(full[...], stacked[...], nt)
    if split:
        kept, sent = outs[:2]
        both = grads.shape[1]
        chunk = full.shape[0] // seq_count
        mine = place & 1
        for q in range(seq_count // 2):
            base = q * packed_rows(chunk, both)
            packed(kept, base, grads, pl.multiple_of((2 * q + mine) * chunk, 8), chunk, both)
            packed(sent, base, grads, pl.multiple_of((2 * q + 1 - mine) * chunk, 8), chunk, both)
    total[...] = dot(weight[...], stacked[...], tn)
    own[...] = inner + total[block_rows(column, 0, width), :]
    for j, out in zip(range(1, mp_count), carry):
        out[...] = total[block_rows(column, j, width), :].astype(bf16)


def quartered(count, kept, got, own, *outs):
    rows = own.shape[0]
    at = lax.axis_index("seq") >> 1
    total = outs[-1]
    total[...] = kept[...] + got[...].astype(f32)
    own[...] = total[pl.ds(pl.multiple_of(at * rows, 8), rows), :]
    for j, out in zip(range(1, count), outs):
        out[...] = total[pl.ds(pl.multiple_of((at ^ j) * rows, 8), rows), :].astype(bf16)


def summed_up(scale, own, *refs):
    *parts, grad_head, grad_conv, whole = refs
    total = own[...]
    for part in parts:
        total = total + part[...].astype(f32)
    total = total * scale
    chunk, both = whole.shape
    if total.shape == whole.shape:
        whole[...] = total
    else:
        tiles, half = both // 128, chunk // 2
        for t in range(tiles):
            whole[:, t * 128 : (t + 1) * 128] = total[t * chunk : (t + 1) * chunk, :]
        for i in range(2 if both % 128 else 0):
            at = tiles * chunk
            whole[i * half : (i + 1) * half, tiles * 128 :] = total[at : at + half, i * 64 : (i + 1) * 64]
    tracks, wide = grad_head.shape[1], grad_conv.shape[2]
    grad_head[...] = whole[:, :tracks]
    for k in range(grad_conv.shape[0]):
        grad_conv[k] = whole[:, tracks + k * wide : tracks + (k + 1) * wide]


def finish(mp_count, *refs):
    own, parts, (grad_skip, grad_coarse) = refs[0], refs[1:mp_count], refs[mp_count:]
    total = own[...]
    for part in parts:
        total = total + part[...].astype(f32)
    grad_skip[...] = total.astype(bf16)
    length, half = grad_skip.shape[1], grad_coarse.shape[1]
    pairs = jnp.where(iota((length, half), 0) // 2 == iota((length, half), 1), 1.0, 0.0)
    grad_coarse[...] = dot(total, pairs, nn, lax.Precision.HIGHEST).astype(bf16)


def shards(coarse, skip, conv_weight, conv_bias, head_weight, head_bias, counts, seg_mask):
    width, length = skip.shape
    taps = conv_weight.shape[0]
    seq_count, mp_count = lax.axis_size("seq"), lax.axis_size("mp")
    channels, tracks = head_weight.shape
    scale_back = 1.0 / math.sqrt(length * seq_count)
    place, column = lax.axis_index("seq"), lax.axis_index("mp")
    weight = conv_weight.reshape(taps * width, channels)
    tall = width + edge_rows

    tile = ((edge_rows, length), bf16)
    summed, ahead, behind, own = call(
        prepare, [((width, length), bf16), tile, tile, tile], coarse, skip, counts,
        scratch=[
            (coarse.shape, bf16), (skip.shape, bf16), ((8, tracks), jnp.int32), ((8, tracks), jnp.int32), ((4,), None),
        ],
        outside=(0, 1, 2),
    )
    low = shifted(ahead, "seq", 1)
    high = shifted(behind, "seq", -1)
    edges = low + high + own
    head_rows = head_weight.reshape(mp_count, width, tracks)
    heads = [lax.dynamic_index_in_dim(head_rows, column, 0, keepdims=False)]
    for j in range(1, mp_count):
        heads.append(swap(lax.dynamic_index_in_dim(head_rows, column ^ j, 0, keepdims=False), "mp", j))
    pieces = gathered(jnp.concatenate([summed, edges], axis=0), "mp")
    (weight,) = call(
        stage, [(weight.shape, bf16)], pieces[0], weight, scratch=[((1,), None)], outside=(1,)
    )
    wide = length + edge_lanes
    message, gelu, full_in = call(
        functools.partial(convolve, mp_count),
        [((tall, length), bf16), ((width, wide), f32), ((channels, length), bf16)],
        *pieces, weight, conv_bias[:, None],
        scratch=[((channels, wide), bf16)],
    )
    pieces = gathered(message, "mp")
    logits, sums, full = call(
        functools.partial(score, mp_count),
        [((length + edge_rows, tracks), f32), ((8, tracks), f32), ((channels, length), bf16)],
        *pieces, head_weight, head_bias[None, :], counts,
        scratch=[((channels, wide), bf16)],
    )
    span = seq_count // seg_mask.shape[0]
    totals = totalled(sums, "seq", span)
    mask_row = lax.dynamic_slice_in_dim(seg_mask, place // span, 1, 0).astype(f32)
    (slope,) = call(
        differentiate, [((length + edge_rows, tracks), bf16)], logits, counts, edges, totals, mask_row
    )
    slopes = gathered(slope, "mp")
    chunk = channels // seq_count
    both = tracks + taps * width
    split = chunk % (2 * edge_rows) == 0 and both % 64 == 0 and len(list(staged(0, seq_count.bit_length() - 1))) == 2
    quarter = (packed_rows(chunk, both), 128)
    half = (seq_count // 2 * quarter[0], 128)
    grads_at = ((channels, both), f32)
    scratch = [((channels, length), f32), ((taps * width, length), bf16)]
    own, *outs = call(
        functools.partial(backward, mp_count, seq_count, split),
        [((width, length), f32)]
        + [((width, length), bf16)] * (mp_count - 1)
        + ([(half, f32), (half, bf16)] if split else [grads_at]),
        *slopes, *heads, gelu, full_in, full, weight,
        scratch=([grads_at] if split else []) + scratch,
    )
    carry, grads = outs[: mp_count - 1], outs[mp_count - 1 :]
    if split:
        got = swap(grads[1], "seq", 1)
    parts = []
    for j in range(mp_count - 1, 0, -1):
        parts.append(swap(carry[j - 1], "mp", j))
    if split:
        count = seq_count // 2
        grad_own, *sends = call(
            functools.partial(quartered, count),
            [(quarter, f32)] + [(quarter, bf16)] * (count - 1),
            grads[0], got,
            scratch=[(half, f32)],
        )
        gots = []
        for j in range(count - 1, 0, -1):
            gots.append(swap(sends[j - 1], "seq", 2 * j))
    else:
        grad_own, gots = scattered(grads[0].reshape(seq_count, chunk, both), "seq"), []
    grad_skip, grad_coarse = call(
        functools.partial(finish, mp_count),
        [((width, length), bf16), ((width, length // 2), bf16)],
        own, *parts, last=True,
    )
    grad_head, grad_conv = call(
        functools.partial(summed_up, scale_back),
        [((chunk, tracks), f32), ((taps, chunk, width), f32)],
        grad_own, *gots, scratch=[((chunk, both), f32)], last=True,
    )
    return (grad_skip, grad_coarse, grad_head, grad_conv.transpose(1, 0, 2))


def solution(mesh):
    in_specs = (
        P("mp", "seq"),
        P("mp", "seq"),
        P(None, "mp", None),
        P("mp"),
        P(None, "mp"),
        P("mp"),
        P("seq", "mp"),
        P(None, "mp"),
    )
    out_specs = (P("mp", "seq"), P("mp", "seq"), P("seq", "mp"), P("seq", None, "mp"))

    return jax.shard_map(shards, mesh=mesh, in_specs=in_specs, out_specs=out_specs, check_vma=False)
```

```python
import functools
import math

import jax
import jax.numpy as jnp
from jax import lax
from jax.experimental import pallas as pl
from jax.experimental.pallas import tpu as pltpu
from jax.sharding import PartitionSpec as P


root_two_pi = 0.7978845608028654
cubic_coef = 0.044715
multi_weight = 5.0
pseudo_count = 0.5
edge_rows = 8
edge_lanes = 128
bf16, f32 = jnp.bfloat16, jnp.float32


def swap(block, axis, mask):
    count = lax.axis_size(axis)
    return lax.ppermute(block, axis, [(i, i ^ mask) for i in range(count)])


def crossed(block, axis):
    count = lax.axis_size(axis)
    pairs = [(i, i + 1) for i in range(1, count - 1, 2)]
    return lax.ppermute(block, axis, pairs + [(b, a) for a, b in pairs])


def gathered(block, axis):
    parts = [block]
    for j in range(1, lax.axis_size(axis)):
        parts.append(swap(block, axis, j))
    return parts


def staged(low, bits):
    while low < bits:
        wide = 1 if low == 0 else min(2, bits - low)
        yield low, wide
        low += wide


def scattered(parts, axis):
    bits = lax.axis_size(axis).bit_length() - 1
    mine = lax.axis_index(axis)
    for low, wide in staged(0, bits):
        size = 1 << wide
        parts = parts.reshape((parts.shape[0] // size, size) + parts.shape[1:])
        at = (mine >> low) & (size - 1)
        small = parts.astype(bf16)
        kept = lax.dynamic_index_in_dim(parts, at, 1, keepdims=False)
        for step in range(1, size):
            piece = lax.dynamic_index_in_dim(small, at ^ step, 1, keepdims=False)
            kept = kept + swap(piece, axis, step << low).astype(f32)
        parts = kept
    return parts[0]


def totalled(block, axis, span):
    for low, wide in staged(0, span.bit_length() - 1):
        parts = []
        for step in range(1, 1 << wide):
            parts.append(swap(block, axis, step << low))
        block = sum(parts, block)
    return block


def dot(left, right, dims, precision=None):
    return lax.dot_general(
        left, right, (dims, ((), ())), preferred_element_type=f32, precision=precision
    )


nn, nt, tn = ((1,), (0,)), ((1,), (1,)), ((0,), (0,))


def iota(shape, axis):
    return lax.broadcasted_iota(jnp.int32, shape, axis)


def chosen(shape, pairs):
    rows, columns = iota(shape, 0), iota(shape, 1)
    hit = functools.reduce(jnp.logical_or, [(rows == r) & (columns == c) for r, c in pairs])
    return jnp.where(hit, 1.0, 0.0).astype(bf16)


def call(body, outs, *args, scratch=(), grant=16 << 20, outside=(), last=False):
    spaces = [pltpu.HBM if i in outside else pltpu.VMEM for i in range(len(args))]
    return pl.pallas_call(
        body,
        out_shape=[
            jax.ShapeDtypeStruct(shape, kind) if last else pltpu.VMEM(shape, kind)
            for shape, kind in outs
        ],
        in_specs=[pl.BlockSpec(memory_space=space) for space in spaces],
        out_specs=[pl.BlockSpec(memory_space=pltpu.VMEM)] * len(outs),
        scratch_shapes=[
            pltpu.SemaphoreType.DMA(shape) if kind is None else pltpu.VMEM(shape, kind)
            for shape, kind in scratch
        ],
        compiler_params=pltpu.CompilerParams(vmem_limit_bytes=grant),
    )(*[pltpu.with_memory_space_constraint(arg, space) for arg, space in zip(args, spaces)])


def block_rows(column, j, size):
    return pl.ds(pl.multiple_of((column ^ j) * size, size), size)


def prepare(coarse_in, skip_in, counts_in, summed, pair, cross, own, coarse, skip, top, bottom, done):
    width, length = skip.shape
    rows, tracks = top.shape
    copies = [
        pltpu.make_async_copy(source, target, done.at[i])
        for i, (source, target) in enumerate(
            (
                (coarse_in, coarse),
                (skip_in, skip),
                (counts_in.at[pl.ds(0, rows)], top),
                (counts_in.at[pl.ds(length - rows, rows)], bottom),
            )
        )
    ]
    for copy in copies:
        copy.start()
    for copy in copies:
        copy.wait()
    pairs = jnp.where(
        iota((coarse.shape[1], length), 0) == iota((coarse.shape[1], length), 1) // 2, 1.0, 0.0
    ).astype(bf16)
    total = (dot(coarse[...], pairs, nn) + skip[...].astype(f32)).astype(bf16)
    summed[...] = total
    slot = iota((edge_rows, tracks), 0)
    ahead = dot(chosen((edge_rows, length), ((0, length - 2), (1, length - 1))), total, nt)
    behind = dot(chosen((edge_rows, length), ((4, 0), (5, 1))), total, nt)
    mine = dot(chosen((edge_rows, length), ((2, 0), (3, length - 1))), total, nt)
    first = jnp.where(slot == 7, top[0:1, :].astype(f32), behind[:, :tracks])
    last = jnp.where(slot == 6, bottom[rows - 1 : rows, :].astype(f32), ahead[:, :tracks])
    even = lax.axis_index("seq") % 2 == 0
    for out, (left, right) in (
        (pair, (jnp.where(even, last, first), jnp.where(even, ahead, behind))),
        (cross, (jnp.where(even, first, last), jnp.where(even, behind, ahead))),
        (own, (mine[:, :tracks], mine)),
    ):
        out[...] = jnp.zeros(out.shape, bf16)
        out[:, :tracks] = left.astype(bf16)
        out[:, tracks:width] = right[:, tracks:].astype(bf16)


def stage(after, weight_in, weight, done):
    copy = pltpu.make_async_copy(weight_in, weight, done.at[0])
    copy.start()
    copy.wait()


def joined(after, *refs):
    *parts, out = refs
    rows = parts[0].shape[0]
    for i, part in enumerate(parts):
        out[i * rows : (i + 1) * rows, :] = part[...]


def gelu_parts(inputs):
    inner = root_two_pi * (inputs + cubic_coef * inputs * inputs * inputs)
    tangent = jnp.tanh(inner)
    value = 0.5 * inputs * (1.0 + tangent)
    slope = 0.5 * (1.0 + tangent) + 0.5 * inputs * (1.0 - tangent * tangent) * root_two_pi * (
        1.0 + 3.0 * cubic_coef * inputs * inputs
    )
    return value, slope


def assembled(pieces, whole, column, width, length):
    spread = jnp.where(
        iota((edge_rows, edge_lanes), 0) == iota((edge_rows, edge_lanes), 1), 1.0, 0.0
    ).astype(bf16)
    for j, piece in enumerate(pieces):
        rows = block_rows(column, j, width)
        whole[rows, :length] = piece[:width, :]
        whole[rows, length:] = dot(piece[width:, :width], spread, tn).astype(bf16)


def convolve(mp_count, *refs):
    pieces, (weight, bias, message, slopes, full, whole) = refs[:mp_count], refs[mp_count:]
    width = weight.shape[0] // 3
    length = message.shape[1]
    column = lax.axis_index("mp")
    assembled(pieces, whole, column, width, length)
    full[...] = whole[:, :length]
    taps = [dot(weight[k * width : (k + 1) * width, :], whole[...], nn) for k in range(3)]
    lanes = iota((width, length), 1)
    edge = iota((width, edge_lanes), 1)
    inner = (
        taps[1][:, :length]
        + jnp.where(lanes == 0, taps[0][:, length + 1 : length + 2], pltpu.roll(taps[0][:, :length], 1, 1))
        + jnp.where(
            lanes == length - 1,
            taps[2][:, length + 4 : length + 5],
            pltpu.roll(taps[2][:, :length], length - 1, 1),
        )
        + bias[...]
    )
    outer = [
        sum(taps[k][:, length + first + k : length + first + k + 1] for k in range(3)) + bias[...]
        for first in (0, 3)
    ]
    outer = jnp.where(edge == 0, outer[0], jnp.where(edge == 1, outer[1], 0.0))
    own = whole[block_rows(column, 0, width), :].astype(f32)
    beside = jnp.where(edge == 0, own[:, length + 1 : length + 2], own[:, length + 4 : length + 5])
    value, slope = gelu_parts(inner)
    message[:width, :] = (own[:, :length] + value).astype(bf16)
    slopes[:, :length] = slope
    value, slope = gelu_parts(outer)
    hidden = (beside + value).astype(bf16)
    message[width:, :] = jnp.zeros((edge_rows, length), bf16)
    message[width:, :width] = dot(chosen((edge_rows, edge_lanes), ((0, 0), (1, 1))), hidden, nt).astype(bf16)
    slopes[:, length:] = slope


def predict(logits):
    return jnp.maximum(logits, 0.0) + jnp.log1p(jnp.exp(-jnp.abs(logits))) + pseudo_count


def score(mp_count, *refs):
    pieces, (head, bias, counts, logits, sums, full, whole) = refs[:mp_count], refs[mp_count:]
    width = head.shape[0] // mp_count
    length = counts.shape[0]
    assembled(pieces, whole, lax.axis_index("mp"), width, length)
    full[...] = whole[:, :length]
    scores = dot(whole[...], head[...], tn) + bias[...]
    logits[...] = scores[: length + edge_rows, :]
    tracks = head.shape[1]
    pred = jnp.sum(predict(scores[:length, :]), axis=0, keepdims=True)
    seen = jnp.sum(counts[...].astype(f32), axis=0, keepdims=True)
    row = iota((8, tracks), 0)
    sums[...] = jnp.where(row == 0, pred, jnp.where(row == 1, seen, 0.0))


def differentiate(logits, counts, edges, totals, mask, slope):
    length, tracks = counts.shape
    pred_total, count_total = totals[0:1, :], totals[1:2, :]
    ratio = (multi_weight - 1.0) * count_total / pred_total

    def slope_of(scores, observed):
        inner = 1.0 + ratio - multi_weight * observed / predict(scores)
        return (mask[...] * inner * jax.nn.sigmoid(scores)).astype(bf16)

    slope[:length, :] = slope_of(logits[:length, :], counts[...].astype(f32))
    row = iota((edge_rows, tracks), 0)
    beside = edges[...].astype(f32)
    beside = jnp.where(row == 0, beside[6:7, :tracks], jnp.where(row == 1, beside[7:8, :tracks], 0.0))
    slope[length:, :] = slope_of(logits[length:, :], beside)


def packed(out, base, source, start, chunk, both):
    tiles, half = both // 128, chunk // 2
    for t in range(tiles):
        rows = source[pl.ds(start, chunk), t * 128 : (t + 1) * 128]
        out[base + t * chunk : base + (t + 1) * chunk, :] = rows.astype(out.dtype)
    if both % 128:
        pair = [source[pl.ds(start + i * half, half), tiles * 128 :] for i in range(2)]
        at = base + tiles * chunk
        out[at : at + half, :] = jnp.concatenate(pair, axis=1).astype(out.dtype)


def packed_rows(chunk, both):
    return chunk * both // 128


def backward(mp_count, seq_count, split, group, *refs):
    slopes, head_own, bundles = refs[:mp_count], refs[mp_count], refs[mp_count + 1 : mp_count + 1 + group]
    gelu, full, hidden, weight, *outs = refs[mp_count + 1 + group :]
    head_rows = outs[-3]
    own, *outs = outs
    carry, outs = outs[: mp_count - 1], outs[mp_count - 1 :]
    width, length = head_own.shape[0], full.shape[1]
    tracks = head_own.shape[1]
    place, column = lax.axis_index("seq"), lax.axis_index("mp")
    part = width // group
    for r, bundle in enumerate(bundles):
        at = pl.multiple_of((((place >> 1) & (group - 1)) ^ r) * part, 16)
        for j in range(mp_count - 1):
            head_rows[j, pl.ds(at, part), :] = bundle[j * part : (j + 1) * part, :]
    heads = [head_own] + [head_rows.at[j] for j in range(mp_count - 1)]
    inner = sum(dot(head[...], part[:length, :], nt) for head, part in zip(heads, slopes))
    outer = sum(dot(head[...], part[length:, :], nt) for head, part in zip(heads, slopes))
    middle = (inner * gelu[:, :length]).astype(bf16).astype(f32)
    outer = (outer * gelu[:, length : length + edge_rows]).astype(bf16).astype(f32)
    low = jnp.where(place == 0, 0.0, outer[:, 0:1])
    high = jnp.where(place == seq_count - 1, 0.0, outer[:, 1:2])
    lanes = iota((width, length), 1)
    stacked = outs[-1]
    stacked[:width, :] = jnp.where(lanes == length - 1, high, pltpu.roll(middle, length - 1, 1)).astype(bf16)
    stacked[width : 2 * width, :] = middle.astype(bf16)
    stacked[2 * width :, :] = jnp.where(lanes == 0, low, pltpu.roll(middle, 1, 1)).astype(bf16)
    grads, total = outs[-4], outs[-2]
    grads[:, :tracks] = dot(hidden[...], slopes[0][:length, :], nn)
    grads[:, tracks:] = dot(full[...], stacked[...], nt)
    if split:
        kept, sent = outs[:2]
        both = grads.shape[1]
        chunk = full.shape[0] // seq_count
        mine = place & 1
        for q in range(seq_count // 2):
            base = q * packed_rows(chunk, both)
            packed(kept, base, grads, pl.multiple_of((2 * q + mine) * chunk, 8), chunk, both)
            packed(sent, base, grads, pl.multiple_of((2 * q + 1 - mine) * chunk, 8), chunk, both)
    total[...] = dot(weight[...], stacked[...], tn)
    own[...] = inner + total[block_rows(column, 0, width), :]
    for j, out in zip(range(1, mp_count), carry):
        out[...] = total[block_rows(column, j, width), :].astype(bf16)


def quartered(count, kept, got, own, *outs):
    rows = own.shape[0]
    at = lax.axis_index("seq") >> 1
    total = outs[-1]
    total[...] = kept[...] + got[...].astype(f32)
    own[...] = total[pl.ds(pl.multiple_of(at * rows, 8), rows), :]
    for j, out in zip(range(1, count), outs):
        out[...] = total[pl.ds(pl.multiple_of((at ^ j) * rows, 8), rows), :].astype(bf16)


def summed_up(scale, own, *refs):
    *parts, grad_head, grad_conv, whole = refs
    total = own[...]
    for part in parts:
        total = total + part[...].astype(f32)
    total = total * scale
    chunk, both = whole.shape
    if total.shape == whole.shape:
        whole[...] = total
    else:
        tiles, half = both // 128, chunk // 2
        for t in range(tiles):
            whole[:, t * 128 : (t + 1) * 128] = total[t * chunk : (t + 1) * chunk, :]
        for i in range(2 if both % 128 else 0):
            at = tiles * chunk
            whole[i * half : (i + 1) * half, tiles * 128 :] = total[at : at + half, i * 64 : (i + 1) * 64]
    tracks, wide = grad_head.shape[1], grad_conv.shape[2]
    grad_head[...] = whole[:, :tracks]
    for k in range(grad_conv.shape[0]):
        grad_conv[k] = whole[:, tracks + k * wide : tracks + (k + 1) * wide]


def finish(mp_count, *refs):
    own, parts, (_, grad_skip, grad_coarse) = refs[0], refs[1:mp_count], refs[mp_count:]
    total = own[...]
    for part in parts:
        total = total + part[...].astype(f32)
    grad_skip[...] = total.astype(bf16)
    length, half = grad_skip.shape[1], grad_coarse.shape[1]
    pairs = jnp.where(iota((length, half), 0) // 2 == iota((length, half), 1), 1.0, 0.0)
    grad_coarse[...] = dot(total, pairs, nn, lax.Precision.HIGHEST).astype(bf16)


def shards(coarse, skip, conv_weight, conv_bias, head_weight, head_bias, counts, seg_mask):
    width, length = skip.shape
    taps = conv_weight.shape[0]
    seq_count, mp_count = lax.axis_size("seq"), lax.axis_size("mp")
    channels, tracks = head_weight.shape
    scale_back = 1.0 / math.sqrt(length * seq_count)
    place, column = lax.axis_index("seq"), lax.axis_index("mp")
    weight = conv_weight.reshape(taps * width, channels)
    tall = width + edge_rows

    tile = ((edge_rows, length), bf16)
    summed, pair, cross, own = call(
        prepare, [((width, length), bf16), tile, tile, tile], coarse, skip, counts,
        scratch=[
            (coarse.shape, bf16), (skip.shape, bf16), ((8, tracks), jnp.int32), ((8, tracks), jnp.int32), ((4,), None),
        ],
        outside=(0, 1, 2),
    )
    cross = crossed(cross, "seq")
    pair = swap(pair, "seq", 1)
    edges = cross + pair + own
    group = min(4, seq_count // 2)
    head_parts = head_weight.reshape(mp_count, group, width // group, tracks)
    head_own = lax.dynamic_index_in_dim(head_weight.reshape(mp_count, width, tracks), column, 0, keepdims=False)
    shares = []
    for j in range(1, mp_count):
        share = lax.dynamic_slice(
            head_parts, (column ^ j, (place >> 1) & (group - 1), 0, 0), (1, 1, width // group, tracks)
        )
        shares.append(swap(share.reshape(width // group, tracks), "mp", j))
    pieces = gathered(jnp.concatenate([summed, edges], axis=0), "mp")
    (weight,) = call(
        stage, [(weight.shape, bf16)], pieces[0], weight, scratch=[((1,), None)], outside=(1,)
    )
    wide = length + edge_lanes
    message, gelu, full_in = call(
        functools.partial(convolve, mp_count),
        [((tall, length), bf16), ((width, wide), f32), ((channels, length), bf16)],
        *pieces, weight, conv_bias[:, None],
        scratch=[((channels, wide), bf16)],
    )
    pieces = gathered(message, "mp")
    (share,) = call(joined, [((width // group * (mp_count - 1), tracks), bf16)], message, *shares)
    bundles = [share]
    for r in range(1, group):
        bundles.append(swap(share, "seq", 2 * r))
    logits, sums, full = call(
        functools.partial(score, mp_count),
        [((length + edge_rows, tracks), f32), ((8, tracks), f32), ((channels, length), bf16)],
        *pieces, head_weight, head_bias[None, :], counts,
        scratch=[((channels, wide), bf16)],
    )
    span = seq_count // seg_mask.shape[0]
    totals = totalled(sums, "seq", span)
    mask_row = lax.dynamic_slice_in_dim(seg_mask, place // span, 1, 0).astype(f32)
    (slope,) = call(
        differentiate, [((length + edge_rows, tracks), bf16)], logits, counts, edges, totals, mask_row
    )
    slopes = gathered(slope, "mp")
    chunk = channels // seq_count
    both = tracks + taps * width
    split = chunk % (2 * edge_rows) == 0 and both % 64 == 0 and len(list(staged(0, seq_count.bit_length() - 1))) == 2
    quarter = (packed_rows(chunk, both), 128)
    half = (seq_count // 2 * quarter[0], 128)
    grads_at = ((channels, both), f32)
    scratch = [((channels, length), f32), ((taps * width, length), bf16)]
    head_at = [((mp_count - 1, width, tracks), bf16)]
    own, *outs = call(
        functools.partial(backward, mp_count, seq_count, split, group),
        [((width, length), f32)]
        + [((width, length), bf16)] * (mp_count - 1)
        + ([(half, f32), (half, bf16)] if split else [grads_at]),
        *slopes, head_own, *bundles, gelu, full_in, full, weight,
        scratch=([grads_at] if split else []) + head_at + scratch,
    )
    carry, grads = outs[: mp_count - 1], outs[mp_count - 1 :]
    if split:
        got = swap(grads[1], "seq", 1)
    parts = []
    for j in range(mp_count - 1, 0, -1):
        parts.append(swap(carry[j - 1], "mp", j))
    if split:
        count = seq_count // 2
        grad_own, *sends = call(
            functools.partial(quartered, count),
            [(quarter, f32)] + [(quarter, bf16)] * (count - 1),
            grads[0], got,
            scratch=[(half, f32)],
        )
        gots = []
        for j in range(count - 1, 0, -1):
            gots.append(swap(sends[j - 1], "seq", 2 * j))
    else:
        grad_own, gots = scattered(grads[0].reshape(seq_count, chunk, both), "seq"), []
    grad_head, grad_conv = call(
        functools.partial(summed_up, scale_back),
        [((chunk, tracks), f32), ((taps, chunk, width), f32)],
        grad_own, *gots, scratch=[((chunk, both), f32)], last=True,
    )
    grad_skip, grad_coarse = call(
        functools.partial(finish, mp_count),
        [((width, length), bf16), ((width, length // 2), bf16)],
        own, *parts, grad_head, outside=(mp_count,), last=True,
    )
    return (grad_skip, grad_coarse, grad_head, grad_conv.transpose(1, 0, 2))


def solution(mesh):
    in_specs = (
        P("mp", "seq"),
        P("mp", "seq"),
        P(None, "mp", None),
        P("mp"),
        P(None, "mp"),
        P("mp"),
        P("seq", "mp"),
        P(None, "mp"),
    )
    out_specs = (P("mp", "seq"), P("mp", "seq"), P("seq", "mp"), P("seq", None, "mp"))

    return jax.shard_map(shards, mesh=mesh, in_specs=in_specs, out_specs=out_specs, check_vma=False)
```

```python
import functools
import math

import jax
import jax.numpy as jnp
from jax import lax
from jax.experimental import pallas as pl
from jax.experimental.pallas import tpu as pltpu
from jax.sharding import PartitionSpec as P


root_two_pi = 0.7978845608028654
cubic_coef = 0.044715
multi_weight = 5.0
pseudo_count = 0.5
edge_rows = 8
edge_lanes = 128
bf16, f32 = jnp.bfloat16, jnp.float32


def swap(block, axis, mask):
    count = lax.axis_size(axis)
    return lax.ppermute(block, axis, [(i, i ^ mask) for i in range(count)])


def crossed(block, axis):
    count = lax.axis_size(axis)
    pairs = [(i, i + 1) for i in range(1, count - 1, 2)]
    return lax.ppermute(block, axis, pairs + [(b, a) for a, b in pairs])


def gathered(block, axis):
    parts = [block]
    for j in range(1, lax.axis_size(axis)):
        parts.append(swap(block, axis, j))
    return parts


def staged(low, bits):
    while low < bits:
        wide = 1 if low == 0 else min(2, bits - low)
        yield low, wide
        low += wide


def scattered(parts, axis):
    bits = lax.axis_size(axis).bit_length() - 1
    mine = lax.axis_index(axis)
    for low, wide in staged(0, bits):
        size = 1 << wide
        parts = parts.reshape((parts.shape[0] // size, size) + parts.shape[1:])
        at = (mine >> low) & (size - 1)
        small = parts.astype(bf16)
        kept = lax.dynamic_index_in_dim(parts, at, 1, keepdims=False)
        for step in range(1, size):
            piece = lax.dynamic_index_in_dim(small, at ^ step, 1, keepdims=False)
            kept = kept + swap(piece, axis, step << low).astype(f32)
        parts = kept
    return parts[0]


def totalled(block, axis, span):
    for low, wide in staged(0, span.bit_length() - 1):
        parts = []
        for step in range(1, 1 << wide):
            parts.append(swap(block, axis, step << low))
        block = sum(parts, block)
    return block


def dot(left, right, dims, precision=None):
    return lax.dot_general(
        left, right, (dims, ((), ())), preferred_element_type=f32, precision=precision
    )


nn, nt, tn = ((1,), (0,)), ((1,), (1,)), ((0,), (0,))


def iota(shape, axis):
    return lax.broadcasted_iota(jnp.int32, shape, axis)


def chosen(shape, pairs):
    rows, columns = iota(shape, 0), iota(shape, 1)
    hit = functools.reduce(jnp.logical_or, [(rows == r) & (columns == c) for r, c in pairs])
    return jnp.where(hit, 1.0, 0.0).astype(bf16)


def call(body, outs, *args, scratch=(), grant=16 << 20, outside=(), last=False):
    spaces = [pltpu.HBM if i in outside else pltpu.VMEM for i in range(len(args))]
    return pl.pallas_call(
        body,
        out_shape=[
            jax.ShapeDtypeStruct(shape, kind) if last else pltpu.VMEM(shape, kind)
            for shape, kind in outs
        ],
        in_specs=[pl.BlockSpec(memory_space=space) for space in spaces],
        out_specs=[pl.BlockSpec(memory_space=pltpu.VMEM)] * len(outs),
        scratch_shapes=[
            pltpu.SemaphoreType.DMA(shape) if kind is None else pltpu.VMEM(shape, kind)
            for shape, kind in scratch
        ],
        compiler_params=pltpu.CompilerParams(vmem_limit_bytes=grant),
    )(*[pltpu.with_memory_space_constraint(arg, space) for arg, space in zip(args, spaces)])


def block_rows(column, j, size):
    return pl.ds(pl.multiple_of((column ^ j) * size, size), size)


def prepare(mp_count, group, coarse_in, skip_in, counts_in, head_in, weight_in, *refs):
    messages, (pair, cross, weight, coarse, skip, top, bottom, done) = refs[: mp_count - 1], refs[mp_count - 1 :]
    width, length = skip.shape
    rows, tracks = top.shape
    place, column = lax.axis_index("seq"), lax.axis_index("mp")
    moves = [
        (coarse_in, coarse),
        (skip_in, skip),
        (counts_in.at[pl.ds(0, rows)], top),
        (counts_in.at[pl.ds(length - rows, rows)], bottom),
        (weight_in, weight),
    ]
    share = width // group
    for j, message in zip(range(1, mp_count), messages):
        for i in range(2):
            start = (column ^ j) * width + ((place >> 1) & (group - 1)) * share + i * (share // 2)
            moves.append(
                (
                    head_in.at[pl.ds(pl.multiple_of(start, 8), share // 2)],
                    message.at[pl.ds(width, share // 2), pl.ds(i * tracks, tracks)],
                )
            )
    copies = [pltpu.make_async_copy(*move, done.at[i]) for i, move in enumerate(moves)]
    for copy in copies:
        copy.start()
    for copy in copies[:4]:
        copy.wait()
    pairs = jnp.where(
        iota((coarse.shape[1], length), 0) == iota((coarse.shape[1], length), 1) // 2, 1.0, 0.0
    ).astype(bf16)
    total = (dot(coarse[...], pairs, nn) + skip[...].astype(f32)).astype(bf16)
    for message in messages:
        message[:width, :] = total
    slot = iota((edge_rows, tracks), 0)
    ahead = dot(chosen((edge_rows, length), ((0, length - 2), (1, length - 1))), total, nt)
    behind = dot(chosen((edge_rows, length), ((4, 0), (5, 1))), total, nt)
    first = jnp.where(slot == 7, top[0:1, :].astype(f32), behind[:, :tracks])
    last = jnp.where(slot == 6, bottom[rows - 1 : rows, :].astype(f32), ahead[:, :tracks])
    even = place % 2 == 0
    for out, left, right in (
        (pair, jnp.where(even, last, first), jnp.where(even, ahead, behind)),
        (cross, jnp.where(even, first, last), jnp.where(even, behind, ahead)),
    ):
        out[...] = jnp.zeros(out.shape, bf16)
        out[:, :tracks] = left.astype(bf16)
        out[:, tracks:width] = right[:, tracks:].astype(bf16)
    for copy in copies[4:]:
        copy.wait()


def gelu_parts(inputs):
    inner = root_two_pi * (inputs + cubic_coef * inputs * inputs * inputs)
    tangent = jnp.tanh(inner)
    value = 0.5 * inputs * (1.0 + tangent)
    slope = 0.5 * (1.0 + tangent) + 0.5 * inputs * (1.0 - tangent * tangent) * root_two_pi * (
        1.0 + 3.0 * cubic_coef * inputs * inputs
    )
    return value, slope


def assembled(blocks, whole, column, width, length):
    spread = jnp.where(
        iota((edge_rows, edge_lanes), 0) == iota((edge_rows, edge_lanes), 1), 1.0, 0.0
    ).astype(bf16)
    for j, (block, edges) in enumerate(blocks):
        rows = block_rows(column, j, width)
        whole[rows, :length] = block
        whole[rows, length:] = dot(edges, spread, tn).astype(bf16)


def regrouped(out, whole, length, halves):
    if not halves:
        out[...] = whole[:, :length]
        return
    mine = lax.axis_index("seq") & 1
    chunk = whole.shape[0] // (2 * halves)
    for q in range(halves):
        for i, core in enumerate((mine, 1 - mine)):
            start = pl.multiple_of((2 * q + core) * chunk, 16)
            at = (i * halves + q) * chunk
            out[at : at + chunk, :] = whole[pl.ds(start, chunk), :length]


def convolve(mp_count, halves, *refs):
    pieces, edges = refs[:mp_count], refs[mp_count : 2 * mp_count]
    weight, bias, message, slopes, full, bundle, whole = refs[2 * mp_count :]
    width = weight.shape[0] // 3
    length = message.shape[1]
    half, tracks = pieces[1].shape[0] - width, bundle.shape[1]
    column = lax.axis_index("mp")
    for j, piece in enumerate(pieces[1:]):
        for i in range(2):
            bundle[(2 * j + i) * half : (2 * j + i + 1) * half, :] = piece[width:, i * tracks : (i + 1) * tracks]
    blocks = [(piece[:width, :], edge[:, :width]) for piece, edge in zip(pieces, edges)]
    assembled(blocks, whole, column, width, length)
    regrouped(full, whole, length, halves)
    taps = [dot(weight[k * width : (k + 1) * width, :], whole[...], nn) for k in range(3)]
    lanes = iota((width, length), 1)
    edge = iota((width, edge_lanes), 1)
    square = (width, width)
    shift = jnp.sum(jnp.where(iota(square, 0) == iota(square, 1), bias[...], 0.0), axis=1, keepdims=True)

    def at(tap, lane):
        return taps[tap][:, lane : lane + 1]

    inner = (
        taps[1][:, :length]
        + jnp.where(lanes == 0, at(0, length + 1), pltpu.roll(taps[0][:, :length], 1, 1))
        + jnp.where(lanes == length - 1, at(2, length + 4), pltpu.roll(taps[2][:, :length], length - 1, 1))
        + shift
    )
    outer = jnp.where(
        edge == 0,
        at(0, length) + at(1, length + 1) + at(2, 0) + shift,
        jnp.where(edge == 1, at(0, length - 1) + at(1, length + 4) + at(2, length + 5) + shift, 0.0),
    )
    own = whole[block_rows(column, 0, width), :].astype(f32)
    beside = jnp.where(edge == 0, own[:, length + 1 : length + 2], own[:, length + 4 : length + 5])
    value, slope = gelu_parts(inner)
    message[:width, :] = (own[:, :length] + value).astype(bf16)
    slopes[:, :length] = slope
    value, slope = gelu_parts(outer)
    hidden = (beside + value).astype(bf16)
    message[width:, :] = jnp.zeros((edge_rows, length), bf16)
    message[width:, :width] = dot(chosen((edge_rows, edge_lanes), ((0, 0), (1, 1))), hidden, nt).astype(bf16)
    slopes[:, length:] = slope


def predict(logits):
    return jnp.maximum(logits, 0.0) + jnp.log1p(jnp.exp(-jnp.abs(logits))) + pseudo_count


def score(mp_count, halves, *refs):
    pieces, (head, bias, counts, logits, sums, full, whole) = refs[:mp_count], refs[mp_count:]
    width = head.shape[0] // mp_count
    length = counts.shape[0]
    blocks = [(piece[:width, :], piece[width:, :width]) for piece in pieces]
    assembled(blocks, whole, lax.axis_index("mp"), width, length)
    regrouped(full, whole, length, halves)
    scores = dot(whole[...], head[...], tn) + bias[...]
    logits[...] = scores[: length + edge_rows, :]
    tracks = head.shape[1]
    pred = jnp.sum(predict(scores[:length, :]), axis=0, keepdims=True)
    seen = jnp.sum(counts[...].astype(f32), axis=0, keepdims=True)
    row = iota((8, tracks), 0)
    sums[...] = jnp.where(row == 0, pred, jnp.where(row == 1, seen, 0.0))


def differentiate(logits, counts, edges, totals, mask, slope):
    length, tracks = counts.shape
    pred_total, count_total = totals[0:1, :], totals[1:2, :]
    ratio = (multi_weight - 1.0) * count_total / pred_total

    def slope_of(scores, observed):
        inner = 1.0 + ratio - multi_weight * observed / predict(scores)
        return (mask[...] * inner * jax.nn.sigmoid(scores)).astype(bf16)

    slope[:length, :] = slope_of(logits[:length, :], counts[...].astype(f32))
    row = iota((edge_rows, tracks), 0)
    beside = edges[...].astype(f32)
    beside = jnp.where(row == 0, beside[6:7, :tracks], jnp.where(row == 1, beside[7:8, :tracks], 0.0))
    slope[length:, :] = slope_of(logits[length:, :], beside)


def packed(out, base, value, start, chunk):
    tiles, half = value.shape[1] // 128, chunk // 2
    for t in range(tiles):
        rows = value[start : start + chunk, t * 128 : (t + 1) * 128]
        out[base + t * chunk : base + (t + 1) * chunk, :] = rows.astype(out.dtype)
    if value.shape[1] % 128:
        pair = [value[start + i * half : start + (i + 1) * half, tiles * 128 :] for i in range(2)]
        at = base + tiles * chunk
        out[at : at + half, :] = jnp.concatenate(pair, axis=1).astype(out.dtype)


def packed_rows(chunk, both):
    return chunk * both // 128


def backward(mp_count, seq_count, split, group, *refs):
    slopes, head_own, bundles = refs[:mp_count], refs[mp_count], refs[mp_count + 1 : mp_count + 1 + group]
    gelu, full, hidden, weight, *outs = refs[mp_count + 1 + group :]
    head_rows = outs[-3]
    own, *outs = outs
    carry, outs = outs[: mp_count - 1], outs[mp_count - 1 :]
    width, length = head_own.shape[0], full.shape[1]
    tracks = head_own.shape[1]
    place, column = lax.axis_index("seq"), lax.axis_index("mp")
    part = width // group
    for r, bundle in enumerate(bundles):
        at = pl.multiple_of((((place >> 1) & (group - 1)) ^ r) * part, 16)
        for j in range(mp_count - 1):
            head_rows[j, pl.ds(at, part), :] = bundle[j * part : (j + 1) * part, :]
    heads = [head_own] + [head_rows.at[j] for j in range(mp_count - 1)]
    inner = sum(dot(head[...], part[:length, :], nt) for head, part in zip(heads, slopes))
    outer = sum(dot(head[...], part[length:, :], nt) for head, part in zip(heads, slopes))
    middle = (inner * gelu[:, :length]).astype(bf16).astype(f32)
    outer = (outer * gelu[:, length : length + edge_rows]).astype(bf16).astype(f32)
    low = jnp.where(place == 0, 0.0, outer[:, 0:1])
    high = jnp.where(place == seq_count - 1, 0.0, outer[:, 1:2])
    lanes = iota((width, length), 1)
    stacked = outs[-1]
    stacked[:width, :] = jnp.where(lanes == length - 1, high, pltpu.roll(middle, length - 1, 1)).astype(bf16)
    stacked[width : 2 * width, :] = middle.astype(bf16)
    stacked[2 * width :, :] = jnp.where(lanes == 0, low, pltpu.roll(middle, 1, 1)).astype(bf16)
    total = outs[-2]
    own_slope = slopes[0][:length, :]
    if split:
        rows = full.shape[0] // 2
        chunk = full.shape[0] // seq_count
        for i, out in ((1, outs[1]), (0, outs[0])):
            at = slice(i * rows, (i + 1) * rows)
            value = jnp.concatenate(
                [dot(hidden[at, :], own_slope, nn), dot(full[at, :], stacked[...], nt)], axis=1
            )
            for q in range(seq_count // 2):
                packed(out, q * packed_rows(chunk, value.shape[1]), value, q * chunk, chunk)
    else:
        grads = outs[0]
        grads[:, :tracks] = dot(hidden[...], own_slope, nn)
        grads[:, tracks:] = dot(full[...], stacked[...], nt)
    total[...] = dot(weight[...], stacked[...], tn)
    own[...] = inner + total[block_rows(column, 0, width), :]
    for j, out in zip(range(1, mp_count), carry):
        out[...] = total[block_rows(column, j, width), :].astype(bf16)


def quartered(count, kept, got, own, *outs):
    rows = own.shape[0]
    at = lax.axis_index("seq") >> 1
    total = outs[-1]
    total[...] = kept[...] + got[...].astype(f32)
    own[...] = total[pl.ds(pl.multiple_of(at * rows, 8), rows), :]
    for j, out in zip(range(1, count), outs):
        out[...] = total[pl.ds(pl.multiple_of((at ^ j) * rows, 8), rows), :].astype(bf16)


def summed_up(scale, own, *refs):
    *parts, grad_head, grad_conv, whole = refs
    total = own[...]
    for part in parts:
        total = total + part[...].astype(f32)
    total = total * scale
    chunk, both = whole.shape
    if total.shape == whole.shape:
        whole[...] = total
    else:
        tiles, half = both // 128, chunk // 2
        for t in range(tiles):
            whole[:, t * 128 : (t + 1) * 128] = total[t * chunk : (t + 1) * chunk, :]
        for i in range(2 if both % 128 else 0):
            at = tiles * chunk
            whole[i * half : (i + 1) * half, tiles * 128 :] = total[at : at + half, i * 64 : (i + 1) * 64]
    tracks, wide = grad_head.shape[1], grad_conv.shape[2]
    grad_head[...] = whole[:, :tracks]
    for k in range(grad_conv.shape[0]):
        grad_conv[k] = whole[:, tracks + k * wide : tracks + (k + 1) * wide]


def finish(mp_count, *refs):
    own, parts, (_, grad_skip, grad_coarse) = refs[0], refs[1:mp_count], refs[mp_count:]
    total = own[...]
    for part in parts:
        total = total + part[...].astype(f32)
    grad_skip[...] = total.astype(bf16)
    length, half = grad_skip.shape[1], grad_coarse.shape[1]
    pairs = jnp.where(iota((length, half), 0) // 2 == iota((length, half), 1), 1.0, 0.0)
    grad_coarse[...] = dot(total, pairs, nn, lax.Precision.HIGHEST).astype(bf16)


def shards(coarse, skip, conv_weight, conv_bias, head_weight, head_bias, counts, seg_mask):
    width, length = skip.shape
    taps = conv_weight.shape[0]
    seq_count, mp_count = lax.axis_size("seq"), lax.axis_size("mp")
    channels, tracks = head_weight.shape
    scale_back = 1.0 / math.sqrt(length * seq_count)
    place, column = lax.axis_index("seq"), lax.axis_index("mp")
    group = min(4, seq_count // 2)
    share = width // group
    chunk = channels // seq_count
    both = tracks + taps * width
    split = chunk % 32 == 0 and both % 64 == 0 and len(list(staged(0, seq_count.bit_length() - 1))) == 2
    halves = seq_count // 2 if split else 0
    tall = width + edge_rows
    tile = ((edge_rows, length), bf16)
    *messages, pair, cross, weight = call(
        functools.partial(prepare, mp_count, group),
        [((width + share // 2, length), bf16)] * (mp_count - 1) + [tile, tile, ((taps * width, channels), bf16)],
        coarse, skip, counts, head_weight, conv_weight.reshape(taps * width, channels),
        scratch=[
            (coarse.shape, bf16), (skip.shape, bf16), ((8, tracks), jnp.int32), ((8, tracks), jnp.int32),
            ((5 + 2 * (mp_count - 1),), None),
        ],
        outside=range(5),
    )
    pieces = [messages[0]]
    for j, message in zip(range(1, mp_count), messages):
        pieces.append(swap(message, "mp", j))
    cross = crossed(cross, "seq")
    pair = swap(pair, "seq", 1)
    edges = cross + pair
    wide = length + edge_lanes
    message, gelu, full_in, bundle = call(
        functools.partial(convolve, mp_count, halves),
        [((tall, length), bf16), ((width, wide), f32), ((channels, length), bf16)]
        + [(((mp_count - 1) * share, tracks), bf16)],
        *pieces, *gathered(edges, "mp"), weight, conv_bias[None, :],
        scratch=[((channels, wide), bf16)],
    )
    pieces = gathered(message, "mp")
    bundles = [bundle]
    for r in range(1, group):
        bundles.append(swap(bundle, "seq", 2 * r))
    head_own = lax.dynamic_index_in_dim(head_weight.reshape(mp_count, width, tracks), column, 0, keepdims=False)
    logits, sums, full = call(
        functools.partial(score, mp_count, halves),
        [((length + edge_rows, tracks), f32), ((8, tracks), f32), ((channels, length), bf16)],
        *pieces, head_weight, head_bias[None, :], counts,
        scratch=[((channels, wide), bf16)],
    )
    span = seq_count // seg_mask.shape[0]
    totals = totalled(sums, "seq", span)
    mask_row = lax.dynamic_slice_in_dim(seg_mask, place // span, 1, 0).astype(f32)
    (slope,) = call(
        differentiate, [((length + edge_rows, tracks), bf16)], logits, counts, edges, totals, mask_row
    )
    slopes = gathered(slope, "mp")
    quarter = (packed_rows(chunk, both), 128)
    half = (seq_count // 2 * quarter[0], 128)
    grads_at = ((channels, both), f32)
    scratch = [((channels, length), f32), ((taps * width, length), bf16)]
    head_at = [((mp_count - 1, width, tracks), bf16)]
    own, *outs = call(
        functools.partial(backward, mp_count, seq_count, split, group),
        [((width, length), f32)]
        + [((width, length), bf16)] * (mp_count - 1)
        + ([(half, f32), (half, bf16)] if split else [grads_at]),
        *slopes, head_own, *bundles, gelu, full_in, full, weight,
        scratch=head_at + scratch,
    )
    carry, grads = outs[: mp_count - 1], outs[mp_count - 1 :]
    if split:
        got = swap(grads[1], "seq", 1)
    parts = []
    for j in range(mp_count - 1, 0, -1):
        parts.append(swap(carry[j - 1], "mp", j))
    if split:
        count = seq_count // 2
        grad_own, *sends = call(
            functools.partial(quartered, count),
            [(quarter, f32)] + [(quarter, bf16)] * (count - 1),
            grads[0], got,
            scratch=[(half, f32)],
        )
        gots = []
        for j in range(count - 1, 0, -1):
            gots.append(swap(sends[j - 1], "seq", 2 * j))
    else:
        grad_own, gots = scattered(grads[0].reshape(seq_count, chunk, both), "seq"), []
    grad_head, grad_conv = call(
        functools.partial(summed_up, scale_back),
        [((chunk, tracks), f32), ((taps, chunk, width), f32)],
        grad_own, *gots, scratch=[((chunk, both), f32)], last=True,
    )
    grad_skip, grad_coarse = call(
        functools.partial(finish, mp_count),
        [((width, length), bf16), ((width, length // 2), bf16)],
        own, *parts, grad_head, outside=(mp_count,), last=True,
    )
    return (grad_skip, grad_coarse, grad_head, grad_conv.transpose(1, 0, 2))


def solution(mesh):
    in_specs = (
        P("mp", "seq"),
        P("mp", "seq"),
        P(None, "mp", None),
        P("mp"),
        P(None, "mp"),
        P("mp"),
        P("seq", "mp"),
        P(None, "mp"),
    )
    out_specs = (P("mp", "seq"), P("mp", "seq"), P("seq", "mp"), P("seq", None, "mp"))

    return jax.shard_map(shards, mesh=mesh, in_specs=in_specs, out_specs=out_specs, check_vma=False)
```

```python
import functools
import math

import jax
import jax.numpy as jnp
from jax import lax
from jax.experimental import pallas as pl
from jax.experimental.pallas import tpu as pltpu
from jax.sharding import PartitionSpec as P


root_two_pi = 0.7978845608028654
cubic_coef = 0.044715
multi_weight = 5.0
pseudo_count = 0.5
edge_rows = 8
edge_lanes = 128
bf16, f32 = jnp.bfloat16, jnp.float32


def swap(block, axis, mask):
    count = lax.axis_size(axis)
    return lax.ppermute(block, axis, [(i, i ^ mask) for i in range(count)])


def crossed(block, axis):
    count = lax.axis_size(axis)
    pairs = [(i, i + 1) for i in range(1, count - 1, 2)]
    return lax.ppermute(block, axis, pairs + [(b, a) for a, b in pairs])


def gathered(block, axis):
    parts = [block]
    for j in range(1, lax.axis_size(axis)):
        parts.append(swap(block, axis, j))
    return parts


def staged(low, bits):
    while low < bits:
        wide = 1 if low == 0 else min(2, bits - low)
        yield low, wide
        low += wide


def scattered(parts, axis):
    bits = lax.axis_size(axis).bit_length() - 1
    mine = lax.axis_index(axis)
    for low, wide in staged(0, bits):
        size = 1 << wide
        parts = parts.reshape((parts.shape[0] // size, size) + parts.shape[1:])
        at = (mine >> low) & (size - 1)
        small = parts.astype(bf16)
        kept = lax.dynamic_index_in_dim(parts, at, 1, keepdims=False)
        for step in range(1, size):
            piece = lax.dynamic_index_in_dim(small, at ^ step, 1, keepdims=False)
            kept = kept + swap(piece, axis, step << low).astype(f32)
        parts = kept
    return parts[0]


def totalled(block, axis, span):
    for low, wide in staged(0, span.bit_length() - 1):
        parts = []
        for step in range(1, 1 << wide):
            parts.append(swap(block, axis, step << low))
        block = sum(parts, block)
    return block


def dot(left, right, dims, precision=None):
    return lax.dot_general(
        left, right, (dims, ((), ())), preferred_element_type=f32, precision=precision
    )


nn, nt, tn = ((1,), (0,)), ((1,), (1,)), ((0,), (0,))


def iota(shape, axis):
    return lax.broadcasted_iota(jnp.int32, shape, axis)


def chosen(shape, pairs):
    rows, columns = iota(shape, 0), iota(shape, 1)
    hit = functools.reduce(jnp.logical_or, [(rows == r) & (columns == c) for r, c in pairs])
    return jnp.where(hit, 1.0, 0.0).astype(bf16)


def call(body, outs, *args, scratch=(), grant=16 << 20, outside=(), last=False):
    spaces = [pltpu.HBM if i in outside else pltpu.VMEM for i in range(len(args))]
    return pl.pallas_call(
        body,
        out_shape=[
            jax.ShapeDtypeStruct(shape, kind) if last else pltpu.VMEM(shape, kind)
            for shape, kind in outs
        ],
        in_specs=[pl.BlockSpec(memory_space=space) for space in spaces],
        out_specs=[pl.BlockSpec(memory_space=pltpu.HBM if last else pltpu.VMEM)] * len(outs),
        scratch_shapes=[
            pltpu.SemaphoreType.DMA(shape) if kind is None else pltpu.VMEM(shape, kind)
            for shape, kind in scratch
        ],
        compiler_params=pltpu.CompilerParams(vmem_limit_bytes=grant),
    )(*[pltpu.with_memory_space_constraint(arg, space) for arg, space in zip(args, spaces)])


def block_rows(column, j, size):
    return pl.ds(pl.multiple_of((column ^ j) * size, size), size)


def prepare(mp_count, group, coarse_in, skip_in, counts_in, head_in, weight_in, *refs):
    messages, (pair, cross, weight, coarse, skip, top, bottom, done) = refs[: mp_count - 1], refs[mp_count - 1 :]
    width, length = skip.shape
    rows, tracks = top.shape
    place, column = lax.axis_index("seq"), lax.axis_index("mp")
    moves = [
        (coarse_in, coarse),
        (skip_in, skip),
        (counts_in.at[pl.ds(0, rows)], top),
        (counts_in.at[pl.ds(length - rows, rows)], bottom),
        (weight_in, weight),
    ]
    share = width // group
    for j, message in zip(range(1, mp_count), messages):
        for i in range(2):
            start = (column ^ j) * width + ((place >> 1) & (group - 1)) * share + i * (share // 2)
            moves.append(
                (
                    head_in.at[pl.ds(pl.multiple_of(start, 8), share // 2)],
                    message.at[pl.ds(width, share // 2), pl.ds(i * tracks, tracks)],
                )
            )
    copies = [pltpu.make_async_copy(*move, done.at[i]) for i, move in enumerate(moves)]
    for copy in copies:
        copy.start()
    for copy in copies[:4]:
        copy.wait()
    pairs = jnp.where(
        iota((coarse.shape[1], length), 0) == iota((coarse.shape[1], length), 1) // 2, 1.0, 0.0
    ).astype(bf16)
    total = (dot(coarse[...], pairs, nn) + skip[...].astype(f32)).astype(bf16)
    for message in messages:
        message[:width, :] = total
    slot = iota((edge_rows, tracks), 0)
    ahead = dot(chosen((edge_rows, length), ((0, length - 2), (1, length - 1))), total, nt)
    behind = dot(chosen((edge_rows, length), ((4, 0), (5, 1))), total, nt)
    first = jnp.where(slot == 7, top[0:1, :].astype(f32), behind[:, :tracks])
    last = jnp.where(slot == 6, bottom[rows - 1 : rows, :].astype(f32), ahead[:, :tracks])
    even = place % 2 == 0
    for out, left, right in (
        (pair, jnp.where(even, last, first), jnp.where(even, ahead, behind)),
        (cross, jnp.where(even, first, last), jnp.where(even, behind, ahead)),
    ):
        out[...] = jnp.zeros(out.shape, bf16)
        out[:, :tracks] = left.astype(bf16)
        out[:, tracks:width] = right[:, tracks:].astype(bf16)
    for copy in copies[4:]:
        copy.wait()


def gelu_parts(inputs):
    inner = root_two_pi * (inputs + cubic_coef * inputs * inputs * inputs)
    tangent = jnp.tanh(inner)
    value = 0.5 * inputs * (1.0 + tangent)
    slope = 0.5 * (1.0 + tangent) + 0.5 * inputs * (1.0 - tangent * tangent) * root_two_pi * (
        1.0 + 3.0 * cubic_coef * inputs * inputs
    )
    return value, slope


def assembled(blocks, whole, column, width, length):
    spread = jnp.where(
        iota((edge_rows, edge_lanes), 0) == iota((edge_rows, edge_lanes), 1), 1.0, 0.0
    ).astype(bf16)
    for j, (block, edges) in enumerate(blocks):
        rows = block_rows(column, j, width)
        whole[rows, :length] = block
        whole[rows, length:] = dot(edges, spread, tn).astype(bf16)


def regrouped(out, whole, length, halves):
    if not halves:
        out[...] = whole[:, :length]
        return
    mine = lax.axis_index("seq") & 1
    chunk = whole.shape[0] // (2 * halves)
    for q in range(halves):
        for i, core in enumerate((mine, 1 - mine)):
            start = pl.multiple_of((2 * q + core) * chunk, 16)
            at = (i * halves + q) * chunk
            out[at : at + chunk, :] = whole[pl.ds(start, chunk), :length]


def convolve(mp_count, halves, *refs):
    pieces, edges = refs[:mp_count], refs[mp_count : 2 * mp_count]
    weight, bias, message, slopes, full, bundle, whole = refs[2 * mp_count :]
    width = weight.shape[0] // 3
    length = message.shape[1]
    half, tracks = pieces[1].shape[0] - width, bundle.shape[1]
    column = lax.axis_index("mp")
    for j, piece in enumerate(pieces[1:]):
        for i in range(2):
            bundle[(2 * j + i) * half : (2 * j + i + 1) * half, :] = piece[width:, i * tracks : (i + 1) * tracks]
    blocks = [(piece[:width, :], edge[:, :width]) for piece, edge in zip(pieces, edges)]
    assembled(blocks, whole, column, width, length)
    regrouped(full, whole, length, halves)
    taps = [dot(weight[k * width : (k + 1) * width, :], whole[...], nn) for k in range(3)]
    lanes = iota((width, length), 1)
    edge = iota((width, edge_lanes), 1)
    square = (width, width)
    shift = jnp.sum(jnp.where(iota(square, 0) == iota(square, 1), bias[...], 0.0), axis=1, keepdims=True)

    def at(tap, lane):
        return taps[tap][:, lane : lane + 1]

    inner = (
        taps[1][:, :length]
        + jnp.where(lanes == 0, at(0, length + 1), pltpu.roll(taps[0][:, :length], 1, 1))
        + jnp.where(lanes == length - 1, at(2, length + 4), pltpu.roll(taps[2][:, :length], length - 1, 1))
        + shift
    )
    outer = jnp.where(
        edge == 0,
        at(0, length) + at(1, length + 1) + at(2, 0) + shift,
        jnp.where(edge == 1, at(0, length - 1) + at(1, length + 4) + at(2, length + 5) + shift, 0.0),
    )
    own = whole[block_rows(column, 0, width), :].astype(f32)
    beside = jnp.where(edge == 0, own[:, length + 1 : length + 2], own[:, length + 4 : length + 5])
    value, slope = gelu_parts(inner)
    message[:width, :] = (own[:, :length] + value).astype(bf16)
    slopes[:, :length] = slope
    value, slope = gelu_parts(outer)
    hidden = (beside + value).astype(bf16)
    message[width:, :] = jnp.zeros((edge_rows, length), bf16)
    message[width:, :width] = dot(chosen((edge_rows, edge_lanes), ((0, 0), (1, 1))), hidden, nt).astype(bf16)
    slopes[:, length:] = slope


def predict(logits):
    return jnp.maximum(logits, 0.0) + jnp.log1p(jnp.exp(-jnp.abs(logits))) + pseudo_count


def score(mp_count, halves, *refs):
    pieces, (head, bias, counts, logits, sums, full, whole) = refs[:mp_count], refs[mp_count:]
    width = head.shape[0] // mp_count
    length = counts.shape[0]
    blocks = [(piece[:width, :], piece[width:, :width]) for piece in pieces]
    assembled(blocks, whole, lax.axis_index("mp"), width, length)
    regrouped(full, whole, length, halves)
    scores = dot(whole[...], head[...], tn) + bias[...]
    logits[...] = scores[: length + edge_rows, :]
    tracks = head.shape[1]
    pred = jnp.sum(predict(scores[:length, :]), axis=0, keepdims=True)
    seen = jnp.sum(counts[...].astype(f32), axis=0, keepdims=True)
    row = iota((8, tracks), 0)
    sums[...] = jnp.where(row == 0, pred, jnp.where(row == 1, seen, 0.0))


def differentiate(logits, counts, edges, totals, mask, slope):
    length, tracks = counts.shape
    pred_total, count_total = totals[0:1, :], totals[1:2, :]
    ratio = (multi_weight - 1.0) * count_total / pred_total

    def slope_of(scores, observed):
        inner = 1.0 + ratio - multi_weight * observed / predict(scores)
        return (mask[...] * inner * jax.nn.sigmoid(scores)).astype(bf16)

    slope[:length, :] = slope_of(logits[:length, :], counts[...].astype(f32))
    row = iota((edge_rows, tracks), 0)
    beside = edges[...].astype(f32)
    beside = jnp.where(row == 0, beside[6:7, :tracks], jnp.where(row == 1, beside[7:8, :tracks], 0.0))
    slope[length:, :] = slope_of(logits[length:, :], beside)


def packed(out, base, value, start, chunk):
    tiles, half = value.shape[1] // 128, chunk // 2
    for t in range(tiles):
        rows = value[start : start + chunk, t * 128 : (t + 1) * 128]
        out[base + t * chunk : base + (t + 1) * chunk, :] = rows.astype(out.dtype)
    if value.shape[1] % 128:
        pair = [value[start + i * half : start + (i + 1) * half, tiles * 128 :] for i in range(2)]
        at = base + tiles * chunk
        out[at : at + half, :] = jnp.concatenate(pair, axis=1).astype(out.dtype)


def packed_rows(chunk, both):
    return chunk * both // 128


def backward(mp_count, seq_count, split, group, *refs):
    slopes, head_own, bundles = refs[:mp_count], refs[mp_count], refs[mp_count + 1 : mp_count + 1 + group]
    gelu, full, hidden, weight, *outs = refs[mp_count + 1 + group :]
    head_rows = outs[-3]
    own, *outs = outs
    carry, outs = outs[: mp_count - 1], outs[mp_count - 1 :]
    width, length = head_own.shape[0], full.shape[1]
    tracks = head_own.shape[1]
    place, column = lax.axis_index("seq"), lax.axis_index("mp")
    part = width // group
    for r, bundle in enumerate(bundles):
        at = pl.multiple_of((((place >> 1) & (group - 1)) ^ r) * part, 16)
        for j in range(mp_count - 1):
            head_rows[j, pl.ds(at, part), :] = bundle[j * part : (j + 1) * part, :]
    heads = [head_own] + [head_rows.at[j] for j in range(mp_count - 1)]
    inner = sum(dot(head[...], part[:length, :], nt) for head, part in zip(heads, slopes))
    outer = sum(dot(head[...], part[length:, :], nt) for head, part in zip(heads, slopes))
    middle = (inner * gelu[:, :length]).astype(bf16).astype(f32)
    outer = (outer * gelu[:, length : length + edge_rows]).astype(bf16).astype(f32)
    low = jnp.where(place == 0, 0.0, outer[:, 0:1])
    high = jnp.where(place == seq_count - 1, 0.0, outer[:, 1:2])
    lanes = iota((width, length), 1)
    stacked = outs[-1]
    stacked[:width, :] = jnp.where(lanes == length - 1, high, pltpu.roll(middle, length - 1, 1)).astype(bf16)
    stacked[width : 2 * width, :] = middle.astype(bf16)
    stacked[2 * width :, :] = jnp.where(lanes == 0, low, pltpu.roll(middle, 1, 1)).astype(bf16)
    total = outs[-2]
    own_slope = slopes[0][:length, :]
    if split:
        rows = full.shape[0] // 2
        chunk = full.shape[0] // seq_count
        for i, out in ((1, outs[1]), (0, outs[0])):
            at = slice(i * rows, (i + 1) * rows)
            value = jnp.concatenate(
                [dot(hidden[at, :], own_slope, nn), dot(full[at, :], stacked[...], nt)], axis=1
            )
            for q in range(seq_count // 2):
                packed(out, q * packed_rows(chunk, value.shape[1]), value, q * chunk, chunk)
    else:
        grads = outs[0]
        grads[:, :tracks] = dot(hidden[...], own_slope, nn)
        grads[:, tracks:] = dot(full[...], stacked[...], nt)
    total[...] = dot(weight[...], stacked[...], tn)
    own[...] = inner + total[block_rows(column, 0, width), :]
    for j, out in zip(range(1, mp_count), carry):
        out[...] = total[block_rows(column, j, width), :].astype(bf16)


def quartered(count, kept, got, own, *outs):
    rows = own.shape[0]
    at = lax.axis_index("seq") >> 1
    total = outs[-1]
    total[...] = kept[...] + got[...].astype(f32)
    own[...] = total[pl.ds(pl.multiple_of(at * rows, 8), rows), :]
    for j, out in zip(range(1, count), outs):
        out[...] = total[pl.ds(pl.multiple_of((at ^ j) * rows, 8), rows), :].astype(bf16)


def unpacked(whole, total):
    chunk, both = whole.shape
    if total.shape == whole.shape:
        whole[...] = total
        return
    tiles, half = both // 128, chunk // 2
    for t in range(tiles):
        whole[:, t * 128 : (t + 1) * 128] = total[t * chunk : (t + 1) * chunk, :]
    for i in range(2 if both % 128 else 0):
        at = tiles * chunk
        whole[i * half : (i + 1) * half, tiles * 128 :] = total[at : at + half, i * 64 : (i + 1) * 64]


def finish(mp_count, scale, *refs):
    carried, rest = refs[:mp_count], refs[mp_count:]
    *summands, grad_skip, grad_coarse, grad_head, grad_conv, skip, coarse, whole, conv, done = rest
    total = summands[0][...]
    for part in summands[1:]:
        total = total + part[...].astype(f32)
    unpacked(whole, total * scale)
    tracks, wide = grad_head.shape[1], grad_conv.shape[2]
    copies = [pltpu.make_async_copy(whole.at[:, pl.ds(0, tracks)], grad_head, done.at[0])]
    copies[0].start()
    for k in range(grad_conv.shape[0]):
        conv[k] = whole[:, tracks + k * wide : tracks + (k + 1) * wide]
    copies.append(pltpu.make_async_copy(conv, grad_conv, done.at[1]))
    copies[1].start()
    total = carried[0][...]
    for part in carried[1:]:
        total = total + part[...].astype(f32)
    skip[...] = total.astype(bf16)
    copies.append(pltpu.make_async_copy(skip, grad_skip, done.at[2]))
    copies[2].start()
    length, half = grad_skip.shape[1], grad_coarse.shape[1]
    pairs = jnp.where(iota((length, half), 0) // 2 == iota((length, half), 1), 1.0, 0.0).astype(bf16)
    terms, left = [], total
    for _ in range(3):
        terms.append(left.astype(bf16))
        left = left - terms[-1].astype(f32)
    coarse[...] = sum(dot(term, pairs, nn) for term in terms).astype(bf16)
    copies.append(pltpu.make_async_copy(coarse, grad_coarse, done.at[3]))
    copies[3].start()
    for copy in copies:
        copy.wait()


def shards(coarse, skip, conv_weight, conv_bias, head_weight, head_bias, counts, seg_mask):
    width, length = skip.shape
    taps = conv_weight.shape[0]
    seq_count, mp_count = lax.axis_size("seq"), lax.axis_size("mp")
    channels, tracks = head_weight.shape
    scale_back = 1.0 / math.sqrt(length * seq_count)
    place, column = lax.axis_index("seq"), lax.axis_index("mp")
    group = min(4, seq_count // 2)
    share = width // group
    chunk = channels // seq_count
    both = tracks + taps * width
    split = chunk % 32 == 0 and both % 64 == 0 and len(list(staged(0, seq_count.bit_length() - 1))) == 2
    halves = seq_count // 2 if split else 0
    tall = width + edge_rows
    tile = ((edge_rows, length), bf16)
    *messages, pair, cross, weight = call(
        functools.partial(prepare, mp_count, group),
        [((width + share // 2, length), bf16)] * (mp_count - 1) + [tile, tile, ((taps * width, channels), bf16)],
        coarse, skip, counts, head_weight, conv_weight.reshape(taps * width, channels),
        scratch=[
            (coarse.shape, bf16), (skip.shape, bf16), ((8, tracks), jnp.int32), ((8, tracks), jnp.int32),
            ((5 + 2 * (mp_count - 1),), None),
        ],
        outside=range(5),
    )
    pieces = [messages[0]]
    for j, message in zip(range(1, mp_count), messages):
        pieces.append(swap(message, "mp", j))
    cross = crossed(cross, "seq")
    pair = swap(pair, "seq", 1)
    edges = cross + pair
    wide = length + edge_lanes
    message, gelu, full_in, bundle = call(
        functools.partial(convolve, mp_count, halves),
        [((tall, length), bf16), ((width, wide), f32), ((channels, length), bf16)]
        + [(((mp_count - 1) * share, tracks), bf16)],
        *pieces, *gathered(edges, "mp"), weight, conv_bias[None, :],
        scratch=[((channels, wide), bf16)],
    )
    pieces = gathered(message, "mp")
    bundles = [bundle]
    for r in range(1, group):
        bundles.append(swap(bundle, "seq", 2 * r))
    head_own = lax.dynamic_index_in_dim(head_weight.reshape(mp_count, width, tracks), column, 0, keepdims=False)
    logits, sums, full = call(
        functools.partial(score, mp_count, halves),
        [((length + edge_rows, tracks), f32), ((8, tracks), f32), ((channels, length), bf16)],
        *pieces, head_weight, head_bias[None, :], counts,
        scratch=[((channels, wide), bf16)],
    )
    span = seq_count // seg_mask.shape[0]
    totals = totalled(sums, "seq", span)
    mask_row = lax.dynamic_slice_in_dim(seg_mask, place // span, 1, 0).astype(f32)
    (slope,) = call(
        differentiate, [((length + edge_rows, tracks), bf16)], logits, counts, edges, totals, mask_row
    )
    slopes = gathered(slope, "mp")
    quarter = (packed_rows(chunk, both), 128)
    half = (seq_count // 2 * quarter[0], 128)
    grads_at = ((channels, both), f32)
    scratch = [((channels, length), f32), ((taps * width, length), bf16)]
    head_at = [((mp_count - 1, width, tracks), bf16)]
    own, *outs = call(
        functools.partial(backward, mp_count, seq_count, split, group),
        [((width, length), f32)]
        + [((width, length), bf16)] * (mp_count - 1)
        + ([(half, f32), (half, bf16)] if split else [grads_at]),
        *slopes, head_own, *bundles, gelu, full_in, full, weight,
        scratch=head_at + scratch,
    )
    carry, grads = outs[: mp_count - 1], outs[mp_count - 1 :]
    if split:
        got = swap(grads[1], "seq", 1)
    parts = []
    for j in range(mp_count - 1, 0, -1):
        parts.append(swap(carry[j - 1], "mp", j))
    if split:
        count = seq_count // 2
        grad_own, *sends = call(
            functools.partial(quartered, count),
            [(quarter, f32)] + [(quarter, bf16)] * (count - 1),
            grads[0], got,
            scratch=[(half, f32)],
        )
        gots = []
        for j in range(count - 1, 0, -1):
            gots.append(swap(sends[j - 1], "seq", 2 * j))
    else:
        grad_own, gots = scattered(grads[0].reshape(seq_count, chunk, both), "seq"), []
    outs = [((width, length), bf16), ((width, length // 2), bf16), ((chunk, tracks), f32), ((taps, chunk, width), f32)]
    grad_skip, grad_coarse, grad_head, grad_conv = call(
        functools.partial(finish, mp_count, scale_back),
        outs,
        own, *parts, grad_own, *gots,
        scratch=outs[:2] + [((chunk, both), f32), outs[3], ((len(outs),), None)],
        last=True,
    )
    return (grad_skip, grad_coarse, grad_head, grad_conv.transpose(1, 0, 2))


def solution(mesh):
    in_specs = (
        P("mp", "seq"),
        P("mp", "seq"),
        P(None, "mp", None),
        P("mp"),
        P(None, "mp"),
        P("mp"),
        P("seq", "mp"),
        P(None, "mp"),
    )
    out_specs = (P("mp", "seq"), P("mp", "seq"), P("seq", "mp"), P("seq", None, "mp"))

    return jax.shard_map(shards, mesh=mesh, in_specs=in_specs, out_specs=out_specs, check_vma=False)
```

```python
import functools
import math

import jax
import jax.numpy as jnp
from jax import lax
from jax.experimental import pallas as pl
from jax.experimental.pallas import tpu as pltpu
from jax.sharding import PartitionSpec as P


root_two_pi = 0.7978845608028654
cubic_coef = 0.044715
multi_weight = 5.0
pseudo_count = 0.5
edge_rows = 8
bf16, f32 = jnp.bfloat16, jnp.float32


def swap(block, axis, mask):
    count = lax.axis_size(axis)
    return lax.ppermute(block, axis, [(i, i ^ mask) for i in range(count)])


def crossed(block, axis):
    count = lax.axis_size(axis)
    pairs = [(i, i + 1) for i in range(1, count - 1, 2)]
    return lax.ppermute(block, axis, pairs + [(b, a) for a, b in pairs])


def gathered(block, axis):
    parts = [block]
    for j in range(1, lax.axis_size(axis)):
        parts.append(swap(block, axis, j))
    return parts


def staged(low, bits):
    while low < bits:
        wide = 1 if low == 0 else min(2, bits - low)
        yield low, wide
        low += wide


def scattered(parts, axis):
    bits = lax.axis_size(axis).bit_length() - 1
    mine = lax.axis_index(axis)
    for low, wide in staged(0, bits):
        size = 1 << wide
        parts = parts.reshape((parts.shape[0] // size, size) + parts.shape[1:])
        at = (mine >> low) & (size - 1)
        small = parts.astype(bf16)
        kept = lax.dynamic_index_in_dim(parts, at, 1, keepdims=False)
        for step in range(1, size):
            piece = lax.dynamic_index_in_dim(small, at ^ step, 1, keepdims=False)
            kept = kept + swap(piece, axis, step << low).astype(f32)
        parts = kept
    return parts[0]


def totalled(block, axis, span):
    for low, wide in staged(0, span.bit_length() - 1):
        parts = []
        for step in range(1, 1 << wide):
            parts.append(swap(block, axis, step << low))
        block = sum(parts, block)
    return block


def dot(left, right, dims, precision=None):
    return lax.dot_general(
        left, right, (dims, ((), ())), preferred_element_type=f32, precision=precision
    )


nn, nt, tn = ((1,), (0,)), ((1,), (1,)), ((0,), (0,))


def iota(shape, axis):
    return lax.broadcasted_iota(jnp.int32, shape, axis)


def chosen(shape, pairs):
    rows, columns = iota(shape, 0), iota(shape, 1)
    hit = functools.reduce(jnp.logical_or, [(rows == r) & (columns == c) for r, c in pairs])
    return jnp.where(hit, 1.0, 0.0).astype(bf16)


def call(body, outs, *args, scratch=(), grant=16 << 20, outside=(), last=False):
    spaces = [pltpu.HBM if i in outside else pltpu.VMEM for i in range(len(args))]
    return pl.pallas_call(
        body,
        out_shape=[
            jax.ShapeDtypeStruct(shape, kind) if last else pltpu.VMEM(shape, kind)
            for shape, kind in outs
        ],
        in_specs=[pl.BlockSpec(memory_space=space) for space in spaces],
        out_specs=[pl.BlockSpec(memory_space=pltpu.HBM if last else pltpu.VMEM)] * len(outs),
        scratch_shapes=[
            pltpu.SemaphoreType.DMA(shape) if kind is None else pltpu.VMEM(shape, kind)
            for shape, kind in scratch
        ],
        compiler_params=pltpu.CompilerParams(vmem_limit_bytes=grant),
    )(*[pltpu.with_memory_space_constraint(arg, space) for arg, space in zip(args, spaces)])


def block_rows(column, j, size):
    return pl.ds(pl.multiple_of((column ^ j) * size, size), size)


def prepare(mp_count, group, coarse_in, skip_in, counts_in, head_in, weight_in, *refs):
    messages, (pair, cross, own, weight, coarse, skip, top, bottom, done) = refs[: mp_count - 1], refs[mp_count - 1 :]
    width, length = skip.shape
    rows, tracks = top.shape
    place, column = lax.axis_index("seq"), lax.axis_index("mp")
    moves = [
        (coarse_in, coarse),
        (skip_in, skip),
        (counts_in.at[pl.ds(0, rows)], top),
        (counts_in.at[pl.ds(length - rows, rows)], bottom),
        (weight_in, weight),
    ]
    share = width // group
    for j, message in zip(range(1, mp_count), messages):
        for i in range(2):
            start = (column ^ j) * width + ((place >> 1) & (group - 1)) * share + i * (share // 2)
            moves.append(
                (
                    head_in.at[pl.ds(pl.multiple_of(start, 8), share // 2)],
                    message.at[pl.ds(width, share // 2), pl.ds(i * tracks, tracks)],
                )
            )
    copies = [pltpu.make_async_copy(*move, done.at[i]) for i, move in enumerate(moves)]
    for copy in copies:
        copy.start()
    for copy in copies[:4]:
        copy.wait()
    pairs = jnp.where(
        iota((coarse.shape[1], length), 0) == iota((coarse.shape[1], length), 1) // 2, 1.0, 0.0
    ).astype(bf16)
    total = (dot(coarse[...], pairs, nn) + skip[...].astype(f32)).astype(bf16)
    for message in messages:
        message[:width, :] = total
    slot = iota((edge_rows, tracks), 0)
    ahead = dot(chosen((edge_rows, length), ((0, length - 2), (1, length - 1))), total, nt)
    behind = dot(chosen((edge_rows, length), ((4, 0), (5, 1))), total, nt)
    mine = dot(chosen((edge_rows, length), ((2, 0), (3, length - 1))), total, nt)
    first = jnp.where(slot == 7, top[0:1, :].astype(f32), behind[:, :tracks])
    last = jnp.where(slot == 6, bottom[rows - 1 : rows, :].astype(f32), ahead[:, :tracks])
    even = place % 2 == 0
    for out, left, right in (
        (pair, jnp.where(even, last, first), jnp.where(even, ahead, behind)),
        (cross, jnp.where(even, first, last), jnp.where(even, behind, ahead)),
        (own, mine[:, :tracks], mine),
    ):
        out[...] = jnp.zeros(out.shape, bf16)
        out[:, :tracks] = left.astype(bf16)
        out[:, tracks:width] = right[:, tracks:].astype(bf16)
    for copy in copies[4:]:
        copy.wait()


def gelu_parts(inputs):
    inner = root_two_pi * (inputs + cubic_coef * inputs * inputs * inputs)
    tangent = jnp.tanh(inner)
    value = 0.5 * inputs * (1.0 + tangent)
    slope = 0.5 * (1.0 + tangent) + 0.5 * inputs * (1.0 - tangent * tangent) * root_two_pi * (
        1.0 + 3.0 * cubic_coef * inputs * inputs
    )
    return value, slope


def assembled(blocks, whole, column, width):
    channels = whole.shape[0]
    edges = 0.0
    for j, (block, rows) in enumerate(blocks):
        whole[block_rows(column, j, width), :] = block
        wide = jnp.concatenate([rows.astype(f32), jnp.zeros((edge_rows, channels - rows.shape[1]), f32)], axis=1)
        edges = edges + pltpu.roll(wide, (column ^ j) * width, 1)
    return edges.astype(bf16)


def regrouped(out, whole, halves):
    if not halves:
        out[...] = whole[...]
        return
    mine = lax.axis_index("seq") & 1
    chunk = whole.shape[0] // (2 * halves)
    for q in range(halves):
        for i, core in enumerate((mine, 1 - mine)):
            start = pl.multiple_of((2 * q + core) * chunk, 16)
            at = (i * halves + q) * chunk
            out[at : at + chunk, :] = whole[pl.ds(start, chunk), :]


def two_rows(first, second, shape):
    row = iota(shape, 0)
    return jnp.where(row == 0, first, jnp.where(row == 1, second, 0.0))


def convolve(mp_count, halves, *refs):
    pieces, edges = refs[:mp_count], refs[mp_count : 2 * mp_count]
    weight, bias, message, slopes, slopes_beside, full, bundle, whole = refs[2 * mp_count :]
    width = weight.shape[0] // 3
    length = message.shape[1]
    half, tracks = pieces[1].shape[0] - width, bundle.shape[1]
    column = lax.axis_index("mp")
    for j, piece in enumerate(pieces[1:]):
        for i in range(2):
            bundle[(2 * j + i) * half : (2 * j + i + 1) * half, :] = piece[width:, i * tracks : (i + 1) * tracks]
    slots = assembled(
        [(piece[:width, :], edge[...]) for piece, edge in zip(pieces, edges)], whole, column, width
    )
    regrouped(full, whole, halves)
    rows = [weight[k * width : (k + 1) * width, :] for k in range(3)]
    taps = [dot(row, whole[...], nn) for row in rows]
    beside = [dot(slots, row, nt) for row in rows]
    lanes = iota((width, length), 1)
    place = iota((edge_rows, length), 0)
    lane = iota((edge_rows, length), 1)
    spread = (place == 0) | ((place == 1) & (lane == 0)) | ((place == 2) & (lane == length - 1))
    spread = jnp.where(spread, 1.0, 0.0).astype(bf16)
    row = iota((edge_rows, width), 0)
    left = jnp.where(
        row == 0, bias[...], jnp.where(row == 1, beside[0][1:2, :], jnp.where(row == 2, beside[2][4:5, :], 0.0))
    )
    inner = (
        taps[1]
        + jnp.where(lanes == 0, 0.0, pltpu.roll(taps[0], 1, 1))
        + jnp.where(lanes == length - 1, 0.0, pltpu.roll(taps[2], length - 1, 1))
    )
    for _ in range(3):
        term = left.astype(bf16)
        inner = inner + dot(term, spread, tn)
        left = left - term.astype(f32)
    value, slope = gelu_parts(inner)
    own = whole[block_rows(column, 0, width), :].astype(f32)
    message[:width, :] = (own + value).astype(bf16)
    slopes[...] = slope
    shape = (edge_rows, width)
    outer = two_rows(
        *[sum(beside[k][first + k : first + k + 1, :] for k in range(3)) + bias[...] for first in (0, 3)], shape
    )
    near = edges[0][:, :width].astype(f32)
    value, slope = gelu_parts(outer)
    message[width:, :] = jnp.zeros((edge_rows, length), bf16)
    message[width:, :width] = (two_rows(near[1:2, :], near[4:5, :], shape) + value).astype(bf16)
    slopes_beside[...] = slope


def predict(logits):
    return jnp.maximum(logits, 0.0) + jnp.log1p(jnp.exp(-jnp.abs(logits))) + pseudo_count


def score(mp_count, halves, *refs):
    pieces, (head, bias, counts, logits, sums, full, whole) = refs[:mp_count], refs[mp_count:]
    width = head.shape[0] // mp_count
    length, tracks = counts.shape
    blocks = [(piece[:width, :], piece[width:, :]) for piece in pieces]
    slots = assembled(blocks, whole, lax.axis_index("mp"), width)
    regrouped(full, whole, halves)
    scores = dot(whole[...], head[...], tn) + bias[...]
    logits[:length, :] = scores
    logits[length:, :] = dot(slots, head[...], nn) + bias[...]
    pred = jnp.sum(predict(scores), axis=0, keepdims=True)
    seen = jnp.sum(counts[...].astype(f32), axis=0, keepdims=True)
    sums[...] = two_rows(pred, seen, (8, tracks))


def differentiate(logits, counts, edges, totals, mask, slope):
    length, tracks = counts.shape
    pred_total, count_total = totals[0:1, :], totals[1:2, :]
    ratio = (multi_weight - 1.0) * count_total / pred_total

    def slope_of(scores, observed):
        inner = 1.0 + ratio - multi_weight * observed / predict(scores)
        return (mask[...] * inner * jax.nn.sigmoid(scores)).astype(bf16)

    slope[:length, :] = slope_of(logits[:length, :], counts[...].astype(f32))
    row = iota((edge_rows, tracks), 0)
    beside = edges[...].astype(f32)
    beside = jnp.where(row == 0, beside[6:7, :tracks], jnp.where(row == 1, beside[7:8, :tracks], 0.0))
    slope[length:, :] = slope_of(logits[length:, :], beside)


def packed(out, base, value, start, chunk):
    tiles, half = value.shape[1] // 128, chunk // 2
    for t in range(tiles):
        rows = value[start : start + chunk, t * 128 : (t + 1) * 128]
        out[base + t * chunk : base + (t + 1) * chunk, :] = rows.astype(out.dtype)
    if value.shape[1] % 128:
        pair = [value[start + i * half : start + (i + 1) * half, tiles * 128 :] for i in range(2)]
        at = base + tiles * chunk
        out[at : at + half, :] = jnp.concatenate(pair, axis=1).astype(out.dtype)


def packed_rows(chunk, both):
    return chunk * both // 128


def backward(mp_count, seq_count, split, group, *refs):
    slopes, head_own, bundles = refs[:mp_count], refs[mp_count], refs[mp_count + 1 : mp_count + 1 + group]
    gelu, gelu_beside, full, hidden, weight, *outs = refs[mp_count + 1 + group :]
    head_rows, slope_rows = outs[-3], outs[-4]
    own, *outs = outs
    carry, outs = outs[: mp_count - 1], outs[mp_count - 1 :]
    width, length = head_own.shape[0], full.shape[1]
    tracks = head_own.shape[1]
    place, column = lax.axis_index("seq"), lax.axis_index("mp")
    part = width // group
    for r, bundle in enumerate(bundles):
        at = pl.multiple_of((((place >> 1) & (group - 1)) ^ r) * part, 16)
        for j in range(mp_count - 1):
            head_rows[pl.ds(at, part), (j + 1) * tracks : (j + 2) * tracks] = bundle[j * part : (j + 1) * part, :]
    head_rows[:, :tracks] = head_own[...]
    for j, slope in enumerate(slopes):
        slope_rows[:, j * tracks : (j + 1) * tracks] = slope[...]
    inner = dot(head_rows[...], slope_rows[:length, :], nt)
    outer = dot(slope_rows[length:, :], head_rows[...], nt)
    middle = (inner * gelu[...]).astype(bf16).astype(f32)
    row = iota(outer.shape, 0)
    absent = ((row == 0) & (place == 0)) | ((row == 1) & (place == seq_count - 1))
    outer = jnp.where(absent, 0.0, outer * gelu_beside[...]).astype(bf16)
    ends = dot(outer, chosen((edge_rows, length), ((0, 0), (1, length - 1))), tn)
    lanes = iota((width, length), 1)
    stacked = outs[-1]
    stacked[:width, :] = jnp.where(lanes == length - 1, ends, pltpu.roll(middle, length - 1, 1)).astype(bf16)
    stacked[width : 2 * width, :] = middle.astype(bf16)
    stacked[2 * width :, :] = jnp.where(lanes == 0, ends, pltpu.roll(middle, 1, 1)).astype(bf16)
    total = outs[-2]
    total[...] = dot(weight[...], stacked[...], tn)
    own[...] = inner + total[block_rows(column, 0, width), :]
    for j, out in zip(range(1, mp_count), carry):
        out[...] = total[block_rows(column, j, width), :].astype(bf16)
    own_slope = slopes[0][:length, :]
    if split:
        rows = full.shape[0] // 2
        chunk = full.shape[0] // seq_count
        for i, out in ((1, outs[1]), (0, outs[0])):
            at = slice(i * rows, (i + 1) * rows)
            value = jnp.concatenate(
                [dot(hidden[at, :], own_slope, nn), dot(full[at, :], stacked[...], nt)], axis=1
            )
            for q in range(seq_count // 2):
                packed(out, q * packed_rows(chunk, value.shape[1]), value, q * chunk, chunk)
    else:
        grads = outs[0]
        grads[:, :tracks] = dot(hidden[...], own_slope, nn)
        grads[:, tracks:] = dot(full[...], stacked[...], nt)


def quartered(count, kept, got, own, *outs):
    rows = own.shape[0]
    at = lax.axis_index("seq") >> 1
    total = outs[-1]
    total[...] = kept[...] + got[...].astype(f32)
    own[...] = total[pl.ds(pl.multiple_of(at * rows, 8), rows), :]
    for j, out in zip(range(1, count), outs):
        out[...] = total[pl.ds(pl.multiple_of((at ^ j) * rows, 8), rows), :].astype(bf16)


def unpacked(whole, total):
    chunk, both = whole.shape
    if total.shape == whole.shape:
        whole[...] = total
        return
    tiles, half = both // 128, chunk // 2
    for t in range(tiles):
        whole[:, t * 128 : (t + 1) * 128] = total[t * chunk : (t + 1) * chunk, :]
    for i in range(2 if both % 128 else 0):
        at = tiles * chunk
        whole[i * half : (i + 1) * half, tiles * 128 :] = total[at : at + half, i * 64 : (i + 1) * 64]


def finish(mp_count, scale, *refs):
    carried, rest = refs[:mp_count], refs[mp_count:]
    *summands, grad_skip, grad_coarse, grad_head, grad_conv, skip, coarse, whole, conv, done = rest
    total = summands[0][...]
    for part in summands[1:]:
        total = total + part[...].astype(f32)
    unpacked(whole, total * scale)
    tracks, wide = grad_head.shape[1], grad_conv.shape[2]
    copies = [pltpu.make_async_copy(whole.at[:, pl.ds(0, tracks)], grad_head, done.at[0])]
    copies[0].start()
    for k in range(grad_conv.shape[0]):
        conv[k] = whole[:, tracks + k * wide : tracks + (k + 1) * wide]
    copies.append(pltpu.make_async_copy(conv, grad_conv, done.at[1]))
    copies[1].start()
    total = carried[0][...]
    for part in carried[1:]:
        total = total + part[...].astype(f32)
    skip[...] = total.astype(bf16)
    copies.append(pltpu.make_async_copy(skip, grad_skip, done.at[2]))
    copies[2].start()
    length, half = grad_skip.shape[1], grad_coarse.shape[1]
    pairs = jnp.where(iota((length, half), 0) // 2 == iota((length, half), 1), 1.0, 0.0).astype(bf16)
    terms, left = [], total
    for _ in range(3):
        terms.append(left.astype(bf16))
        left = left - terms[-1].astype(f32)
    coarse[...] = sum(dot(term, pairs, nn) for term in terms).astype(bf16)
    copies.append(pltpu.make_async_copy(coarse, grad_coarse, done.at[3]))
    copies[3].start()
    for copy in copies:
        copy.wait()


def shards(coarse, skip, conv_weight, conv_bias, head_weight, head_bias, counts, seg_mask):
    width, length = skip.shape
    taps = conv_weight.shape[0]
    seq_count, mp_count = lax.axis_size("seq"), lax.axis_size("mp")
    channels, tracks = head_weight.shape
    scale_back = 1.0 / math.sqrt(length * seq_count)
    place, column = lax.axis_index("seq"), lax.axis_index("mp")
    group = min(4, seq_count // 2)
    share = width // group
    chunk = channels // seq_count
    both = tracks + taps * width
    split = chunk % 32 == 0 and both % 64 == 0 and len(list(staged(0, seq_count.bit_length() - 1))) == 2
    halves = seq_count // 2 if split else 0
    tall = width + edge_rows
    tile = ((edge_rows, length), bf16)
    *messages, pair, cross, own, weight = call(
        functools.partial(prepare, mp_count, group),
        [((width + share // 2, length), bf16)] * (mp_count - 1) + [tile, tile, tile, ((taps * width, channels), bf16)],
        coarse, skip, counts, head_weight, conv_weight.reshape(taps * width, channels),
        scratch=[
            (coarse.shape, bf16), (skip.shape, bf16), ((8, tracks), jnp.int32), ((8, tracks), jnp.int32),
            ((5 + 2 * (mp_count - 1),), None),
        ],
        outside=range(5),
    )
    pieces = [messages[0]]
    for j, message in zip(range(1, mp_count), messages):
        pieces.append(swap(message, "mp", j))
    cross = crossed(cross, "seq")
    pair = swap(pair, "seq", 1)
    edges = cross + pair + own
    message, gelu, gelu_beside, full_in, bundle = call(
        functools.partial(convolve, mp_count, halves),
        [((tall, length), bf16), ((width, length), f32), ((edge_rows, width), f32), ((channels, length), bf16)]
        + [(((mp_count - 1) * share, tracks), bf16)],
        *pieces, *gathered(edges, "mp"), weight, conv_bias[None, :],
        scratch=[((channels, length), bf16)],
    )
    pieces = gathered(message, "mp")
    bundles = [bundle]
    for r in range(1, group):
        bundles.append(swap(bundle, "seq", 2 * r))
    head_own = lax.dynamic_index_in_dim(head_weight.reshape(mp_count, width, tracks), column, 0, keepdims=False)
    logits, sums, full = call(
        functools.partial(score, mp_count, halves),
        [((length + edge_rows, tracks), f32), ((8, tracks), f32), ((channels, length), bf16)],
        *pieces, head_weight, head_bias[None, :], counts,
        scratch=[((channels, length), bf16)],
    )
    span = seq_count // seg_mask.shape[0]
    totals = totalled(sums, "seq", span)
    mask_row = lax.dynamic_slice_in_dim(seg_mask, place // span, 1, 0).astype(f32)
    (slope,) = call(
        differentiate, [((length + edge_rows, tracks), bf16)], logits, counts, edges, totals, mask_row
    )
    slopes = gathered(slope, "mp")
    quarter = (packed_rows(chunk, both), 128)
    half = (seq_count // 2 * quarter[0], 128)
    grads_at = ((channels, both), f32)
    scratch = [((channels, length), f32), ((taps * width, length), bf16)]
    head_at = [((length + edge_rows, mp_count * tracks), bf16), ((width, mp_count * tracks), bf16)]
    own, *outs = call(
        functools.partial(backward, mp_count, seq_count, split, group),
        [((width, length), f32)]
        + [((width, length), bf16)] * (mp_count - 1)
        + ([(half, f32), (half, bf16)] if split else [grads_at]),
        *slopes, head_own, *bundles, gelu, gelu_beside, full_in, full, weight,
        scratch=head_at + scratch,
    )
    carry, grads = outs[: mp_count - 1], outs[mp_count - 1 :]
    if split:
        got = swap(grads[1], "seq", 1)
    parts = []
    for j in range(mp_count - 1, 0, -1):
        parts.append(swap(carry[j - 1], "mp", j))
    if split:
        count = seq_count // 2
        grad_own, *sends = call(
            functools.partial(quartered, count),
            [(quarter, f32)] + [(quarter, bf16)] * (count - 1),
            grads[0], got,
            scratch=[(half, f32)],
        )
        gots = []
        for j in range(count - 1, 0, -1):
            gots.append(swap(sends[j - 1], "seq", 2 * j))
    else:
        grad_own, gots = scattered(grads[0].reshape(seq_count, chunk, both), "seq"), []
    outs = [((width, length), bf16), ((width, length // 2), bf16), ((chunk, tracks), f32), ((taps, chunk, width), f32)]
    grad_skip, grad_coarse, grad_head, grad_conv = call(
        functools.partial(finish, mp_count, scale_back),
        outs,
        own, *parts, grad_own, *gots,
        scratch=outs[:2] + [((chunk, both), f32), outs[3], ((len(outs),), None)],
        last=True,
    )
    return (grad_skip, grad_coarse, grad_head, grad_conv.transpose(1, 0, 2))


def solution(mesh):
    in_specs = (
        P("mp", "seq"),
        P("mp", "seq"),
        P(None, "mp", None),
        P("mp"),
        P(None, "mp"),
        P("mp"),
        P("seq", "mp"),
        P(None, "mp"),
    )
    out_specs = (P("mp", "seq"), P("mp", "seq"), P("seq", "mp"), P("seq", None, "mp"))

    return jax.shard_map(shards, mesh=mesh, in_specs=in_specs, out_specs=out_specs, check_vma=False)
```

```python
import functools
import math

import jax
import jax.numpy as jnp
from jax import lax
from jax.experimental import pallas as pl
from jax.experimental.pallas import tpu as pltpu
from jax.sharding import PartitionSpec as P


root_two_pi = 0.7978845608028654
cubic_coef = 0.044715
multi_weight = 5.0
pseudo_count = 0.5
edge_rows = 8
bf16, f32 = jnp.bfloat16, jnp.float32


def swap(block, axis, mask):
    count = lax.axis_size(axis)
    return lax.ppermute(block, axis, [(i, i ^ mask) for i in range(count)])


def crossed(block, axis):
    count = lax.axis_size(axis)
    pairs = [(i, i + 1) for i in range(1, count - 1, 2)]
    return lax.ppermute(block, axis, pairs + [(b, a) for a, b in pairs])


def gathered(block, axis):
    parts = [block]
    for j in range(1, lax.axis_size(axis)):
        parts.append(swap(block, axis, j))
    return parts


def staged(low, bits):
    while low < bits:
        wide = 1 if low == 0 else min(2, bits - low)
        yield low, wide
        low += wide


def scattered(parts, axis):
    bits = lax.axis_size(axis).bit_length() - 1
    mine = lax.axis_index(axis)
    for low, wide in staged(0, bits):
        size = 1 << wide
        parts = parts.reshape((parts.shape[0] // size, size) + parts.shape[1:])
        at = (mine >> low) & (size - 1)
        small = parts.astype(bf16)
        kept = lax.dynamic_index_in_dim(parts, at, 1, keepdims=False)
        for step in range(1, size):
            piece = lax.dynamic_index_in_dim(small, at ^ step, 1, keepdims=False)
            kept = kept + swap(piece, axis, step << low).astype(f32)
        parts = kept
    return parts[0]


def totalled(block, axis, span):
    for low, wide in staged(0, span.bit_length() - 1):
        parts = []
        for step in range(1, 1 << wide):
            parts.append(swap(block, axis, step << low))
        block = sum(parts, block)
    return block


def dot(left, right, dims, precision=None):
    return lax.dot_general(
        left, right, (dims, ((), ())), preferred_element_type=f32, precision=precision
    )


nn, nt, tn = ((1,), (0,)), ((1,), (1,)), ((0,), (0,))


def iota(shape, axis):
    return lax.broadcasted_iota(jnp.int32, shape, axis)


def chosen(shape, pairs):
    rows, columns = iota(shape, 0), iota(shape, 1)
    hit = functools.reduce(jnp.logical_or, [(rows == r) & (columns == c) for r, c in pairs])
    return jnp.where(hit, 1.0, 0.0).astype(bf16)


def call(body, outs, *args, scratch=(), grant=16 << 20, outside=(), last=False, aliases={}):
    spaces = [pltpu.HBM if i in outside else pltpu.VMEM for i in range(len(args))]
    return pl.pallas_call(
        body,
        out_shape=[
            jax.ShapeDtypeStruct(shape, kind) if last else pltpu.VMEM(shape, kind)
            for shape, kind in outs
        ],
        in_specs=[pl.BlockSpec(memory_space=space) for space in spaces],
        out_specs=[pl.BlockSpec(memory_space=pltpu.HBM if last else pltpu.VMEM)] * len(outs),
        scratch_shapes=[
            pltpu.SemaphoreType.DMA(shape) if kind is None else pltpu.VMEM(shape, kind)
            for shape, kind in scratch
        ],
        input_output_aliases=aliases,
        compiler_params=pltpu.CompilerParams(vmem_limit_bytes=grant),
    )(*[pltpu.with_memory_space_constraint(arg, space) for arg, space in zip(args, spaces)])


def block_rows(column, j, size):
    return pl.ds(pl.multiple_of((column ^ j) * size, size), size)


def prepare(mp_count, group, coarse_in, skip_in, counts_in, head_in, weight_in, *refs):
    messages, (pair, cross, own, weight, coarse, skip, top, bottom, done) = refs[: mp_count - 1], refs[mp_count - 1 :]
    width, length = skip.shape
    rows, tracks = top.shape
    place, column = lax.axis_index("seq"), lax.axis_index("mp")
    moves = [
        (coarse_in, coarse),
        (skip_in, skip),
        (counts_in.at[pl.ds(0, rows)], top),
        (counts_in.at[pl.ds(length - rows, rows)], bottom),
        (weight_in, weight),
    ]
    share = width // group
    for j, message in zip(range(1, mp_count), messages):
        for i in range(2):
            start = (column ^ j) * width + ((place >> 1) & (group - 1)) * share + i * (share // 2)
            moves.append(
                (
                    head_in.at[pl.ds(pl.multiple_of(start, 8), share // 2)],
                    message.at[pl.ds(width, share // 2), pl.ds(i * tracks, tracks)],
                )
            )
    copies = [pltpu.make_async_copy(*move, done.at[i]) for i, move in enumerate(moves)]
    for copy in copies:
        copy.start()
    for copy in copies[:4]:
        copy.wait()
    pairs = jnp.where(
        iota((coarse.shape[1], length), 0) == iota((coarse.shape[1], length), 1) // 2, 1.0, 0.0
    ).astype(bf16)
    total = (dot(coarse[...], pairs, nn) + skip[...].astype(f32)).astype(bf16)
    for message in messages:
        message[:width, :] = total
    slot = iota((edge_rows, tracks), 0)
    ahead = dot(chosen((edge_rows, length), ((0, length - 2), (1, length - 1))), total, nt)
    behind = dot(chosen((edge_rows, length), ((4, 0), (5, 1))), total, nt)
    mine = dot(chosen((edge_rows, length), ((2, 0), (3, length - 1))), total, nt)
    first = jnp.where(slot == 7, top[0:1, :].astype(f32), behind[:, :tracks])
    last = jnp.where(slot == 6, bottom[rows - 1 : rows, :].astype(f32), ahead[:, :tracks])
    even = place % 2 == 0
    for out, left, right in (
        (pair, jnp.where(even, last, first), jnp.where(even, ahead, behind)),
        (cross, jnp.where(even, first, last), jnp.where(even, behind, ahead)),
        (own, mine[:, :tracks], mine),
    ):
        out[...] = jnp.zeros(out.shape, bf16)
        out[:, :tracks] = left.astype(bf16)
        out[:, tracks:width] = right[:, tracks:].astype(bf16)
    for copy in copies[4:]:
        copy.wait()


def attach(cross, pair, own, message_in, edges, message):
    total = cross[...] + pair[...] + own[...]
    edges[...] = total
    message[message.shape[0] - edge_rows :, :] = total


def gelu_parts(inputs):
    inner = root_two_pi * (inputs + cubic_coef * inputs * inputs * inputs)
    tangent = jnp.tanh(inner)
    value = 0.5 * inputs * (1.0 + tangent)
    slope = 0.5 * (1.0 + tangent) + 0.5 * inputs * (1.0 - tangent * tangent) * root_two_pi * (
        1.0 + 3.0 * cubic_coef * inputs * inputs
    )
    return value, slope


def assembled(blocks, whole, column, width):
    channels = whole.shape[0]
    edges = 0.0
    for j, (block, rows) in enumerate(blocks):
        whole[block_rows(column, j, width), :] = block
        wide = jnp.concatenate([rows.astype(f32), jnp.zeros((edge_rows, channels - rows.shape[1]), f32)], axis=1)
        edges = edges + pltpu.roll(wide, (column ^ j) * width, 1)
    return edges.astype(bf16)


def regrouped(out, whole, halves):
    if not halves:
        out[...] = whole[...]
        return
    mine = lax.axis_index("seq") & 1
    chunk = whole.shape[0] // (2 * halves)
    for q in range(halves):
        for i, core in enumerate((mine, 1 - mine)):
            start = pl.multiple_of((2 * q + core) * chunk, 16)
            at = (i * halves + q) * chunk
            out[at : at + chunk, :] = whole[pl.ds(start, chunk), :]


def two_rows(first, second, shape):
    row = iota(shape, 0)
    return jnp.where(row == 0, first, jnp.where(row == 1, second, 0.0))


def convolve(mp_count, halves, *refs):
    pieces, (near, *far) = refs[:mp_count], refs[mp_count : 2 * mp_count - 1]
    weight, bias, message, slopes, slopes_beside, full, bundle, whole = refs[2 * mp_count - 1 :]
    width = weight.shape[0] // 3
    length = message.shape[1]
    half, tracks = pieces[1].shape[0] - edge_rows - width, bundle.shape[1]
    edges = [near[...], pieces[1][width + half :, :]] + [rows[...] for rows in far]
    column = lax.axis_index("mp")
    for j, piece in enumerate(pieces[1:]):
        for i in range(2):
            bundle[(2 * j + i) * half : (2 * j + i + 1) * half, :] = piece[width : width + half, i * tracks : (i + 1) * tracks]
    slots = assembled(
        [(piece[:width, :], edge) for piece, edge in zip(pieces, edges)], whole, column, width
    )
    regrouped(full, whole, halves)
    rows = [weight[k * width : (k + 1) * width, :] for k in range(3)]
    taps = [dot(row, whole[...], nn) for row in rows]
    beside = [dot(slots, row, nt) for row in rows]
    lanes = iota((width, length), 1)
    place = iota((edge_rows, length), 0)
    lane = iota((edge_rows, length), 1)
    spread = (place == 0) | ((place == 1) & (lane == 0)) | ((place == 2) & (lane == length - 1))
    spread = jnp.where(spread, 1.0, 0.0).astype(bf16)
    row = iota((edge_rows, width), 0)
    left = jnp.where(
        row == 0, bias[...], jnp.where(row == 1, beside[0][1:2, :], jnp.where(row == 2, beside[2][4:5, :], 0.0))
    )
    inner = (
        taps[1]
        + jnp.where(lanes == 0, 0.0, pltpu.roll(taps[0], 1, 1))
        + jnp.where(lanes == length - 1, 0.0, pltpu.roll(taps[2], length - 1, 1))
    )
    for _ in range(3):
        term = left.astype(bf16)
        inner = inner + dot(term, spread, tn)
        left = left - term.astype(f32)
    value, slope = gelu_parts(inner)
    own = whole[block_rows(column, 0, width), :].astype(f32)
    message[:width, :] = (own + value).astype(bf16)
    slopes[...] = slope
    shape = (edge_rows, width)
    outer = two_rows(
        *[sum(beside[k][first + k : first + k + 1, :] for k in range(3)) + bias[...] for first in (0, 3)], shape
    )
    near = near[:, :width].astype(f32)
    value, slope = gelu_parts(outer)
    message[width:, :] = jnp.zeros((edge_rows, length), bf16)
    message[width:, :width] = (two_rows(near[1:2, :], near[4:5, :], shape) + value).astype(bf16)
    slopes_beside[...] = slope


def predict(logits):
    return jnp.maximum(logits, 0.0) + jnp.log1p(jnp.exp(-jnp.abs(logits))) + pseudo_count


def score(mp_count, halves, *refs):
    pieces, (head, bias, counts, logits, sums, full, whole) = refs[:mp_count], refs[mp_count:]
    width = head.shape[0] // mp_count
    length, tracks = counts.shape
    blocks = [(piece[:width, :], piece[width:, :]) for piece in pieces]
    slots = assembled(blocks, whole, lax.axis_index("mp"), width)
    regrouped(full, whole, halves)
    scores = dot(whole[...], head[...], tn) + bias[...]
    logits[:length, :] = scores
    logits[length:, :] = dot(slots, head[...], nn) + bias[...]
    pred = jnp.sum(predict(scores), axis=0, keepdims=True)
    seen = jnp.sum(counts[...].astype(f32), axis=0, keepdims=True)
    sums[...] = two_rows(pred, seen, (8, tracks))


def differentiate(logits, counts, edges, totals, mask, slope):
    length, tracks = counts.shape
    pred_total, count_total = totals[0:1, :], totals[1:2, :]
    ratio = (multi_weight - 1.0) * count_total / pred_total

    def slope_of(scores, observed):
        inner = 1.0 + ratio - multi_weight * observed / predict(scores)
        return (mask[...] * inner * jax.nn.sigmoid(scores)).astype(bf16)

    slope[:length, :] = slope_of(logits[:length, :], counts[...].astype(f32))
    row = iota((edge_rows, tracks), 0)
    beside = edges[...].astype(f32)
    beside = jnp.where(row == 0, beside[6:7, :tracks], jnp.where(row == 1, beside[7:8, :tracks], 0.0))
    slope[length:, :] = slope_of(logits[length:, :], beside)


def packed(out, base, value, start, chunk):
    tiles, half = value.shape[1] // 128, chunk // 2
    for t in range(tiles):
        rows = value[start : start + chunk, t * 128 : (t + 1) * 128]
        out[base + t * chunk : base + (t + 1) * chunk, :] = rows.astype(out.dtype)
    if value.shape[1] % 128:
        pair = [value[start + i * half : start + (i + 1) * half, tiles * 128 :] for i in range(2)]
        at = base + tiles * chunk
        out[at : at + half, :] = jnp.concatenate(pair, axis=1).astype(out.dtype)


def packed_rows(chunk, both):
    return chunk * both // 128


def backward(mp_count, seq_count, split, group, *refs):
    slopes, head_own, bundles = refs[:mp_count], refs[mp_count], refs[mp_count + 1 : mp_count + 1 + group]
    gelu, gelu_beside, full, hidden, weight, *outs = refs[mp_count + 1 + group :]
    head_rows, slope_rows = outs[-3], outs[-4]
    own, *outs = outs
    carry, outs = outs[: mp_count - 1], outs[mp_count - 1 :]
    width, length = head_own.shape[0], full.shape[1]
    tracks = head_own.shape[1]
    place, column = lax.axis_index("seq"), lax.axis_index("mp")
    part = width // group
    for r, bundle in enumerate(bundles):
        at = pl.multiple_of((((place >> 1) & (group - 1)) ^ r) * part, 16)
        for j in range(mp_count - 1):
            head_rows[pl.ds(at, part), (j + 1) * tracks : (j + 2) * tracks] = bundle[j * part : (j + 1) * part, :]
    head_rows[:, :tracks] = head_own[...]
    for j, slope in enumerate(slopes):
        slope_rows[:, j * tracks : (j + 1) * tracks] = slope[...]
    inner = dot(head_rows[...], slope_rows[:length, :], nt)
    outer = dot(slope_rows[length:, :], head_rows[...], nt)
    middle = (inner * gelu[...]).astype(bf16).astype(f32)
    row = iota(outer.shape, 0)
    absent = ((row == 0) & (place == 0)) | ((row == 1) & (place == seq_count - 1))
    outer = jnp.where(absent, 0.0, outer * gelu_beside[...]).astype(bf16)
    ends = dot(outer, chosen((edge_rows, length), ((0, 0), (1, length - 1))), tn)
    lanes = iota((width, length), 1)
    stacked = outs[-1]
    stacked[:width, :] = jnp.where(lanes == length - 1, ends, pltpu.roll(middle, length - 1, 1)).astype(bf16)
    stacked[width : 2 * width, :] = middle.astype(bf16)
    stacked[2 * width :, :] = jnp.where(lanes == 0, ends, pltpu.roll(middle, 1, 1)).astype(bf16)
    total = outs[-2]
    total[...] = dot(weight[...], stacked[...], tn)
    own[...] = inner + total[block_rows(column, 0, width), :]
    for j, out in zip(range(1, mp_count), carry):
        out[...] = total[block_rows(column, j, width), :].astype(bf16)
    own_slope = slopes[0][:length, :]
    if split:
        rows = full.shape[0] // 2
        chunk = full.shape[0] // seq_count
        for i, out in ((1, outs[1]), (0, outs[0])):
            at = slice(i * rows, (i + 1) * rows)
            value = jnp.concatenate(
                [dot(hidden[at, :], own_slope, nn), dot(full[at, :], stacked[...], nt)], axis=1
            )
            for q in range(seq_count // 2):
                packed(out, q * packed_rows(chunk, value.shape[1]), value, q * chunk, chunk)
    else:
        grads = outs[0]
        grads[:, :tracks] = dot(hidden[...], own_slope, nn)
        grads[:, tracks:] = dot(full[...], stacked[...], nt)


def quartered(count, kept, got, own, *outs):
    rows = own.shape[0]
    at = lax.axis_index("seq") >> 1
    total = outs[-1]
    total[...] = kept[...] + got[...].astype(f32)
    own[...] = total[pl.ds(pl.multiple_of(at * rows, 8), rows), :]
    for j, out in zip(range(1, count), outs):
        out[...] = total[pl.ds(pl.multiple_of((at ^ j) * rows, 8), rows), :].astype(bf16)


def unpacked(whole, total):
    chunk, both = whole.shape
    if total.shape == whole.shape:
        whole[...] = total
        return
    tiles, half = both // 128, chunk // 2
    for t in range(tiles):
        whole[:, t * 128 : (t + 1) * 128] = total[t * chunk : (t + 1) * chunk, :]
    for i in range(2 if both % 128 else 0):
        at = tiles * chunk
        whole[i * half : (i + 1) * half, tiles * 128 :] = total[at : at + half, i * 64 : (i + 1) * 64]


def finish(mp_count, scale, *refs):
    carried, rest = refs[:mp_count], refs[mp_count:]
    *summands, grad_skip, grad_coarse, grad_head, grad_conv, skip, coarse, whole, conv, done = rest
    total = summands[0][...]
    for part in summands[1:]:
        total = total + part[...].astype(f32)
    unpacked(whole, total * scale)
    tracks, wide = grad_head.shape[1], grad_conv.shape[2]
    copies = [pltpu.make_async_copy(whole.at[:, pl.ds(0, tracks)], grad_head, done.at[0])]
    copies[0].start()
    for k in range(grad_conv.shape[0]):
        conv[k] = whole[:, tracks + k * wide : tracks + (k + 1) * wide]
    copies.append(pltpu.make_async_copy(conv, grad_conv, done.at[1]))
    copies[1].start()
    total = carried[0][...]
    for part in carried[1:]:
        total = total + part[...].astype(f32)
    skip[...] = total.astype(bf16)
    copies.append(pltpu.make_async_copy(skip, grad_skip, done.at[2]))
    copies[2].start()
    length, half = grad_skip.shape[1], grad_coarse.shape[1]
    pairs = jnp.where(iota((length, half), 0) // 2 == iota((length, half), 1), 1.0, 0.0).astype(bf16)
    terms, left = [], total
    for _ in range(3):
        terms.append(left.astype(bf16))
        left = left - terms[-1].astype(f32)
    coarse[...] = sum(dot(term, pairs, nn) for term in terms).astype(bf16)
    copies.append(pltpu.make_async_copy(coarse, grad_coarse, done.at[3]))
    copies[3].start()
    for copy in copies:
        copy.wait()


def shards(coarse, skip, conv_weight, conv_bias, head_weight, head_bias, counts, seg_mask):
    width, length = skip.shape
    taps = conv_weight.shape[0]
    seq_count, mp_count = lax.axis_size("seq"), lax.axis_size("mp")
    channels, tracks = head_weight.shape
    scale_back = 1.0 / math.sqrt(length * seq_count)
    place, column = lax.axis_index("seq"), lax.axis_index("mp")
    group = min(4, seq_count // 2)
    share = width // group
    chunk = channels // seq_count
    both = tracks + taps * width
    split = chunk % 32 == 0 and both % 64 == 0 and len(list(staged(0, seq_count.bit_length() - 1))) == 2
    halves = seq_count // 2 if split else 0
    tall = width + edge_rows
    tile = ((edge_rows, length), bf16)
    block = ((width + share // 2, length), bf16)
    nearest = ((width + share // 2 + edge_rows, length), bf16)
    *messages, pair, cross, own, weight = call(
        functools.partial(prepare, mp_count, group),
        [nearest] + [block] * (mp_count - 2) + [tile, tile, tile, ((taps * width, channels), bf16)],
        coarse, skip, counts, head_weight, conv_weight.reshape(taps * width, channels),
        scratch=[
            (coarse.shape, bf16), (skip.shape, bf16), ((8, tracks), jnp.int32), ((8, tracks), jnp.int32),
            ((5 + 2 * (mp_count - 1),), None),
        ],
        outside=range(5),
    )
    cross = crossed(cross, "seq")
    pair = swap(pair, "seq", 1)
    edges, messages[0] = call(attach, [tile, nearest], cross, pair, own, messages[0], aliases={3: 1})
    pieces = [messages[-1]]
    for j, message in zip(range(1, mp_count), messages):
        pieces.append(swap(message, "mp", j))
    halos = [edges]
    for j in range(2, mp_count):
        halos.append(swap(edges, "mp", j))
    message, gelu, gelu_beside, full_in, bundle = call(
        functools.partial(convolve, mp_count, halves),
        [((tall, length), bf16), ((width, length), f32), ((edge_rows, width), f32), ((channels, length), bf16)]
        + [(((mp_count - 1) * share, tracks), bf16)],
        *pieces, *halos, weight, conv_bias[None, :],
        scratch=[((channels, length), bf16)],
    )
    pieces = gathered(message, "mp")
    bundles = [bundle]
    for r in range(1, group):
        bundles.append(swap(bundle, "seq", 2 * r))
    head_own = lax.dynamic_index_in_dim(head_weight.reshape(mp_count, width, tracks), column, 0, keepdims=False)
    logits, sums, full = call(
        functools.partial(score, mp_count, halves),
        [((length + edge_rows, tracks), f32), ((8, tracks), f32), ((channels, length), bf16)],
        *pieces, head_weight, head_bias[None, :], counts,
        scratch=[((channels, length), bf16)],
    )
    span = seq_count // seg_mask.shape[0]
    totals = totalled(sums, "seq", span)
    mask_row = lax.dynamic_slice_in_dim(seg_mask, place // span, 1, 0).astype(f32)
    (slope,) = call(
        differentiate, [((length + edge_rows, tracks), bf16)], logits, counts, edges, totals, mask_row
    )
    slopes = gathered(slope, "mp")
    quarter = (packed_rows(chunk, both), 128)
    half = (seq_count // 2 * quarter[0], 128)
    grads_at = ((channels, both), f32)
    scratch = [((channels, length), f32), ((taps * width, length), bf16)]
    head_at = [((length + edge_rows, mp_count * tracks), bf16), ((width, mp_count * tracks), bf16)]
    own, *outs = call(
        functools.partial(backward, mp_count, seq_count, split, group),
        [((width, length), f32)]
        + [((width, length), bf16)] * (mp_count - 1)
        + ([(half, f32), (half, bf16)] if split else [grads_at]),
        *slopes, head_own, *bundles, gelu, gelu_beside, full_in, full, weight,
        scratch=head_at + scratch,
    )
    carry, grads = outs[: mp_count - 1], outs[mp_count - 1 :]
    if split:
        got = swap(grads[1], "seq", 1)
    parts = []
    for j in range(mp_count - 1, 0, -1):
        parts.append(swap(carry[j - 1], "mp", j))
    if split:
        count = seq_count // 2
        grad_own, *sends = call(
            functools.partial(quartered, count),
            [(quarter, f32)] + [(quarter, bf16)] * (count - 1),
            grads[0], got,
            scratch=[(half, f32)],
        )
        gots = []
        for j in range(count - 1, 0, -1):
            gots.append(swap(sends[j - 1], "seq", 2 * j))
    else:
        grad_own, gots = scattered(grads[0].reshape(seq_count, chunk, both), "seq"), []
    outs = [((width, length), bf16), ((width, length // 2), bf16), ((chunk, tracks), f32), ((taps, chunk, width), f32)]
    grad_skip, grad_coarse, grad_head, grad_conv = call(
        functools.partial(finish, mp_count, scale_back),
        outs,
        own, *parts, grad_own, *gots,
        scratch=outs[:2] + [((chunk, both), f32), outs[3], ((len(outs),), None)],
        last=True,
    )
    return (grad_skip, grad_coarse, grad_head, grad_conv.transpose(1, 0, 2))


def solution(mesh):
    in_specs = (
        P("mp", "seq"),
        P("mp", "seq"),
        P(None, "mp", None),
        P("mp"),
        P(None, "mp"),
        P("mp"),
        P("seq", "mp"),
        P(None, "mp"),
    )
    out_specs = (P("mp", "seq"), P("mp", "seq"), P("seq", "mp"), P("seq", None, "mp"))

    return jax.shard_map(shards, mesh=mesh, in_specs=in_specs, out_specs=out_specs, check_vma=False)
```

```python
import functools
import math

import jax
import jax.numpy as jnp
from jax import lax
from jax.experimental import pallas as pl
from jax.experimental.pallas import tpu as pltpu
from jax.sharding import PartitionSpec as P


root_two_pi = 0.7978845608028654
cubic_coef = 0.044715
multi_weight = 5.0
pseudo_count = 0.5
edge_rows = 8
bf16, f32 = jnp.bfloat16, jnp.float32


def swap(block, axis, mask):
    count = lax.axis_size(axis)
    return lax.ppermute(block, axis, [(i, i ^ mask) for i in range(count)])


def crossed(block, axis):
    count = lax.axis_size(axis)
    pairs = [(i, i + 1) for i in range(1, count - 1, 2)]
    return lax.ppermute(block, axis, pairs + [(b, a) for a, b in pairs])


def gathered(block, axis):
    parts = [block]
    for j in range(1, lax.axis_size(axis)):
        parts.append(swap(block, axis, j))
    return parts


def staged(low, bits):
    while low < bits:
        wide = 1 if low == 0 else min(2, bits - low)
        yield low, wide
        low += wide


def scattered(parts, axis):
    bits = lax.axis_size(axis).bit_length() - 1
    mine = lax.axis_index(axis)
    for low, wide in staged(0, bits):
        size = 1 << wide
        parts = parts.reshape((parts.shape[0] // size, size) + parts.shape[1:])
        at = (mine >> low) & (size - 1)
        small = parts.astype(bf16)
        kept = lax.dynamic_index_in_dim(parts, at, 1, keepdims=False)
        for step in range(1, size):
            piece = lax.dynamic_index_in_dim(small, at ^ step, 1, keepdims=False)
            kept = kept + swap(piece, axis, step << low).astype(f32)
        parts = kept
    return parts[0]


def totalled(block, axis, span):
    for low, wide in staged(0, span.bit_length() - 1):
        parts = []
        for step in range(1, 1 << wide):
            parts.append(swap(block, axis, step << low))
        block = sum(parts, block)
    return block


def dot(left, right, dims, precision=None):
    return lax.dot_general(
        left, right, (dims, ((), ())), preferred_element_type=f32, precision=precision
    )


nn, nt, tn = ((1,), (0,)), ((1,), (1,)), ((0,), (0,))


def iota(shape, axis):
    return lax.broadcasted_iota(jnp.int32, shape, axis)


def chosen(shape, pairs):
    rows, columns = iota(shape, 0), iota(shape, 1)
    hit = functools.reduce(jnp.logical_or, [(rows == r) & (columns == c) for r, c in pairs])
    return jnp.where(hit, 1.0, 0.0).astype(bf16)


def call(body, outs, *args, scratch=(), grant=16 << 20, outside=(), last=False, aliases={}):
    spaces = [pltpu.HBM if i in outside else pltpu.VMEM for i in range(len(args))]
    return pl.pallas_call(
        body,
        out_shape=[
            jax.ShapeDtypeStruct(shape, kind) if last else pltpu.VMEM(shape, kind)
            for shape, kind in outs
        ],
        in_specs=[pl.BlockSpec(memory_space=space) for space in spaces],
        out_specs=[pl.BlockSpec(memory_space=pltpu.HBM if last else pltpu.VMEM)] * len(outs),
        scratch_shapes=[
            pltpu.SemaphoreType.DMA(shape) if kind is None else pltpu.VMEM(shape, kind)
            for shape, kind in scratch
        ],
        input_output_aliases=aliases,
        compiler_params=pltpu.CompilerParams(vmem_limit_bytes=grant),
    )(*[pltpu.with_memory_space_constraint(arg, space) for arg, space in zip(args, spaces)])


def block_rows(column, j, size):
    return pl.ds(pl.multiple_of((column ^ j) * size, size), size)


def prepare(mp_count, group, coarse_in, skip_in, counts_in, head_in, weight_in, *refs):
    messages, (pair, cross, own, weight, coarse, skip, top, bottom, done) = refs[: mp_count - 1], refs[mp_count - 1 :]
    width, length = skip.shape
    rows, tracks = top.shape
    place, column = lax.axis_index("seq"), lax.axis_index("mp")
    moves = [
        (coarse_in, coarse),
        (skip_in, skip),
        (counts_in.at[pl.ds(0, rows)], top),
        (counts_in.at[pl.ds(length - rows, rows)], bottom),
        (weight_in, weight),
    ]
    share = width // group
    for j, message in zip(range(1, mp_count), messages):
        for i in range(2):
            start = (column ^ j) * width + ((place >> 1) & (group - 1)) * share + i * (share // 2)
            moves.append(
                (
                    head_in.at[pl.ds(pl.multiple_of(start, 8), share // 2)],
                    message.at[pl.ds(width, share // 2), pl.ds(i * tracks, tracks)],
                )
            )
    copies = [pltpu.make_async_copy(*move, done.at[i]) for i, move in enumerate(moves)]
    for copy in copies:
        copy.start()
    for copy in copies[:4]:
        copy.wait()
    pairs = jnp.where(
        iota((coarse.shape[1], length), 0) == iota((coarse.shape[1], length), 1) // 2, 1.0, 0.0
    ).astype(bf16)
    total = (dot(coarse[...], pairs, nn) + skip[...].astype(f32)).astype(bf16)
    for message in messages:
        message[:width, :] = total
    slot = iota((edge_rows, tracks), 0)
    ahead = dot(chosen((edge_rows, length), ((0, length - 2), (1, length - 1))), total, nt)
    behind = dot(chosen((edge_rows, length), ((4, 0), (5, 1))), total, nt)
    mine = dot(chosen((edge_rows, length), ((2, 0), (3, length - 1))), total, nt)
    first = jnp.where(slot == 7, top[0:1, :].astype(f32), behind[:, :tracks])
    last = jnp.where(slot == 6, bottom[rows - 1 : rows, :].astype(f32), ahead[:, :tracks])
    even = place % 2 == 0
    for out, left, right in (
        (pair, jnp.where(even, last, first), jnp.where(even, ahead, behind)),
        (cross, jnp.where(even, first, last), jnp.where(even, behind, ahead)),
        (own, mine[:, :tracks], mine),
    ):
        out[...] = jnp.zeros(out.shape, bf16)
        out[:, :tracks] = left.astype(bf16)
        out[:, tracks:width] = right[:, tracks:].astype(bf16)
    for copy in copies[4:]:
        copy.wait()


def attach(cross, pair, own, message_in, edges, message):
    total = cross[...] + pair[...] + own[...]
    edges[...] = total
    message[message.shape[0] - edge_rows :, :] = total


def gelu_parts(inputs):
    inner = root_two_pi * (inputs + cubic_coef * inputs * inputs * inputs)
    tangent = jnp.tanh(inner)
    value = 0.5 * inputs * (1.0 + tangent)
    slope = 0.5 * (1.0 + tangent) + 0.5 * inputs * (1.0 - tangent * tangent) * root_two_pi * (
        1.0 + 3.0 * cubic_coef * inputs * inputs
    )
    return value, slope


def assembled(blocks, whole, column, width):
    channels = whole.shape[0]
    edges = 0.0
    for j, (block, rows) in enumerate(blocks):
        whole[block_rows(column, j, width), :] = block
        wide = jnp.concatenate([rows.astype(f32), jnp.zeros((edge_rows, channels - rows.shape[1]), f32)], axis=1)
        edges = edges + pltpu.roll(wide, (column ^ j) * width, 1)
    return edges.astype(bf16)


def regrouped(out, whole, halves):
    if not halves:
        out[...] = whole[...]
        return
    mine = lax.axis_index("seq") & 1
    chunk = whole.shape[0] // (2 * halves)
    for q in range(halves):
        for i, core in enumerate((mine, 1 - mine)):
            start = pl.multiple_of((2 * q + core) * chunk, 16)
            at = (i * halves + q) * chunk
            out[at : at + chunk, :] = whole[pl.ds(start, chunk), :]


def two_rows(first, second, shape):
    row = iota(shape, 0)
    return jnp.where(row == 0, first, jnp.where(row == 1, second, 0.0))


def convolve(mp_count, halves, *refs):
    pieces, (near, *far) = refs[:mp_count], refs[mp_count : 2 * mp_count - 1]
    weight, bias, message, slopes, slopes_beside, full, bundle, whole = refs[2 * mp_count - 1 :]
    width = weight.shape[0] // 3
    length = message.shape[1]
    half, tracks = pieces[1].shape[0] - edge_rows - width, bundle.shape[1]
    edges = [near[...], pieces[1][width + half :, :]] + [rows[...] for rows in far]
    column = lax.axis_index("mp")
    for j, piece in enumerate(pieces[1:]):
        for i in range(2):
            bundle[(2 * j + i) * half : (2 * j + i + 1) * half, :] = piece[width : width + half, i * tracks : (i + 1) * tracks]
    slots = assembled(
        [(piece[:width, :], edge) for piece, edge in zip(pieces, edges)], whole, column, width
    )
    regrouped(full, whole, halves)
    rows = [weight[k * width : (k + 1) * width, :] for k in range(3)]
    taps = [dot(row, whole[...], nn) for row in rows]
    beside = [dot(slots, row, nt) for row in rows]
    lanes = iota((width, length), 1)
    place = iota((edge_rows, length), 0)
    lane = iota((edge_rows, length), 1)
    spread = (place == 0) | ((place == 1) & (lane == 0)) | ((place == 2) & (lane == length - 1))
    spread = jnp.where(spread, 1.0, 0.0).astype(bf16)
    row = iota((edge_rows, width), 0)
    left = jnp.where(
        row == 0, bias[...], jnp.where(row == 1, beside[0][1:2, :], jnp.where(row == 2, beside[2][4:5, :], 0.0))
    )
    inner = (
        taps[1]
        + jnp.where(lanes == 0, 0.0, pltpu.roll(taps[0], 1, 1))
        + jnp.where(lanes == length - 1, 0.0, pltpu.roll(taps[2], length - 1, 1))
    )
    for _ in range(3):
        term = left.astype(bf16)
        inner = inner + dot(term, spread, tn)
        left = left - term.astype(f32)
    value, slope = gelu_parts(inner)
    own = whole[block_rows(column, 0, width), :].astype(f32)
    message[:width, :] = (own + value).astype(bf16)
    slopes[...] = slope
    shape = (edge_rows, width)
    outer = two_rows(
        *[sum(beside[k][first + k : first + k + 1, :] for k in range(3)) + bias[...] for first in (0, 3)], shape
    )
    near = near[:, :width].astype(f32)
    value, slope = gelu_parts(outer)
    message[width:, :] = jnp.zeros((edge_rows, length), bf16)
    message[width:, :width] = (two_rows(near[1:2, :], near[4:5, :], shape) + value).astype(bf16)
    slopes_beside[...] = slope


def predict(logits):
    return jnp.maximum(logits, 0.0) + jnp.log1p(jnp.exp(-jnp.abs(logits))) + pseudo_count


def score(mp_count, halves, *refs):
    pieces, (head, bias, counts, logits, sums, full, whole) = refs[:mp_count], refs[mp_count:]
    width = head.shape[0] // mp_count
    length, tracks = counts.shape
    blocks = [(piece[:width, :], piece[width:, :]) for piece in pieces]
    slots = assembled(blocks, whole, lax.axis_index("mp"), width)
    regrouped(full, whole, halves)
    scores = dot(whole[...], head[...], tn) + bias[...]
    logits[:length, :] = scores
    logits[length:, :] = dot(slots, head[...], nn) + bias[...]
    pred = jnp.sum(predict(scores), axis=0, keepdims=True)
    seen = jnp.sum(counts[...].astype(f32), axis=0, keepdims=True)
    sums[...] = two_rows(pred, seen, (8, tracks))


def differentiate(logits, counts, edges, totals, mask, slope):
    length, tracks = counts.shape
    pred_total, count_total = totals[0:1, :], totals[1:2, :]
    ratio = (multi_weight - 1.0) * count_total / pred_total

    def slope_of(scores, observed):
        inner = 1.0 + ratio - multi_weight * observed / predict(scores)
        return (mask[...] * inner * jax.nn.sigmoid(scores)).astype(bf16)

    slope[:length, :] = slope_of(logits[:length, :], counts[...].astype(f32))
    row = iota((edge_rows, tracks), 0)
    beside = edges[...].astype(f32)
    beside = jnp.where(row == 0, beside[6:7, :tracks], jnp.where(row == 1, beside[7:8, :tracks], 0.0))
    slope[length:, :] = slope_of(logits[length:, :], beside)


def packed(out, base, value, start, chunk):
    tiles, half = value.shape[1] // 128, chunk // 2
    for t in range(tiles):
        rows = value[start : start + chunk, t * 128 : (t + 1) * 128]
        out[base + t * chunk : base + (t + 1) * chunk, :] = rows.astype(out.dtype)
    if value.shape[1] % 128:
        pair = [value[start + i * half : start + (i + 1) * half, tiles * 128 :] for i in range(2)]
        at = base + tiles * chunk
        out[at : at + half, :] = jnp.concatenate(pair, axis=1).astype(out.dtype)


def packed_rows(chunk, both):
    return chunk * both // 128


def ranked(group, after, head_own, *refs):
    *bundles, out = refs
    width, tracks = head_own.shape
    part = width // group
    out[:, :tracks] = head_own[...]
    for r, bundle in enumerate(bundles):
        at = pl.multiple_of((((lax.axis_index("seq") >> 1) & (group - 1)) ^ r) * part, 16)
        for j in range(out.shape[1] // tracks - 1):
            out[pl.ds(at, part), (j + 1) * tracks : (j + 2) * tracks] = bundle[j * part : (j + 1) * part, :]


def backward(mp_count, seq_count, split, *refs):
    slopes, head_rows = refs[:mp_count], refs[mp_count]
    gelu, gelu_beside, full, hidden, weight, *outs = refs[mp_count + 1 :]
    slope_rows = outs[-3]
    own, *outs = outs
    carry, outs = outs[: mp_count - 1], outs[mp_count - 1 :]
    width, length = head_rows.shape[0], full.shape[1]
    tracks = head_rows.shape[1] // mp_count
    place, column = lax.axis_index("seq"), lax.axis_index("mp")
    for j, slope in enumerate(slopes):
        slope_rows[:, j * tracks : (j + 1) * tracks] = slope[...]
    inner = dot(head_rows[...], slope_rows[:length, :], nt)
    outer = dot(slope_rows[length:, :], head_rows[...], nt)
    middle = (inner * gelu[...]).astype(bf16).astype(f32)
    row = iota(outer.shape, 0)
    absent = ((row == 0) & (place == 0)) | ((row == 1) & (place == seq_count - 1))
    outer = jnp.where(absent, 0.0, outer * gelu_beside[...]).astype(bf16)
    ends = dot(outer, chosen((edge_rows, length), ((0, 0), (1, length - 1))), tn)
    lanes = iota((width, length), 1)
    stacked = outs[-1]
    stacked[:width, :] = jnp.where(lanes == length - 1, ends, pltpu.roll(middle, length - 1, 1)).astype(bf16)
    stacked[width : 2 * width, :] = middle.astype(bf16)
    stacked[2 * width :, :] = jnp.where(lanes == 0, ends, pltpu.roll(middle, 1, 1)).astype(bf16)
    total = outs[-2]
    total[...] = dot(weight[...], stacked[...], tn)
    own[...] = inner + total[block_rows(column, 0, width), :]
    for j, out in zip(range(1, mp_count), carry):
        out[...] = total[block_rows(column, j, width), :].astype(bf16)
    own_slope = slopes[0][:length, :]
    if split:
        rows = full.shape[0] // 2
        chunk = full.shape[0] // seq_count
        for i, out in ((1, outs[1]), (0, outs[0])):
            at = slice(i * rows, (i + 1) * rows)
            value = jnp.concatenate(
                [dot(hidden[at, :], own_slope, nn), dot(full[at, :], stacked[...], nt)], axis=1
            )
            for q in range(seq_count // 2):
                packed(out, q * packed_rows(chunk, value.shape[1]), value, q * chunk, chunk)
    else:
        grads = outs[0]
        grads[:, :tracks] = dot(hidden[...], own_slope, nn)
        grads[:, tracks:] = dot(full[...], stacked[...], nt)


def quartered(count, kept, got, own, *outs):
    rows = own.shape[0]
    at = lax.axis_index("seq") >> 1
    total = outs[-1]
    total[...] = kept[...] + got[...].astype(f32)
    own[...] = total[pl.ds(pl.multiple_of(at * rows, 8), rows), :]
    for j, out in zip(range(1, count), outs):
        out[...] = total[pl.ds(pl.multiple_of((at ^ j) * rows, 8), rows), :].astype(bf16)


def unpacked(whole, total):
    chunk, both = whole.shape
    if total.shape == whole.shape:
        whole[...] = total
        return
    tiles, half = both // 128, chunk // 2
    for t in range(tiles):
        whole[:, t * 128 : (t + 1) * 128] = total[t * chunk : (t + 1) * chunk, :]
    for i in range(2 if both % 128 else 0):
        at = tiles * chunk
        whole[i * half : (i + 1) * half, tiles * 128 :] = total[at : at + half, i * 64 : (i + 1) * 64]


def finish(mp_count, scale, *refs):
    carried, rest = refs[:mp_count], refs[mp_count:]
    *summands, grad_skip, grad_coarse, grad_head, grad_conv, skip, coarse, whole, conv, done = rest
    total = summands[0][...]
    for part in summands[1:]:
        total = total + part[...].astype(f32)
    unpacked(whole, total * scale)
    tracks, wide = grad_head.shape[1], grad_conv.shape[2]
    copies = [pltpu.make_async_copy(whole.at[:, pl.ds(0, tracks)], grad_head, done.at[0])]
    copies[0].start()
    for k in range(grad_conv.shape[0]):
        conv[k] = whole[:, tracks + k * wide : tracks + (k + 1) * wide]
    copies.append(pltpu.make_async_copy(conv, grad_conv, done.at[1]))
    copies[1].start()
    total = carried[0][...]
    for part in carried[1:]:
        total = total + part[...].astype(f32)
    skip[...] = total.astype(bf16)
    copies.append(pltpu.make_async_copy(skip, grad_skip, done.at[2]))
    copies[2].start()
    length, half = grad_skip.shape[1], grad_coarse.shape[1]
    pairs = jnp.where(iota((length, half), 0) // 2 == iota((length, half), 1), 1.0, 0.0).astype(bf16)
    terms, left = [], total
    for _ in range(3):
        terms.append(left.astype(bf16))
        left = left - terms[-1].astype(f32)
    coarse[...] = sum(dot(term, pairs, nn) for term in terms).astype(bf16)
    copies.append(pltpu.make_async_copy(coarse, grad_coarse, done.at[3]))
    copies[3].start()
    for copy in copies:
        copy.wait()


def shards(coarse, skip, conv_weight, conv_bias, head_weight, head_bias, counts, seg_mask):
    width, length = skip.shape
    taps = conv_weight.shape[0]
    seq_count, mp_count = lax.axis_size("seq"), lax.axis_size("mp")
    channels, tracks = head_weight.shape
    scale_back = 1.0 / math.sqrt(length * seq_count)
    place, column = lax.axis_index("seq"), lax.axis_index("mp")
    group = min(4, seq_count // 2)
    share = width // group
    chunk = channels // seq_count
    both = tracks + taps * width
    split = chunk % 32 == 0 and both % 64 == 0 and len(list(staged(0, seq_count.bit_length() - 1))) == 2
    halves = seq_count // 2 if split else 0
    tall = width + edge_rows
    tile = ((edge_rows, length), bf16)
    block = ((width + share // 2, length), bf16)
    nearest = ((width + share // 2 + edge_rows, length), bf16)
    *messages, pair, cross, own, weight = call(
        functools.partial(prepare, mp_count, group),
        [nearest] + [block] * (mp_count - 2) + [tile, tile, tile, ((taps * width, channels), bf16)],
        coarse, skip, counts, head_weight, conv_weight.reshape(taps * width, channels),
        scratch=[
            (coarse.shape, bf16), (skip.shape, bf16), ((8, tracks), jnp.int32), ((8, tracks), jnp.int32),
            ((5 + 2 * (mp_count - 1),), None),
        ],
        outside=range(5),
    )
    cross = crossed(cross, "seq")
    pair = swap(pair, "seq", 1)
    edges, messages[0] = call(attach, [tile, nearest], cross, pair, own, messages[0], aliases={3: 1})
    pieces = [messages[-1]]
    for j, message in zip(range(1, mp_count), messages):
        pieces.append(swap(message, "mp", j))
    halos = [edges]
    for j in range(2, mp_count):
        halos.append(swap(edges, "mp", j))
    message, gelu, gelu_beside, full_in, bundle = call(
        functools.partial(convolve, mp_count, halves),
        [((tall, length), bf16), ((width, length), f32), ((edge_rows, width), f32), ((channels, length), bf16)]
        + [(((mp_count - 1) * share, tracks), bf16)],
        *pieces, *halos, weight, conv_bias[None, :],
        scratch=[((channels, length), bf16)],
    )
    pieces = gathered(message, "mp")
    bundles = [bundle]
    for r in range(1, group):
        bundles.append(swap(bundle, "seq", 2 * r))
    head_own = lax.dynamic_index_in_dim(head_weight.reshape(mp_count, width, tracks), column, 0, keepdims=False)
    logits, sums, full = call(
        functools.partial(score, mp_count, halves),
        [((length + edge_rows, tracks), f32), ((8, tracks), f32), ((channels, length), bf16)],
        *pieces, head_weight, head_bias[None, :], counts,
        scratch=[((channels, length), bf16)],
    )
    span = seq_count // seg_mask.shape[0]
    totals = totalled(sums, "seq", span)
    mask_row = lax.dynamic_slice_in_dim(seg_mask, place // span, 1, 0).astype(f32)
    (slope,) = call(
        differentiate, [((length + edge_rows, tracks), bf16)], logits, counts, edges, totals, mask_row
    )
    slopes = gathered(slope, "mp")
    (head_rows,) = call(
        functools.partial(ranked, group), [((width, mp_count * tracks), bf16)], slope, head_own, *bundles
    )
    quarter = (packed_rows(chunk, both), 128)
    half = (seq_count // 2 * quarter[0], 128)
    grads_at = ((channels, both), f32)
    scratch = [((channels, length), f32), ((taps * width, length), bf16)]
    head_at = [((length + edge_rows, mp_count * tracks), bf16)]
    own, *outs = call(
        functools.partial(backward, mp_count, seq_count, split),
        [((width, length), f32)]
        + [((width, length), bf16)] * (mp_count - 1)
        + ([(half, f32), (half, bf16)] if split else [grads_at]),
        *slopes, head_rows, gelu, gelu_beside, full_in, full, weight,
        scratch=head_at + scratch,
    )
    carry, grads = outs[: mp_count - 1], outs[mp_count - 1 :]
    if split:
        got = swap(grads[1], "seq", 1)
    parts = []
    for j in range(mp_count - 1, 0, -1):
        parts.append(swap(carry[j - 1], "mp", j))
    if split:
        count = seq_count // 2
        grad_own, *sends = call(
            functools.partial(quartered, count),
            [(quarter, f32)] + [(quarter, bf16)] * (count - 1),
            grads[0], got,
            scratch=[(half, f32)],
        )
        gots = []
        for j in range(count - 1, 0, -1):
            gots.append(swap(sends[j - 1], "seq", 2 * j))
    else:
        grad_own, gots = scattered(grads[0].reshape(seq_count, chunk, both), "seq"), []
    outs = [((width, length), bf16), ((width, length // 2), bf16), ((chunk, tracks), f32), ((taps, chunk, width), f32)]
    grad_skip, grad_coarse, grad_head, grad_conv = call(
        functools.partial(finish, mp_count, scale_back),
        outs,
        own, *parts, grad_own, *gots,
        scratch=outs[:2] + [((chunk, both), f32), outs[3], ((len(outs),), None)],
        last=True,
    )
    return (grad_skip, grad_coarse, grad_head, grad_conv.transpose(1, 0, 2))


def solution(mesh):
    in_specs = (
        P("mp", "seq"),
        P("mp", "seq"),
        P(None, "mp", None),
        P("mp"),
        P(None, "mp"),
        P("mp"),
        P("seq", "mp"),
        P(None, "mp"),
    )
    out_specs = (P("mp", "seq"), P("mp", "seq"), P("seq", "mp"), P("seq", None, "mp"))

    return jax.shard_map(shards, mesh=mesh, in_specs=in_specs, out_specs=out_specs, check_vma=False)
```

```python
import functools
import math

import jax
import jax.numpy as jnp
from jax import lax
from jax.experimental import pallas as pl
from jax.experimental.pallas import tpu as pltpu
from jax.sharding import PartitionSpec as P


root_two_pi = 0.7978845608028654
cubic_coef = 0.044715
multi_weight = 5.0
pseudo_count = 0.5
edge_rows = 8
bf16, f32 = jnp.bfloat16, jnp.float32


def swap(block, axis, mask):
    count = lax.axis_size(axis)
    return lax.ppermute(block, axis, [(i, i ^ mask) for i in range(count)])


def crossed(block, axis):
    count = lax.axis_size(axis)
    pairs = [(i, i + 1) for i in range(1, count - 1, 2)]
    return lax.ppermute(block, axis, pairs + [(b, a) for a, b in pairs])


def gathered(block, axis):
    parts = [block]
    for j in range(1, lax.axis_size(axis)):
        parts.append(swap(block, axis, j))
    return parts


def staged(low, bits):
    while low < bits:
        wide = 1 if low == 0 else min(2, bits - low)
        yield low, wide
        low += wide


def scattered(parts, axis):
    bits = lax.axis_size(axis).bit_length() - 1
    mine = lax.axis_index(axis)
    for low, wide in staged(0, bits):
        size = 1 << wide
        parts = parts.reshape((parts.shape[0] // size, size) + parts.shape[1:])
        at = (mine >> low) & (size - 1)
        small = parts.astype(bf16)
        kept = lax.dynamic_index_in_dim(parts, at, 1, keepdims=False)
        for step in range(1, size):
            piece = lax.dynamic_index_in_dim(small, at ^ step, 1, keepdims=False)
            kept = kept + swap(piece, axis, step << low).astype(f32)
        parts = kept
    return parts[0]


def totalled(block, axis, span):
    for low, wide in staged(0, span.bit_length() - 1):
        parts = []
        for step in range(1, 1 << wide):
            parts.append(swap(block, axis, step << low))
        block = sum(parts, block)
    return block


def dot(left, right, dims, precision=None):
    return lax.dot_general(
        left, right, (dims, ((), ())), preferred_element_type=f32, precision=precision
    )


nn, nt, tn = ((1,), (0,)), ((1,), (1,)), ((0,), (0,))


def iota(shape, axis):
    return lax.broadcasted_iota(jnp.int32, shape, axis)


def chosen(shape, pairs):
    rows, columns = iota(shape, 0), iota(shape, 1)
    hit = functools.reduce(jnp.logical_or, [(rows == r) & (columns == c) for r, c in pairs])
    return jnp.where(hit, 1.0, 0.0).astype(bf16)


def call(body, outs, *args, scratch=(), grant=16 << 20, outside=(), last=False, aliases={}):
    spaces = [pltpu.HBM if i in outside else pltpu.VMEM for i in range(len(args))]
    return pl.pallas_call(
        body,
        out_shape=[
            jax.ShapeDtypeStruct(shape, kind) if last else pltpu.VMEM(shape, kind)
            for shape, kind in outs
        ],
        in_specs=[pl.BlockSpec(memory_space=space) for space in spaces],
        out_specs=[pl.BlockSpec(memory_space=pltpu.HBM if last else pltpu.VMEM)] * len(outs),
        scratch_shapes=[
            pltpu.SemaphoreType.DMA(shape) if kind is None else pltpu.VMEM(shape, kind)
            for shape, kind in scratch
        ],
        input_output_aliases=aliases,
        compiler_params=pltpu.CompilerParams(vmem_limit_bytes=grant),
    )(*[pltpu.with_memory_space_constraint(arg, space) for arg, space in zip(args, spaces)])


def block_rows(column, j, size):
    return pl.ds(pl.multiple_of((column ^ j) * size, size), size)


def stage(after, weight_in, weight, done):
    copy = pltpu.make_async_copy(weight_in, weight, done.at[0])
    copy.start()
    copy.wait()


def prepare(mp_count, group, coarse_in, skip_in, counts_in, head_in, *refs):
    messages, (pair, cross, own, coarse, skip, top, bottom, done) = refs[: mp_count - 1], refs[mp_count - 1 :]
    width, length = skip.shape
    rows, tracks = top.shape
    place, column = lax.axis_index("seq"), lax.axis_index("mp")
    moves = [
        (coarse_in, coarse),
        (skip_in, skip),
        (counts_in.at[pl.ds(0, rows)], top),
        (counts_in.at[pl.ds(length - rows, rows)], bottom),
    ]
    share = width // group
    for j, message in zip(range(1, mp_count), messages):
        for i in range(2):
            start = (column ^ j) * width + ((place >> 1) & (group - 1)) * share + i * (share // 2)
            moves.append(
                (
                    head_in.at[pl.ds(pl.multiple_of(start, 8), share // 2)],
                    message.at[pl.ds(width, share // 2), pl.ds(i * tracks, tracks)],
                )
            )
    copies = [pltpu.make_async_copy(*move, done.at[i]) for i, move in enumerate(moves)]
    for copy in copies:
        copy.start()
    for copy in copies[:4]:
        copy.wait()
    pairs = jnp.where(
        iota((coarse.shape[1], length), 0) == iota((coarse.shape[1], length), 1) // 2, 1.0, 0.0
    ).astype(bf16)
    total = (dot(coarse[...], pairs, nn) + skip[...].astype(f32)).astype(bf16)
    for message in messages:
        message[:width, :] = total
    slot = iota((edge_rows, tracks), 0)
    ahead = dot(chosen((edge_rows, length), ((0, length - 2), (1, length - 1))), total, nt)
    behind = dot(chosen((edge_rows, length), ((4, 0), (5, 1))), total, nt)
    mine = dot(chosen((edge_rows, length), ((2, 0), (3, length - 1))), total, nt)
    first = jnp.where(slot == 7, top[0:1, :].astype(f32), behind[:, :tracks])
    last = jnp.where(slot == 6, bottom[rows - 1 : rows, :].astype(f32), ahead[:, :tracks])
    even = place % 2 == 0
    for out, left, right in (
        (pair, jnp.where(even, last, first), jnp.where(even, ahead, behind)),
        (cross, jnp.where(even, first, last), jnp.where(even, behind, ahead)),
        (own, mine[:, :tracks], mine),
    ):
        out[...] = jnp.zeros(out.shape, bf16)
        out[:, :tracks] = left.astype(bf16)
        out[:, tracks:width] = right[:, tracks:].astype(bf16)
    for copy in copies[4:]:
        copy.wait()


def attach(cross, pair, own, message_in, edges, message):
    total = cross[...] + pair[...] + own[...]
    edges[...] = total
    message[message.shape[0] - edge_rows :, :] = total


def gelu_parts(inputs):
    inner = root_two_pi * (inputs + cubic_coef * inputs * inputs * inputs)
    tangent = jnp.tanh(inner)
    value = 0.5 * inputs * (1.0 + tangent)
    slope = 0.5 * (1.0 + tangent) + 0.5 * inputs * (1.0 - tangent * tangent) * root_two_pi * (
        1.0 + 3.0 * cubic_coef * inputs * inputs
    )
    return value, slope


def assembled(blocks, whole, column, width):
    channels = whole.shape[0]
    edges = 0.0
    for j, (block, rows) in enumerate(blocks):
        whole[block_rows(column, j, width), :] = block
        wide = jnp.concatenate([rows.astype(f32), jnp.zeros((edge_rows, channels - rows.shape[1]), f32)], axis=1)
        edges = edges + pltpu.roll(wide, (column ^ j) * width, 1)
    return edges.astype(bf16)


def regrouped(out, whole, halves):
    if not halves:
        out[...] = whole[...]
        return
    mine = lax.axis_index("seq") & 1
    chunk = whole.shape[0] // (2 * halves)
    for q in range(halves):
        for i, core in enumerate((mine, 1 - mine)):
            start = pl.multiple_of((2 * q + core) * chunk, 16)
            at = (i * halves + q) * chunk
            out[at : at + chunk, :] = whole[pl.ds(start, chunk), :]


def two_rows(first, second, shape):
    row = iota(shape, 0)
    return jnp.where(row == 0, first, jnp.where(row == 1, second, 0.0))


def convolve(mp_count, halves, *refs):
    pieces, (near, *far) = refs[:mp_count], refs[mp_count : 2 * mp_count - 1]
    weight, bias, message, slopes, slopes_beside, full, bundle, whole = refs[2 * mp_count - 1 :]
    width = weight.shape[0] // 3
    length = message.shape[1]
    half, tracks = pieces[1].shape[0] - edge_rows - width, bundle.shape[1]
    edges = [near[...], pieces[1][width + half :, :]] + [rows[...] for rows in far]
    column = lax.axis_index("mp")
    for j, piece in enumerate(pieces[1:]):
        for i in range(2):
            bundle[(2 * j + i) * half : (2 * j + i + 1) * half, :] = piece[width : width + half, i * tracks : (i + 1) * tracks]
    slots = assembled(
        [(piece[:width, :], edge) for piece, edge in zip(pieces, edges)], whole, column, width
    )
    regrouped(full, whole, halves)
    rows = [weight[k * width : (k + 1) * width, :] for k in range(3)]
    taps = [dot(row, whole[...], nn) for row in rows]
    beside = [dot(slots, row, nt) for row in rows]
    lanes = iota((width, length), 1)
    place = iota((edge_rows, length), 0)
    lane = iota((edge_rows, length), 1)
    spread = (place == 0) | ((place == 1) & (lane == 0)) | ((place == 2) & (lane == length - 1))
    spread = jnp.where(spread, 1.0, 0.0).astype(bf16)
    row = iota((edge_rows, width), 0)
    left = jnp.where(
        row == 0, bias[...], jnp.where(row == 1, beside[0][1:2, :], jnp.where(row == 2, beside[2][4:5, :], 0.0))
    )
    inner = (
        taps[1]
        + jnp.where(lanes == 0, 0.0, pltpu.roll(taps[0], 1, 1))
        + jnp.where(lanes == length - 1, 0.0, pltpu.roll(taps[2], length - 1, 1))
    )
    for _ in range(3):
        term = left.astype(bf16)
        inner = inner + dot(term, spread, tn)
        left = left - term.astype(f32)
    value, slope = gelu_parts(inner)
    own = whole[block_rows(column, 0, width), :].astype(f32)
    message[:width, :] = (own + value).astype(bf16)
    slopes[...] = slope
    shape = (edge_rows, width)
    outer = two_rows(
        *[sum(beside[k][first + k : first + k + 1, :] for k in range(3)) + bias[...] for first in (0, 3)], shape
    )
    near = near[:, :width].astype(f32)
    value, slope = gelu_parts(outer)
    message[width:, :] = jnp.zeros((edge_rows, length), bf16)
    message[width:, :width] = (two_rows(near[1:2, :], near[4:5, :], shape) + value).astype(bf16)
    slopes_beside[...] = slope


def predict(logits):
    return jnp.maximum(logits, 0.0) + jnp.log1p(jnp.exp(-jnp.abs(logits))) + pseudo_count


def score(mp_count, halves, *refs):
    pieces, (head, bias, counts, logits, sums, full, whole) = refs[:mp_count], refs[mp_count:]
    width = head.shape[0] // mp_count
    length, tracks = counts.shape
    blocks = [(piece[:width, :], piece[width:, :]) for piece in pieces]
    slots = assembled(blocks, whole, lax.axis_index("mp"), width)
    regrouped(full, whole, halves)
    scores = dot(whole[...], head[...], tn) + bias[...]
    logits[:length, :] = scores
    logits[length:, :] = dot(slots, head[...], nn) + bias[...]
    pred = jnp.sum(predict(scores), axis=0, keepdims=True)
    seen = jnp.sum(counts[...].astype(f32), axis=0, keepdims=True)
    sums[...] = two_rows(pred, seen, (8, tracks))


def differentiate(logits, counts, edges, totals, mask, slope):
    length, tracks = counts.shape
    pred_total, count_total = totals[0:1, :], totals[1:2, :]
    ratio = (multi_weight - 1.0) * count_total / pred_total

    def slope_of(scores, observed):
        inner = 1.0 + ratio - multi_weight * observed / predict(scores)
        return (mask[...] * inner * jax.nn.sigmoid(scores)).astype(bf16)

    slope[:length, :] = slope_of(logits[:length, :], counts[...].astype(f32))
    row = iota((edge_rows, tracks), 0)
    beside = edges[...].astype(f32)
    beside = jnp.where(row == 0, beside[6:7, :tracks], jnp.where(row == 1, beside[7:8, :tracks], 0.0))
    slope[length:, :] = slope_of(logits[length:, :], beside)


def packed(out, base, value, start, chunk):
    tiles, half = value.shape[1] // 128, chunk // 2
    for t in range(tiles):
        rows = value[start : start + chunk, t * 128 : (t + 1) * 128]
        out[base + t * chunk : base + (t + 1) * chunk, :] = rows.astype(out.dtype)
    if value.shape[1] % 128:
        pair = [value[start + i * half : start + (i + 1) * half, tiles * 128 :] for i in range(2)]
        at = base + tiles * chunk
        out[at : at + half, :] = jnp.concatenate(pair, axis=1).astype(out.dtype)


def packed_rows(chunk, both):
    return chunk * both // 128


def ranked(group, after, head_own, *refs):
    *bundles, out = refs
    width, tracks = head_own.shape
    part = width // group
    out[:, :tracks] = head_own[...]
    for r, bundle in enumerate(bundles):
        at = pl.multiple_of((((lax.axis_index("seq") >> 1) & (group - 1)) ^ r) * part, 16)
        for j in range(out.shape[1] // tracks - 1):
            out[pl.ds(at, part), (j + 1) * tracks : (j + 2) * tracks] = bundle[j * part : (j + 1) * part, :]


def backward(mp_count, seq_count, split, *refs):
    slopes, head_rows = refs[:mp_count], refs[mp_count]
    gelu, gelu_beside, full, hidden, weight, *outs = refs[mp_count + 1 :]
    slope_rows = outs[-3]
    own, *outs = outs
    carry, outs = outs[: mp_count - 1], outs[mp_count - 1 :]
    width, length = head_rows.shape[0], full.shape[1]
    tracks = head_rows.shape[1] // mp_count
    place, column = lax.axis_index("seq"), lax.axis_index("mp")
    for j, slope in enumerate(slopes):
        slope_rows[:, j * tracks : (j + 1) * tracks] = slope[...]
    inner = dot(head_rows[...], slope_rows[:length, :], nt)
    outer = dot(slope_rows[length:, :], head_rows[...], nt)
    middle = (inner * gelu[...]).astype(bf16).astype(f32)
    row = iota(outer.shape, 0)
    absent = ((row == 0) & (place == 0)) | ((row == 1) & (place == seq_count - 1))
    outer = jnp.where(absent, 0.0, outer * gelu_beside[...]).astype(bf16)
    ends = dot(outer, chosen((edge_rows, length), ((0, 0), (1, length - 1))), tn)
    lanes = iota((width, length), 1)
    stacked = outs[-1]
    stacked[:width, :] = jnp.where(lanes == length - 1, ends, pltpu.roll(middle, length - 1, 1)).astype(bf16)
    stacked[width : 2 * width, :] = middle.astype(bf16)
    stacked[2 * width :, :] = jnp.where(lanes == 0, ends, pltpu.roll(middle, 1, 1)).astype(bf16)
    total = outs[-2]
    total[...] = dot(weight[...], stacked[...], tn)
    own[...] = inner + total[block_rows(column, 0, width), :]
    for j, out in zip(range(1, mp_count), carry):
        out[...] = total[block_rows(column, j, width), :].astype(bf16)
    own_slope = slopes[0][:length, :]
    if split:
        rows = full.shape[0] // 2
        chunk = full.shape[0] // seq_count
        for i, out in ((1, outs[1]), (0, outs[0])):
            at = slice(i * rows, (i + 1) * rows)
            value = jnp.concatenate(
                [dot(hidden[at, :], own_slope, nn), dot(full[at, :], stacked[...], nt)], axis=1
            )
            for q in range(seq_count // 2):
                packed(out, q * packed_rows(chunk, value.shape[1]), value, q * chunk, chunk)
    else:
        grads = outs[0]
        grads[:, :tracks] = dot(hidden[...], own_slope, nn)
        grads[:, tracks:] = dot(full[...], stacked[...], nt)


def quartered(count, kept, got, own, *outs):
    rows = own.shape[0]
    at = lax.axis_index("seq") >> 1
    total = outs[-1]
    total[...] = kept[...] + got[...].astype(f32)
    own[...] = total[pl.ds(pl.multiple_of(at * rows, 8), rows), :]
    for j, out in zip(range(1, count), outs):
        out[...] = total[pl.ds(pl.multiple_of((at ^ j) * rows, 8), rows), :].astype(bf16)


def unpacked(whole, total):
    chunk, both = whole.shape
    if total.shape == whole.shape:
        whole[...] = total
        return
    tiles, half = both // 128, chunk // 2
    for t in range(tiles):
        whole[:, t * 128 : (t + 1) * 128] = total[t * chunk : (t + 1) * chunk, :]
    for i in range(2 if both % 128 else 0):
        at = tiles * chunk
        whole[i * half : (i + 1) * half, tiles * 128 :] = total[at : at + half, i * 64 : (i + 1) * 64]


def finish(mp_count, scale, *refs):
    carried, rest = refs[:mp_count], refs[mp_count:]
    *summands, grad_skip, grad_coarse, grad_head, grad_conv, skip, coarse, whole, conv, done = rest
    total = summands[0][...]
    for part in summands[1:]:
        total = total + part[...].astype(f32)
    unpacked(whole, total * scale)
    tracks, wide = grad_head.shape[1], grad_conv.shape[2]
    copies = [pltpu.make_async_copy(whole.at[:, pl.ds(0, tracks)], grad_head, done.at[0])]
    copies[0].start()
    for k in range(grad_conv.shape[0]):
        conv[k] = whole[:, tracks + k * wide : tracks + (k + 1) * wide]
    copies.append(pltpu.make_async_copy(conv, grad_conv, done.at[1]))
    copies[1].start()
    total = carried[0][...]
    for part in carried[1:]:
        total = total + part[...].astype(f32)
    skip[...] = total.astype(bf16)
    copies.append(pltpu.make_async_copy(skip, grad_skip, done.at[2]))
    copies[2].start()
    length, half = grad_skip.shape[1], grad_coarse.shape[1]
    pairs = jnp.where(iota((length, half), 0) // 2 == iota((length, half), 1), 1.0, 0.0).astype(bf16)
    terms, left = [], total
    for _ in range(2):
        terms.append(left.astype(bf16))
        left = left - terms[-1].astype(f32)
    coarse[...] = sum(dot(term, pairs, nn) for term in terms).astype(bf16)
    copies.append(pltpu.make_async_copy(coarse, grad_coarse, done.at[3]))
    copies[3].start()
    for copy in copies:
        copy.wait()


def shards(coarse, skip, conv_weight, conv_bias, head_weight, head_bias, counts, seg_mask):
    width, length = skip.shape
    taps = conv_weight.shape[0]
    seq_count, mp_count = lax.axis_size("seq"), lax.axis_size("mp")
    channels, tracks = head_weight.shape
    scale_back = 1.0 / math.sqrt(length * seq_count)
    place, column = lax.axis_index("seq"), lax.axis_index("mp")
    group = min(4, seq_count // 2)
    share = width // group
    chunk = channels // seq_count
    both = tracks + taps * width
    split = chunk % 32 == 0 and both % 64 == 0 and len(list(staged(0, seq_count.bit_length() - 1))) == 2
    halves = seq_count // 2 if split else 0
    tall = width + edge_rows
    tile = ((edge_rows, length), bf16)
    block = ((width + share // 2, length), bf16)
    nearest = ((width + share // 2 + edge_rows, length), bf16)
    *messages, pair, cross, own = call(
        functools.partial(prepare, mp_count, group),
        [nearest] + [block] * (mp_count - 2) + [tile, tile, tile],
        coarse, skip, counts, head_weight,
        scratch=[
            (coarse.shape, bf16), (skip.shape, bf16), ((8, tracks), jnp.int32), ((8, tracks), jnp.int32),
            ((4 + 2 * (mp_count - 1),), None),
        ],
        outside=range(4),
    )
    cross = crossed(cross, "seq")
    pair = swap(pair, "seq", 1)
    edges, messages[0] = call(attach, [tile, nearest], cross, pair, own, messages[0], aliases={3: 1})
    pieces = [messages[-1]]
    for j, message in zip(range(1, mp_count), messages):
        pieces.append(swap(message, "mp", j))
    halos = [edges]
    for j in range(2, mp_count):
        halos.append(swap(edges, "mp", j))
    (weight,) = call(
        stage, [((taps * width, channels), bf16)], edges, conv_weight.reshape(taps * width, channels),
        scratch=[((1,), None)], outside=(1,),
    )
    message, gelu, gelu_beside, full_in, bundle = call(
        functools.partial(convolve, mp_count, halves),
        [((tall, length), bf16), ((width, length), f32), ((edge_rows, width), f32), ((channels, length), bf16)]
        + [(((mp_count - 1) * share, tracks), bf16)],
        *pieces, *halos, weight, conv_bias[None, :],
        scratch=[((channels, length), bf16)],
    )
    pieces = gathered(message, "mp")
    bundles = [bundle]
    for r in range(1, group):
        bundles.append(swap(bundle, "seq", 2 * r))
    head_own = lax.dynamic_index_in_dim(head_weight.reshape(mp_count, width, tracks), column, 0, keepdims=False)
    logits, sums, full = call(
        functools.partial(score, mp_count, halves),
        [((length + edge_rows, tracks), f32), ((8, tracks), f32), ((channels, length), bf16)],
        *pieces, head_weight, head_bias[None, :], counts,
        scratch=[((channels, length), bf16)],
    )
    span = seq_count // seg_mask.shape[0]
    totals = totalled(sums, "seq", span)
    mask_row = lax.dynamic_slice_in_dim(seg_mask, place // span, 1, 0).astype(f32)
    (slope,) = call(
        differentiate, [((length + edge_rows, tracks), bf16)], logits, counts, edges, totals, mask_row
    )
    slopes = gathered(slope, "mp")
    (head_rows,) = call(
        functools.partial(ranked, group), [((width, mp_count * tracks), bf16)], slope, head_own, *bundles
    )
    quarter = (packed_rows(chunk, both), 128)
    half = (seq_count // 2 * quarter[0], 128)
    grads_at = ((channels, both), f32)
    scratch = [((channels, length), f32), ((taps * width, length), bf16)]
    head_at = [((length + edge_rows, mp_count * tracks), bf16)]
    own, *outs = call(
        functools.partial(backward, mp_count, seq_count, split),
        [((width, length), f32)]
        + [((width, length), bf16)] * (mp_count - 1)
        + ([(half, f32), (half, bf16)] if split else [grads_at]),
        *slopes, head_rows, gelu, gelu_beside, full_in, full, weight,
        scratch=head_at + scratch,
    )
    carry, grads = outs[: mp_count - 1], outs[mp_count - 1 :]
    if split:
        got = swap(grads[1], "seq", 1)
    parts = []
    for j in range(mp_count - 1, 0, -1):
        parts.append(swap(carry[j - 1], "mp", j))
    if split:
        count = seq_count // 2
        grad_own, *sends = call(
            functools.partial(quartered, count),
            [(quarter, f32)] + [(quarter, bf16)] * (count - 1),
            grads[0], got,
            scratch=[(half, f32)],
        )
        gots = []
        for j in range(count - 1, 0, -1):
            gots.append(swap(sends[j - 1], "seq", 2 * j))
    else:
        grad_own, gots = scattered(grads[0].reshape(seq_count, chunk, both), "seq"), []
    outs = [((width, length), bf16), ((width, length // 2), bf16), ((chunk, tracks), f32), ((taps, chunk, width), f32)]
    grad_skip, grad_coarse, grad_head, grad_conv = call(
        functools.partial(finish, mp_count, scale_back),
        outs,
        own, *parts, grad_own, *gots,
        scratch=outs[:2] + [((chunk, both), f32), outs[3], ((len(outs),), None)],
        last=True,
    )
    return (grad_skip, grad_coarse, grad_head, grad_conv.transpose(1, 0, 2))


def solution(mesh):
    in_specs = (
        P("mp", "seq"),
        P("mp", "seq"),
        P(None, "mp", None),
        P("mp"),
        P(None, "mp"),
        P("mp"),
        P("seq", "mp"),
        P(None, "mp"),
    )
    out_specs = (P("mp", "seq"), P("mp", "seq"), P("seq", "mp"), P("seq", None, "mp"))

    return jax.shard_map(shards, mesh=mesh, in_specs=in_specs, out_specs=out_specs, check_vma=False)
```
